32 devices in a mesh: pour: 2 (over x), brick: 16 (over z, y, core).
Axes of the slice: x: 2, y: 2, z: 4, core: 2. Of those that a mesh axis runs over, the one named last changes fastest.
Arguments:
- initial_voxel_degrees: float32 [256, 256, 256], P(('pour', 'brick')), parts along dimension 0, may hold values from -2 to 4
- alloy_tag_per_voxel: int32 [128, 256, 256], P('brick'), may hold values from 0 to 7
- thermal_conductance_per_alloy: float32 [8], replicated, may hold values from 0.2 to 1
- specific_storage_per_alloy: float32 [8], replicated, may hold values from 1 to 4
- bore_boundary_positions: int32 [16, 32, 256], P('brick'), may hold values from 0 to 524287
- surface_transfer_coefficient: float32 [16, 32], P('brick'), may hold values from 0 to 18
- surface_over_flow_ratio: float32 [32], replicated, may hold values from 0 to 1
- flow_direction_flag: int32 [32], replicated, may hold values from 0 to 1
- entry_coolant_degrees: float32 [64], P('pour'), parts along dimension 0, may hold values from -1 to 0
Outputs:
- die_temperature: float32 [256, 256, 256], P(('pour', 'brick')), parts along dimension 0
- coolant_mid: float32 [32, 32], P(('pour', 'brick')), parts along dimension 0
The draws below stay inside these ranges and needn't reach their ends.
There are 2 independent parts, one for each index of `pour`. The reference program is written for one: setup_inputs(seed, part) draws one part's arguments, and reference() takes and returns one part's arrays. A program takes and returns all parts, laid end to end along the dimension named above; an argument that names none is the same for every part. Nothing has to cross between parts.
Inputs may be any that keep to these rules, and one draw needn't show every extreme that they name: `bore_boundary_positions`: indices refer to cells of the segment's own brick.
All inputs are finite; a program needn't handle non-finite values.
Results may differ from the reference program's by a relative error of at most 0.00006.
Values sent between devices are 32-bit elements; how exact they have to be, the bound alone decides.
No kernel may reach another device: no remote copies, remote signals or barrier semaphores. Data moves between devices by JAX's collectives and lax.ppermute only.
A program may use at most 64 MiB of HBM per device.

```python
import math
import jax
import jax.numpy as jnp
from jax import lax

CX = 8
NY = 256
NZ = 256
STEPS = 3
LINES = 32
WALL = 256
MATS = 8
NXT = 128
N_BRICK = 16


def draw_initial_voxel_degrees(key, part):
    array_extent = (CX * N_BRICK, NY, NZ)
    first = jax.random.fold_in(key, 0)
    rough = jnp.clip(jax.random.normal(first, array_extent, jnp.float32), -4.0, 4.0)
    return 1.0 + 0.6 * rough


def draw_surface_transfer_coefficient(key, part):
    array_extent = (N_BRICK, LINES)
    first, second_operand, third = jax.random.split(key, 3)
    baseline_value = jnp.exp(jax.random.uniform(first, array_extent, jnp.float32, jnp.log(0.5), jnp.log(2.0)))
    pulse_count = jax.random.uniform(second_operand, array_extent, jnp.float32) < 2.0 / N_BRICK
    total_quantity = jax.random.uniform(third, array_extent, jnp.float32, 0.2, 0.5) * N_BRICK
    return baseline_value + jnp.where(pulse_count, total_quantity, 0.0)


def draw_surface_over_flow_ratio(key, part):
    return jnp.exp(jax.random.uniform(key, (LINES,), jnp.float32, jnp.log(0.25), jnp.log(8.0))) / N_BRICK


def touch_ends(entries, rng, low, largest):
    shape = entries.shape
    index_at = [jax.random.randint(jax.random.fold_in(rng, axis), (), 0, shape[axis]) for axis in range(len(shape))]
    entries = entries.at[tuple(index_at)].set(low)
    longest = shape.index(max(shape))
    index_at[longest] = (index_at[longest] + 1) % shape[longest]
    return entries.at[tuple(index_at)].set(largest)


def setup_inputs(seed: int = 0, part: int = 0) -> dict:
    splits = jax.random.split(jax.random.key(seed), 10)
    own_keys = jax.random.split(jax.random.fold_in(splits[9], part), 10)
    return {
        "initial_voxel_degrees": draw_initial_voxel_degrees(jax.random.fold_in(jax.random.fold_in(splits[9], part), 71), part),
        "alloy_tag_per_voxel": touch_ends(jax.random.randint(splits[1], (NXT, NY, NZ), 0, MATS), jax.random.fold_in(splits[1], 1), 0, MATS - 1).astype(jnp.int32),
        "thermal_conductance_per_alloy": jnp.clip(jnp.exp(jax.random.uniform(splits[2], (MATS,), jnp.float32, math.log(0.2), math.log(1.0))), 0.2, 1.0),
        "specific_storage_per_alloy": jnp.clip(jnp.exp(jax.random.uniform(splits[3], (MATS,), jnp.float32, math.log(1.0), math.log(4.0))), 1.0, 4.0),
        "bore_boundary_positions": touch_ends(jax.random.randint(splits[4], (N_BRICK, LINES, WALL), 0, CX * NY * NZ), jax.random.fold_in(splits[4], 1), 0, (CX * NY * NZ) - 1).astype(jnp.int32),
        "surface_transfer_coefficient": draw_surface_transfer_coefficient(jax.random.fold_in(splits[9], 71), part),
        "surface_over_flow_ratio": draw_surface_over_flow_ratio(jax.random.fold_in(splits[9], 71), part),
        "flow_direction_flag": touch_ends(jax.random.randint(splits[7], (LINES,), 0, 2), jax.random.fold_in(splits[7], 1), 0, 1).astype(jnp.int32),
        "entry_coolant_degrees": jnp.clip(jax.random.uniform(own_keys[8], (LINES,), jnp.float32, -1.0, 0.0), -1.0, 0.0),
    }


def lookup(alloy_tag_per_voxel, table):
    result = jnp.zeros(alloy_tag_per_voxel.shape, table.dtype)
    for material in range(table.shape[0]):
        result = jnp.where(alloy_tag_per_voxel == material, table[material], result)
    return result


def face_mean(left, right):
    return 2.0 * left * right / (left + right + 1e-30)


def advance(updated_thermal_state, conduct, coeffs):
    center = updated_thermal_state[1:-1]
    center_cond = conduct[1:-1]
    fluxes = face_mean(center_cond, conduct[2:]) * (updated_thermal_state[2:] - center)
    fluxes = fluxes + face_mean(center_cond, conduct[:-2]) * (updated_thermal_state[:-2] - center)
    widths = ((0, 0), (1, 1), (0, 0))
    cond_pad = jnp.pad(center_cond, widths)
    heat_pad = jnp.pad(center, widths)
    fluxes = fluxes + face_mean(center_cond, cond_pad[:, 2:]) * (heat_pad[:, 2:] - center)
    fluxes = fluxes + face_mean(center_cond, cond_pad[:, :-2]) * (heat_pad[:, :-2] - center)
    widths = ((0, 0), (0, 0), (1, 1))
    cond_pad = jnp.pad(center_cond, widths)
    heat_pad = jnp.pad(center, widths)
    fluxes = fluxes + face_mean(center_cond, cond_pad[:, :, 2:]) * (heat_pad[:, :, 2:] - center)
    fluxes = fluxes + face_mean(center_cond, cond_pad[:, :, :-2]) * (heat_pad[:, :, :-2] - center)
    return center + coeffs[1:-1] * fluxes


def march(carry, pair):
    keep_row, gain_row = pair
    return keep_row * carry + gain_row, carry


def reference(initial_voxel_degrees, alloy_tag_per_voxel, thermal_conductance_per_alloy, specific_storage_per_alloy, bore_boundary_positions, surface_transfer_coefficient, surface_over_flow_ratio, flow_direction_flag, entry_coolant_degrees):
    conduct = lookup(alloy_tag_per_voxel, thermal_conductance_per_alloy)
    coeffs = 0.16 / lookup(alloy_tag_per_voxel, specific_storage_per_alloy)
    widths = ((1, 1), (0, 0), (0, 0))
    cond_pad = jnp.pad(conduct, widths)
    coeff_pad = jnp.pad(coeffs, widths)
    updated_thermal_state = initial_voxel_degrees
    for repeat in range(STEPS):
        updated_thermal_state = advance(jnp.pad(updated_thermal_state, widths), cond_pad, coeff_pad)
    flat = updated_thermal_state.reshape(-1)
    offsets = (jnp.arange(N_BRICK, dtype=jnp.int32) * (CX * NY * NZ))[:, None, None]
    global_cells = (bore_boundary_positions + offsets).astype(jnp.int32)
    wall_temps = flat[global_cells]
    wall_mean = jnp.mean(wall_temps, axis=2)
    keep = jnp.exp(-surface_over_flow_ratio[None, :] * surface_transfer_coefficient)
    gain = (1.0 - keep) * wall_mean
    _, forward_in = lax.scan(march, entry_coolant_degrees, (keep, gain))
    _, backward_in = lax.scan(march, entry_coolant_degrees, (keep, gain), reverse=True)
    inflow = jnp.where(flow_direction_flag[None, :] == 0, forward_in, backward_in)
    coolant_mid = 0.5 * (inflow + keep * inflow + gain)
    change = 0.5 * (1.0 - keep)[:, :, None] * (coolant_mid[:, :, None] - wall_temps)
    final = flat.at[global_cells.reshape(-1)].add(change.reshape(-1)).reshape(updated_thermal_state.shape)
    return final, coolant_mid
```

```python
import jax
import jax.numpy as jnp
from jax import lax
from jax.experimental import pallas as pl
from jax.experimental.pallas import tpu as pltpu
from jax.sharding import PartitionSpec as P

LANES = 128
PAD = 8
STRIP = 16
VMEM = pl.BlockSpec(memory_space=pltpu.VMEM)
SMEM = pl.BlockSpec(memory_space=pltpu.SMEM)
HBM = pl.BlockSpec(memory_space=pltpu.HBM)
HALVES = (0, 1)


def f32(*shape):
    return jax.ShapeDtypeStruct(shape, jnp.float32)


def i32(*shape):
    return jax.ShapeDtypeStruct(shape, jnp.int32)


def call(kernel, args, in_specs, out_shape, out_specs, scratch=(), cost=2_000_000, **kw):
    return pl.pallas_call(
        kernel,
        out_shape=out_shape,
        in_specs=in_specs,
        out_specs=out_specs,
        scratch_shapes=list(scratch),
        cost_estimate=pl.CostEstimate(flops=cost, bytes_accessed=cost, transcendentals=0),
        compiler_params=pltpu.CompilerParams(vmem_limit_bytes=12 << 20),
        **kw,
    )(*args)


def plane_of(j, planes):
    odd = lax.rem(lax.axis_index("brick"), 2)
    return jnp.where(odd == 1, j, planes - 1 - j)


def lanes_iota(rows):
    return lax.broadcasted_iota(jnp.int32, (rows, LANES), 1)


def pick(tag, table):
    level = [jnp.broadcast_to(v, tag.shape) for v in table]
    bit = 0
    while len(level) > 1:
        on = (tag & (1 << bit)) != 0
        if len(level) % 2:
            level.append(level[-1])
        level = [jnp.where(on, level[k + 1], level[k]) for k in range(0, len(level), 2)]
        bit += 1
    return level[0]


def face_mean(left, right):
    return 2.0 * left * right / (left + right + 1e-30)


def rows_loop(count, body, step=STRIP, unroll=4):
    def turn(s, carry):
        body(pl.multiple_of(s * step, step))
        return carry

    lax.fori_loop(0, count // step, turn, 0, unroll=unroll)


def advance_rows(cur, r, up, down, gx_up, gx_down, gy, ry, gz, coeff, rz):
    n = STRIP
    lane = lanes_iota(n)
    t = [cur[h, pl.ds(r, n), :] for h in HALVES]
    nxt = [pltpu.roll(t[h], LANES - 1, 1) for h in HALVES]
    ahead = [jnp.where(lane == LANES - 1, nxt[1], nxt[0]), nxt[1]]
    prv = [pltpu.roll(t[h], 1, 1) for h in HALVES]
    behind = [prv[0], jnp.where(lane == 0, prv[0], prv[1])]
    new = []
    for h in HALVES:
        c = t[h]
        flux = gx_up(h) * (up(h) - c) + gx_down(h) * (down(h) - c)
        flux = flux + gy[h, pl.ds(ry, n), :] * (cur[h, pl.ds(r + 1, n), :] - c)
        flux = flux + gy[h, pl.ds(ry - 1, n), :] * (cur[h, pl.ds(r - 1, n), :] - c)
        flux = flux + gz[h, pl.ds(rz, n), :] * (ahead[h] - c)
        flux = flux + gz[2 + h, pl.ds(rz, n), :] * (behind[h] - c)
        new.append(c + coeff[h, pl.ds(rz, n), :] * flux)
    return new


def main_planes(cur, last, halo, gxa, gxm, gy, gz, coeff, planes, ny, emit):
    def plane(j, first, final):
        def body(y):
            r = PAD + j * ny + y
            rz = j * ny + y

            def down(h):
                return halo[h, pl.ds(y, STRIP), :] if first else cur[h, pl.ds(r - ny, STRIP), :]

            def gx_down(h):
                return gxa[h, pl.ds(y, STRIP), :] if first else gxm[h, pl.ds(rz - ny, STRIP), :]

            def up(h):
                return last(h, y) if final else cur[h, pl.ds(r + ny, STRIP), :]

            def gx_up(h):
                return gxm[h, pl.ds(rz, STRIP), :]

            new = advance_rows(cur, r, up, down, gx_up, gx_down, gy, PAD + rz, gz, coeff, rz)
            emit(j, y, new, first)

        rows_loop(ny, body, unroll=8)

    plane(0, True, planes == 2)

    def inner(j, carry):
        plane(j, False, False)
        return carry

    lax.fori_loop(1, planes - 2, inner, 0)
    plane(planes - 2, False, True)


def send_kernel(t_ref, tag_ref, a_ref, b_ref, tags, sem):
    planes = t_ref.shape[0]
    copies = []
    for side, out in ((1, b_ref), (0, a_ref)):
        x = plane_of(0 if side == 0 else planes - 1, planes)
        for h in HALVES:
            part = pl.ds(h * LANES, LANES)
            copies.append(
                pltpu.make_async_copy(t_ref.at[x, :, part], out.at[0, h], sem.at[len(copies)])
            )
            copies.append(
                pltpu.make_async_copy(tag_ref.at[x, :, part], tags.at[side, h], sem.at[len(copies)])
            )
    for copy in copies:
        copy.start()
    for copy in copies:
        copy.wait()
    for side, out in ((1, b_ref), (0, a_ref)):
        for h in HALVES:
            out[1, h] = tags[side, h].astype(jnp.float32)


def prepare_kernel(
    t_ref, tag_ref, cond_ref, store_ref, halo, t0, gxa, gxm, gy, gz, coeff, t1, ta, tags, cond, sem
):
    planes, ny = t_ref.shape[0], t_ref.shape[1]
    copies = []
    for j in range(planes):
        x = plane_of(j, planes)
        for h in HALVES:
            part = pl.ds(h * LANES, LANES)
            rows = pl.ds(PAD + j * ny, ny)
            copies.append(pltpu.make_async_copy(tag_ref.at[x, :, part], tags.at[h, pl.ds(j * ny, ny)], sem.at[0, j, h]))
            copies.append(pltpu.make_async_copy(t_ref.at[x, :, part], t0.at[h, rows], sem.at[1, j, h]))
    for copy in copies:
        copy.start()
    zero = jnp.zeros((PAD, LANES), jnp.float32)
    for h in HALVES:
        for ref in (t0, t1, cond):
            ref[h, pl.ds(0, PAD), :] = zero
            ref[h, pl.ds(ref.shape[1] - PAD, PAD), :] = zero
        gy[h, pl.ds(0, PAD), :] = zero
    shape = (STRIP, LANES)
    lane = lanes_iota(STRIP)
    conds = [jnp.full((1, LANES), cond_ref[m], jnp.float32) for m in range(cond_ref.shape[0])]
    scales = [0.16 / jnp.full((1, LANES), store_ref[m], jnp.float32) for m in range(store_ref.shape[0])]
    for copy in copies:
        copy.wait()

    def materials(r):
        for h in HALVES:
            tag = tags[h, pl.ds(r, STRIP), :]
            cond[h, pl.ds(PAD + r, STRIP), :] = pick(tag, conds)
            coeff[h, pl.ds(r, STRIP), :] = pick(tag, scales)

    rows_loop(planes * ny, materials)

    def halo_face(y):
        for h in HALVES:
            other = pick(halo[1, h, pl.ds(y, STRIP), :].astype(jnp.int32), conds)
            gxa[h, pl.ds(y, STRIP), :] = face_mean(cond[h, pl.ds(PAD + y, STRIP), :], other)

    rows_loop(ny, halo_face)

    def x_faces(r):
        for h in HALVES:
            mine = cond[h, pl.ds(PAD + r, STRIP), :]
            gxm[h, pl.ds(r, STRIP), :] = face_mean(mine, cond[h, pl.ds(PAD + r + ny, STRIP), :])

    rows_loop((planes - 1) * ny, x_faces)

    def yz_faces(r):
        y = lax.rem(r, ny) + lax.broadcasted_iota(jnp.int32, shape, 0)
        mine = [cond[h, pl.ds(PAD + r, STRIP), :] for h in HALVES]
        nxt = [pltpu.roll(mine[h], LANES - 1, 1) for h in HALVES]
        ahead = [jnp.where(lane == LANES - 1, nxt[1], nxt[0]), nxt[1]]
        prv = [pltpu.roll(mine[h], 1, 1) for h in HALVES]
        behind = [prv[0], jnp.where(lane == 0, prv[0], prv[1])]
        for h in HALVES:
            below = face_mean(mine[h], cond[h, pl.ds(PAD + r + 1, STRIP), :])
            gy[h, pl.ds(PAD + r, STRIP), :] = jnp.where(y == ny - 1, 0.0, below)
            right = face_mean(mine[h], ahead[h])
            gz[h, pl.ds(r, STRIP), :] = jnp.where(lane == LANES - 1, 0.0, right) if h else right
            left = face_mean(behind[h], mine[h])
            gz[2 + h, pl.ds(r, STRIP), :] = left if h else jnp.where(lane == 0, 0.0, left)

    rows_loop(planes * ny, yz_faces)

    def emit(j, y, new, first):
        for h in HALVES:
            t1[h, pl.ds(PAD + j * ny + y, STRIP), :] = new[h]
            if first:
                ta[h, pl.ds(y, STRIP), :] = new[h]

    def last(h, y):
        return t0[h, pl.ds(PAD + (planes - 1) * ny + y, STRIP), :]

    main_planes(t0, last, halo.at[0], gxa, gxm, gy, gz, coeff, planes, ny, emit)


def last_plane(cur, below, halo, gxb, gxm, gy, gz, coeff, ny, emit):
    rows = gz.shape[1]
    base = rows - ny

    def body(y):
        new = advance_rows(
            cur,
            PAD + y,
            lambda h: halo[h, pl.ds(y, STRIP), :],
            lambda h: below(h, y),
            lambda h: gxb[h, pl.ds(y, STRIP), :],
            lambda h: gxm[h, pl.ds(base - ny + y, STRIP), :],
            gy,
            PAD + base + y,
            gz,
            coeff,
            base + y,
        )
        emit(y, new)

    rows_loop(ny, body, unroll=8)


def padded(pad, rows_of, ny):
    zero = jnp.zeros((PAD, LANES), jnp.float32)
    for h in HALVES:
        pad[h, pl.ds(0, PAD), :] = zero
        pad[h, pl.ds(PAD + ny, PAD), :] = zero

    def body(y):
        for h in HALVES:
            pad[h, pl.ds(PAD + y, STRIP), :] = rows_of(h, y)

    rows_loop(ny, body)


def first_last_kernel(brick_count, tag_ref, cond_ref, t0, halo, gxm, gy, gz, coeff, gxb, tb, pad, tags, sem):
    ny = tb.shape[1]
    planes = gz.shape[1] // ny
    base = (planes - 1) * ny
    x = plane_of(planes - 1, planes)
    copies = [
        pltpu.make_async_copy(tag_ref.at[x, :, pl.ds(h * LANES, LANES)], tags.at[h], sem.at[h])
        for h in HALVES
    ]
    for copy in copies:
        copy.start()
    me = lax.axis_index("brick")
    edge = (me == 0) | (me == brick_count - 1)
    keep = jnp.where(edge, 0.0, 1.0).astype(jnp.float32)
    conds = [jnp.full((1, LANES), cond_ref[m], jnp.float32) for m in range(cond_ref.shape[0])]
    padded(pad, lambda h, y: t0[h, pl.ds(PAD + base + y, STRIP), :], ny)
    for copy in copies:
        copy.wait()

    def faces(y):
        for h in HALVES:
            other = keep * pick(halo[1, h, pl.ds(y, STRIP), :].astype(jnp.int32), conds)
            mine = pick(tags[h, pl.ds(y, STRIP), :], conds)
            gxb[h, pl.ds(y, STRIP), :] = face_mean(mine, other)

    rows_loop(ny, faces)

    def emit(y, new):
        for h in HALVES:
            tb[h, pl.ds(y, STRIP), :] = new[h]

    def below(h, y):
        return t0[h, pl.ds(PAD + base - ny + y, STRIP), :]

    last_plane(pad, below, halo.at[0], gxb, gxm, gy, gz, coeff, ny, emit)


def next_last_kernel(tm, tb_old, halo, gxb, gxm, gy, gz, coeff, tb, pad):
    ny = tb.shape[1]
    planes = gz.shape[1] // ny
    padded(pad, lambda h, y: tb_old[h, pl.ds(y, STRIP), :], ny)

    def emit(y, new):
        for h in HALVES:
            tb[h, pl.ds(y, STRIP), :] = new[h]

    def below(h, y):
        return tm[h, pl.ds(PAD + (planes - 2) * ny + y, STRIP), :]

    last_plane(pad, below, halo, gxb, gxm, gy, gz, coeff, ny, emit)


def next_main_kernel(tm, tb_old, halo, gxa, gxm, gy, gz, coeff, out, ta):
    ny = ta.shape[1]
    planes = gz.shape[1] // ny
    zero = jnp.zeros((PAD, LANES), jnp.float32)
    for h in HALVES:
        out[h, pl.ds(0, PAD), :] = zero
        out[h, pl.ds(out.shape[1] - PAD, PAD), :] = zero

    def emit(j, y, new, first):
        for h in HALVES:
            out[h, pl.ds(PAD + j * ny + y, STRIP), :] = new[h]
            if first:
                ta[h, pl.ds(y, STRIP), :] = new[h]

    def last(h, y):
        return tb_old[h, pl.ds(y, STRIP), :]

    main_planes(tm, last, halo, gxa, gxm, gy, gz, coeff, planes, ny, emit)


def bin_rows(heat, owner, start, count, totals, lines):
    def turn(s, acc):
        r = pl.multiple_of(start + s * 8, 8)
        own = owner[pl.ds(r, 8), :]
        hot = heat[pl.ds(r, 8), :]
        return tuple(acc[k] + jnp.where(own == k, hot, 0.0) for k in range(lines))

    acc = lax.fori_loop(0, count // 8, turn, tuple(totals[k] for k in range(lines)), unroll=4)
    for k in range(lines):
        totals[k] = acc[k]


def final_main_kernel(tm, tb_old, halo, gxa, gxm, gy, gz, coeff, owner, heat, totals):
    ny = tb_old.shape[1]
    planes = gz.shape[1] // ny
    rows = planes * ny

    def emit(j, y, new, first):
        for h in HALVES:
            heat[pl.ds(h * rows + j * ny + y, STRIP), :] = new[h]

    def last(h, y):
        return tb_old[h, pl.ds(y, STRIP), :]

    main_planes(tm, last, halo, gxa, gxm, gy, gz, coeff, planes, ny, emit)
    totals[...] = jnp.zeros_like(totals)
    for h in HALVES:
        bin_rows(heat, owner, h * rows, rows - ny, totals, totals.shape[0])


def unpack(entry):
    row = lax.shift_right_logical(entry, 20)
    lane = lax.shift_right_logical(entry, 13) & (LANES - 1)
    return row, lane


def walls_kernel(
    wall, tm, tb_old, halo, gxb, gxm, gy, gz, coeff, owner, extra, extra_n, totals_in, film, ratio, heat_in, heat, send, pad, totals, sums
):
    ny = tb_old.shape[1]
    rows = gz.shape[1]
    planes = rows // ny
    lines = totals.shape[0]
    padded(pad, lambda h, y: tb_old[h, pl.ds(y, STRIP), :], ny)

    def emit(y, new):
        for h in HALVES:
            heat[pl.ds(h * rows + rows - ny + y, STRIP), :] = new[h]

    def below(h, y):
        return tm[h, pl.ds(PAD + (planes - 2) * ny + y, STRIP), :]

    last_plane(pad, below, halo, gxb, gxm, gy, gz, coeff, ny, emit)
    totals[...] = totals_in[...]
    for h in HALVES:
        bin_rows(heat, owner, h * rows + rows - ny, ny, totals, lines)
    sums[...] = jnp.sum(totals[...], axis=1)
    lane = lanes_iota(1)

    def more(n, carry):
        entry = extra[n]
        row, col = unpack(entry)
        line = lax.shift_right_logical(entry, wall.bit_length() - 1) & (lines - 1)
        hit = jnp.where(lane == col, heat[pl.ds(row, 1), :], 0.0)
        sums[pl.ds(line, 1), :] = sums[pl.ds(line, 1), :] + hit
        return carry

    lax.fori_loop(0, extra_n[0], more, 0)
    mean = lax.dot_general(
        jnp.ones((8, LANES), jnp.float32),
        sums[...],
        (((1,), (1,)), ((), ())),
        precision=lax.Precision.HIGHEST,
        preferred_element_type=jnp.float32,
    )[0:1] * (1.0 / wall)
    keep = jnp.exp(-ratio[...] * film[...])
    gain = (1.0 - keep) * mean
    count = send.shape[0]
    send[...] = jnp.zeros_like(send)
    send[:, 0:lines] = jnp.broadcast_to(keep, (count, lines))
    send[:, lines : 2 * lines] = jnp.broadcast_to(gain, (count, lines))


def owners_kernel(wall, keys, packed, ordered, owner, extra, extra_n, words, words_s, sem):
    rows, total = owner.shape[0], keys.shape[0]
    lines = total // wall
    bits = 32
    one = packed[...]
    depth = one.shape[0]
    nxt = pltpu.roll(one, LANES - 1, 1)
    wrap = pltpu.roll(nxt, depth - 1, 0)
    lane = lanes_iota(depth)
    place = lax.broadcasted_iota(jnp.int32, (depth, LANES), 0)
    after = jnp.where(lane == LANES - 1, wrap, nxt)
    same = lax.shift_right_logical(one ^ after, 13) == 0
    same = same & ((lane < LANES - 1) | (place < depth - 1))
    flag = jnp.where(same, lax.shift_left(jnp.int32(1), place & (bits - 1)), 0)
    words[...] = jnp.zeros_like(words)
    for g in range(depth // bits):
        words[pl.ds(g, 1), :] = jnp.sum(flag[g * bits : (g + 1) * bits], axis=0, keepdims=True)
    copy = pltpu.make_async_copy(words, words_s, sem)
    copy.start()

    def clear(r):
        owner[pl.ds(r, 64), :] = jnp.full((64, LANES), LANES - 1, jnp.int32)

    rows_loop(rows, clear, 64)
    ones = lanes_iota(1)
    unroll = 32

    def line(k, carry):
        value = jnp.full((1, LANES), k, jnp.int32)

        def body(s, inner):
            for u in range(unroll):
                key = keys[k * wall + s * unroll + u]
                row = lax.shift_right_logical(key, 7)
                pltpu.store(owner.at[pl.ds(row, 1), :], value, mask=ones == (key & (LANES - 1)))
            return inner

        return lax.fori_loop(0, wall // unroll, body, carry)

    lax.fori_loop(0, lines, line, 0)
    copy.wait()

    def lane_turn(c, n):
        for g in range(depth // bits):

            def go(state):
                word, n = state
                low = word & (-word)
                bit = 31 - lax.clz(low)
                extra[n] = ordered[(g * bits + bit) * LANES + c]
                return word ^ low, n + 1

            _, n = lax.while_loop(lambda state: state[0] != 0, go, (words_s[g, c], n))
        return n

    extra_n[0] = lax.fori_loop(0, LANES, lane_turn, 0)


def finish_kernel(
    wall, heat, owner, extra, extra_n, rows_all, film, ratio, direction, entry, out, mid, final, table, splat, sem
):
    planes, ny = out.shape[0], out.shape[1]
    rows = planes * ny
    count, lines = rows_all.shape[0], mid.shape[1]
    me = lax.axis_index("brick")

    def pass_on(k, water):
        row = rows_all[pl.ds(k, 1), :]
        return row[:, 0:lines] * water + row[:, lines : 2 * lines]

    start = entry[...]
    ahead = lax.fori_loop(0, me, pass_on, start)
    behind = lax.fori_loop(0, count - 1 - me, lambda k, w: pass_on(count - 1 - k, w), start)
    inflow = jnp.where(direction[...] == 0, ahead, behind)
    own = rows_all[pl.ds(me, 1), :]
    keep, gain = own[:, 0:lines], own[:, lines : 2 * lines]
    coolant = 0.5 * (inflow + keep * inflow + gain)
    mid[...] = coolant
    table[...] = jnp.zeros_like(table)
    table[0:1, 0:lines] = 0.5 * (1.0 - keep)
    table[1:2, 0:lines] = coolant
    eye = lax.broadcasted_iota(jnp.int32, (lines, LANES), 0) == lanes_iota(lines)
    for k in range(2):
        spread = jnp.broadcast_to(table[k : k + 1, :], (lines, LANES))
        column = jnp.sum(jnp.where(eye, spread, 0.0), axis=1, keepdims=True)
        splat[k] = jnp.broadcast_to(column, (lines, LANES))
    pull = jnp.broadcast_to(table[0:1, :], (8, LANES))
    cool = jnp.broadcast_to(table[1:2, :], (8, LANES))

    def dense(r):
        own = owner[pl.ds(r, 8), :]
        hot = heat[pl.ds(r, 8), :]
        a = jnp.take_along_axis(pull, own, axis=1)
        c = jnp.take_along_axis(cool, own, axis=1)
        final[pl.ds(r, 8), :] = hot + a * (c - hot)

    rows_loop(2 * rows, dense, 8, unroll=16)
    lane = lanes_iota(1)

    def more(n, carry):
        item = extra[n]
        row, col = unpack(item)
        line = lax.shift_right_logical(item, wall.bit_length() - 1) & (lines - 1)
        a = splat[0, pl.ds(line, 1), :]
        c = splat[1, pl.ds(line, 1), :]
        hot = heat[pl.ds(row, 1), :]
        final[pl.ds(row, 1), :] = final[pl.ds(row, 1), :] + jnp.where(lane == col, a * (c - hot), 0.0)
        return carry

    lax.fori_loop(0, extra_n[0], more, 0)
    copies = []
    for j in range(planes):
        x = plane_of(j, planes)
        for h in HALVES:
            copies.append(
                pltpu.make_async_copy(
                    final.at[pl.ds(h * rows + j * ny, ny), :],
                    out.at[x, :, pl.ds(h * LANES, LANES)],
                    sem.at[j, h],
                )
            )
    for copy in copies:
        copy.start()
    for copy in copies:
        copy.wait()


def per_device(
    initial_voxel_degrees,
    alloy_tag_per_voxel,
    thermal_conductance_per_alloy,
    specific_storage_per_alloy,
    bore_boundary_positions,
    surface_transfer_coefficient,
    surface_over_flow_ratio,
    flow_direction_flag,
    entry_coolant_degrees,
):
    planes, ny, nz = initial_voxel_degrees.shape
    _, lines, wall = bore_boundary_positions.shape
    rows, hits = planes * ny, lines * wall
    count = lax.axis_size("brick")
    me = lax.axis_index("brick")
    dma = pltpu.SemaphoreType.DMA
    on_chip = [(i, i ^ 1) for i in range(count)]
    across = [(i, (i + 1) % count) for i in range(1, count, 2)]
    across = across + [(b, a) for a, b in across]

    def swap(value, pairs):
        return lax.ppermute(value, "brick", pairs)

    plane = f32(2, ny, LANES)
    pair = f32(2, 2, ny, LANES)
    ta, tb = call(
        send_kernel,
        (initial_voxel_degrees, alloy_tag_per_voxel),
        [HBM, HBM],
        (pair, pair),
        (VMEM, VMEM),
        [pltpu.VMEM((2, 2, ny, LANES), jnp.int32), dma((8,))],
    )
    halo_b = swap(tb, across)
    halo_a = swap(ta, on_chip)

    cell = bore_boundary_positions.reshape(hits)
    flip = jnp.where(lax.rem(me, 2) == 1, 0, (planes - 1) * ny * nz)
    cell = cell ^ flip
    keys = ((cell & LANES) * (rows * LANES // LANES)) | ((cell >> 8) << 7) | (cell & (LANES - 1))
    packed = lax.sort(keys * 8192 + lax.iota(jnp.int32, hits), is_stable=False)
    owner, extra, extra_n = call(
        lambda *refs: owners_kernel(wall, *refs),
        (keys, packed.reshape(hits // LANES, LANES), packed),
        [SMEM, VMEM, SMEM],
        (i32(2 * rows, LANES), i32(hits), i32(1)),
        (VMEM, SMEM, SMEM),
        [pltpu.VMEM((8, LANES), jnp.int32), pltpu.SMEM((8, LANES), jnp.int32), dma],
        cost=20_000_000,
    )

    full = f32(2, rows + 2 * PAD, LANES)
    most = f32(2, rows - ny + 2 * PAD, LANES)
    t0, gxa, gxm, gy, gz, coeff, t1, ta = call(
        prepare_kernel,
        (
            initial_voxel_degrees,
            alloy_tag_per_voxel,
            thermal_conductance_per_alloy,
            specific_storage_per_alloy,
            halo_a,
        ),
        [HBM, HBM, SMEM, SMEM, VMEM],
        (full, plane, f32(2, rows - ny, LANES), full, f32(4, rows, LANES), f32(2, rows, LANES), most, plane),
        (VMEM,) * 8,
        [
            pltpu.VMEM((2, rows, LANES), jnp.int32),
            pltpu.VMEM((2, rows + 2 * PAD, LANES), jnp.float32),
            dma((2, planes, 2)),
        ],
        cost=10_000_000,
    )
    pad = pltpu.VMEM((2, ny + 2 * PAD, LANES), jnp.float32)
    gxb, tb = call(
        lambda *refs: first_last_kernel(count, *refs),
        (alloy_tag_per_voxel, thermal_conductance_per_alloy, t0, halo_b, gxm, gy, gz, coeff),
        [HBM, SMEM] + [VMEM] * 6,
        (plane, plane),
        (VMEM, VMEM),
        [pad, pltpu.VMEM((2, ny, LANES), jnp.int32), dma((2,))],
    )
    halo_b = swap(tb, across)
    halo_a = swap(ta, on_chip)

    t2, ta = call(
        next_main_kernel,
        (t1, tb, halo_a, gxa, gxm, gy, gz, coeff),
        [VMEM] * 8,
        (most, plane),
        (VMEM, VMEM),
        cost=4_000_000,
    )
    tb2 = call(
        next_last_kernel,
        (t1, tb, halo_b, gxb, gxm, gy, gz, coeff),
        [VMEM] * 8,
        plane,
        VMEM,
        [pad],
    )
    halo_b = swap(tb2, across)
    halo_a = swap(ta, on_chip)

    heat, totals = call(
        final_main_kernel,
        (t2, tb2, halo_a, gxa, gxm, gy, gz, coeff, owner),
        [VMEM] * 9,
        (f32(2 * rows, LANES), f32(lines, 8, LANES)),
        (VMEM, VMEM),
        cost=10_000_000,
    )
    ratio = surface_over_flow_ratio.reshape(1, lines)
    heat, send = call(
        lambda *refs: walls_kernel(wall, *refs),
        (t2, tb2, halo_b, gxb, gxm, gy, gz, coeff, owner, extra, extra_n, totals, surface_transfer_coefficient, ratio, heat),
        [VMEM] * 9 + [SMEM, SMEM] + [VMEM] * 4,
        (f32(2 * rows, LANES), f32(count, LANES)),
        (VMEM, VMEM),
        [pad, pltpu.VMEM((lines, 8, LANES), jnp.float32), pltpu.VMEM((lines, LANES), jnp.float32)],
        input_output_aliases={14: 0},
    )
    rows_all = lax.all_to_all(send, "brick", 0, 0, tiled=True)
    final, mid = call(
        lambda *refs: finish_kernel(wall, *refs),
        (
            heat,
            owner,
            extra,
            extra_n,
            rows_all,
            surface_transfer_coefficient,
            ratio,
            flow_direction_flag.reshape(1, lines),
            entry_coolant_degrees.reshape(1, lines),
        ),
        [VMEM, VMEM, SMEM, SMEM] + [VMEM] * 5,
        (f32(planes, ny, nz), f32(1, lines)),
        (HBM, VMEM),
        [
            pltpu.VMEM((2 * rows, LANES), jnp.float32),
            pltpu.VMEM((8, LANES), jnp.float32),
            pltpu.VMEM((2, lines, LANES), jnp.float32),
            dma((planes, 2)),
        ],
    )
    return final, mid


def solution(mesh):
    return jax.shard_map(
        per_device,
        mesh=mesh,
        in_specs=(
            P(("pour", "brick"), None, None),
            P("brick", None, None),
            P(),
            P(),
            P("brick", None, None),
            P("brick", None),
            P(),
            P(),
            P("pour"),
        ),
        out_specs=(P(("pour", "brick"), None, None), P(("pour", "brick"), None)),
        check_vma=False,
    )
```

```python
import jax
import jax.numpy as jnp
from jax import lax
from jax.experimental import pallas as pl
from jax.experimental.pallas import tpu as pltpu
from jax.sharding import PartitionSpec as P

LANES = 128
PAD = 8
STRIP = 16
VMEM = pl.BlockSpec(memory_space=pltpu.VMEM)
SMEM = pl.BlockSpec(memory_space=pltpu.SMEM)
HBM = pl.BlockSpec(memory_space=pltpu.HBM)
HALVES = (0, 1)


def f32(*shape):
    return jax.ShapeDtypeStruct(shape, jnp.float32)


def i32(*shape):
    return jax.ShapeDtypeStruct(shape, jnp.int32)


def call(kernel, args, in_specs, out_shape, out_specs, scratch=(), cost=2_000_000, **kw):
    return pl.pallas_call(
        kernel,
        out_shape=out_shape,
        in_specs=in_specs,
        out_specs=out_specs,
        scratch_shapes=list(scratch),
        cost_estimate=pl.CostEstimate(flops=cost, bytes_accessed=cost, transcendentals=0),
        compiler_params=pltpu.CompilerParams(vmem_limit_bytes=12 << 20),
        **kw,
    )(*args)


def plane_of(j, planes):
    odd = lax.rem(lax.axis_index("brick"), 2)
    return jnp.where(odd == 1, j, planes - 1 - j)


def lanes_iota(rows):
    return lax.broadcasted_iota(jnp.int32, (rows, LANES), 1)


def pick(tag, table):
    level = [jnp.broadcast_to(v, tag.shape) for v in table]
    bit = 0
    while len(level) > 1:
        on = (tag & (1 << bit)) != 0
        if len(level) % 2:
            level.append(level[-1])
        level = [jnp.where(on, level[k + 1], level[k]) for k in range(0, len(level), 2)]
        bit += 1
    return level[0]


def face_mean(left, right):
    return 2.0 * left * right / (left + right + 1e-30)


def rows_loop(count, body, step=STRIP, unroll=4):
    def turn(s, carry):
        body(pl.multiple_of(s * step, step))
        return carry

    lax.fori_loop(0, count // step, turn, 0, unroll=unroll)


def advance_rows(cur, r, up, down, gx_up, gx_down, gy, ry, gz, coeff, rz):
    n = STRIP
    lane = lanes_iota(n)
    t = [cur[h, pl.ds(r, n), :] for h in HALVES]
    nxt = [pltpu.roll(t[h], LANES - 1, 1) for h in HALVES]
    ahead = [jnp.where(lane == LANES - 1, nxt[1], nxt[0]), nxt[1]]
    prv = [pltpu.roll(t[h], 1, 1) for h in HALVES]
    behind = [prv[0], jnp.where(lane == 0, prv[0], prv[1])]
    new = []
    for h in HALVES:
        c = t[h]
        flux = gx_up(h) * (up(h) - c) + gx_down(h) * (down(h) - c)
        flux = flux + gy[h, pl.ds(ry, n), :] * (cur[h, pl.ds(r + 1, n), :] - c)
        flux = flux + gy[h, pl.ds(ry - 1, n), :] * (cur[h, pl.ds(r - 1, n), :] - c)
        flux = flux + gz[h, pl.ds(rz, n), :] * (ahead[h] - c)
        flux = flux + gz[2 + h, pl.ds(rz, n), :] * (behind[h] - c)
        new.append(c + coeff[h, pl.ds(rz, n), :] * flux)
    return new


def main_planes(cur, last, halo, gxa, gxm, gy, gz, coeff, planes, ny, emit):
    def plane(j, first, final):
        def body(y):
            r = PAD + j * ny + y
            rz = j * ny + y

            def down(h):
                return halo[h, pl.ds(y, STRIP), :] if first else cur[h, pl.ds(r - ny, STRIP), :]

            def gx_down(h):
                return gxa[h, pl.ds(y, STRIP), :] if first else gxm[h, pl.ds(rz - ny, STRIP), :]

            def up(h):
                return last(h, y) if final else cur[h, pl.ds(r + ny, STRIP), :]

            def gx_up(h):
                return gxm[h, pl.ds(rz, STRIP), :]

            new = advance_rows(cur, r, up, down, gx_up, gx_down, gy, PAD + rz, gz, coeff, rz)
            emit(j, y, new, first)

        rows_loop(ny, body, unroll=8)

    plane(0, True, planes == 2)

    def inner(j, carry):
        plane(j, False, False)
        return carry

    lax.fori_loop(1, planes - 2, inner, 0)
    plane(planes - 2, False, True)


def send_kernel(t_ref, tag_ref, a_ref, b_ref, tags, sem):
    planes = t_ref.shape[0]
    copies = []
    for side, out in ((1, b_ref), (0, a_ref)):
        x = plane_of(0 if side == 0 else planes - 1, planes)
        for h in HALVES:
            part = pl.ds(h * LANES, LANES)
            copies.append(
                pltpu.make_async_copy(t_ref.at[x, :, part], out.at[0, h], sem.at[len(copies)])
            )
            copies.append(
                pltpu.make_async_copy(tag_ref.at[x, :, part], tags.at[side, h], sem.at[len(copies)])
            )
    for copy in copies:
        copy.start()
    for copy in copies:
        copy.wait()
    for side, out in ((1, b_ref), (0, a_ref)):
        for h in HALVES:
            out[1, h] = tags[side, h].astype(jnp.float32)


def prepare_kernel(
    t_ref, tag_ref, cond_ref, store_ref, halo, t0, gxa, gxm, gy, gz, coeff, t1, ta, tags, cond, sem
):
    planes, ny = t_ref.shape[0], t_ref.shape[1]
    copies = []
    for j in range(planes):
        x = plane_of(j, planes)
        for h in HALVES:
            part = pl.ds(h * LANES, LANES)
            rows = pl.ds(PAD + j * ny, ny)
            copies.append(pltpu.make_async_copy(tag_ref.at[x, :, part], tags.at[h, pl.ds(j * ny, ny)], sem.at[0, j, h]))
            copies.append(pltpu.make_async_copy(t_ref.at[x, :, part], t0.at[h, rows], sem.at[1, j, h]))
    for copy in copies:
        copy.start()
    zero = jnp.zeros((PAD, LANES), jnp.float32)
    for h in HALVES:
        for ref in (t0, t1, cond):
            ref[h, pl.ds(0, PAD), :] = zero
            ref[h, pl.ds(ref.shape[1] - PAD, PAD), :] = zero
        gy[h, pl.ds(0, PAD), :] = zero
    shape = (STRIP, LANES)
    lane = lanes_iota(STRIP)
    conds = [jnp.full((1, LANES), cond_ref[m], jnp.float32) for m in range(cond_ref.shape[0])]
    scales = [0.16 / jnp.full((1, LANES), store_ref[m], jnp.float32) for m in range(store_ref.shape[0])]
    for copy in copies:
        copy.wait()

    def materials(r):
        for h in HALVES:
            tag = tags[h, pl.ds(r, STRIP), :]
            cond[h, pl.ds(PAD + r, STRIP), :] = pick(tag, conds)
            coeff[h, pl.ds(r, STRIP), :] = pick(tag, scales)

    rows_loop(planes * ny, materials)

    def halo_face(y):
        for h in HALVES:
            other = pick(halo[1, h, pl.ds(y, STRIP), :].astype(jnp.int32), conds)
            gxa[h, pl.ds(y, STRIP), :] = face_mean(cond[h, pl.ds(PAD + y, STRIP), :], other)

    rows_loop(ny, halo_face)

    def x_faces(r):
        for h in HALVES:
            mine = cond[h, pl.ds(PAD + r, STRIP), :]
            gxm[h, pl.ds(r, STRIP), :] = face_mean(mine, cond[h, pl.ds(PAD + r + ny, STRIP), :])

    rows_loop((planes - 1) * ny, x_faces)

    def yz_faces(r):
        y = lax.rem(r, ny) + lax.broadcasted_iota(jnp.int32, shape, 0)
        mine = [cond[h, pl.ds(PAD + r, STRIP), :] for h in HALVES]
        nxt = [pltpu.roll(mine[h], LANES - 1, 1) for h in HALVES]
        ahead = [jnp.where(lane == LANES - 1, nxt[1], nxt[0]), nxt[1]]
        prv = [pltpu.roll(mine[h], 1, 1) for h in HALVES]
        behind = [prv[0], jnp.where(lane == 0, prv[0], prv[1])]
        for h in HALVES:
            below = face_mean(mine[h], cond[h, pl.ds(PAD + r + 1, STRIP), :])
            gy[h, pl.ds(PAD + r, STRIP), :] = jnp.where(y == ny - 1, 0.0, below)
            right = face_mean(mine[h], ahead[h])
            gz[h, pl.ds(r, STRIP), :] = jnp.where(lane == LANES - 1, 0.0, right) if h else right
            left = face_mean(behind[h], mine[h])
            gz[2 + h, pl.ds(r, STRIP), :] = left if h else jnp.where(lane == 0, 0.0, left)

    rows_loop(planes * ny, yz_faces)

    def emit(j, y, new, first):
        for h in HALVES:
            t1[h, pl.ds(PAD + j * ny + y, STRIP), :] = new[h]
            if first:
                ta[h, pl.ds(y, STRIP), :] = new[h]

    def last(h, y):
        return t0[h, pl.ds(PAD + (planes - 1) * ny + y, STRIP), :]

    main_planes(t0, last, halo.at[0], gxa, gxm, gy, gz, coeff, planes, ny, emit)


def last_plane(cur, below, halo, gxb, gxm, gy, gz, coeff, ny, emit):
    rows = gz.shape[1]
    base = rows - ny

    def body(y):
        new = advance_rows(
            cur,
            PAD + y,
            lambda h: halo[h, pl.ds(y, STRIP), :],
            lambda h: below(h, y),
            lambda h: gxb[h, pl.ds(y, STRIP), :],
            lambda h: gxm[h, pl.ds(base - ny + y, STRIP), :],
            gy,
            PAD + base + y,
            gz,
            coeff,
            base + y,
        )
        emit(y, new)

    rows_loop(ny, body, unroll=8)


def padded(pad, rows_of, ny):
    zero = jnp.zeros((PAD, LANES), jnp.float32)
    for h in HALVES:
        pad[h, pl.ds(0, PAD), :] = zero
        pad[h, pl.ds(PAD + ny, PAD), :] = zero

    def body(y):
        for h in HALVES:
            pad[h, pl.ds(PAD + y, STRIP), :] = rows_of(h, y)

    rows_loop(ny, body)


def first_last_kernel(brick_count, tag_ref, cond_ref, t0, halo, gxm, gy, gz, coeff, gxb, tb, pad, tags, sem):
    ny = tb.shape[1]
    planes = gz.shape[1] // ny
    base = (planes - 1) * ny
    x = plane_of(planes - 1, planes)
    copies = [
        pltpu.make_async_copy(tag_ref.at[x, :, pl.ds(h * LANES, LANES)], tags.at[h], sem.at[h])
        for h in HALVES
    ]
    for copy in copies:
        copy.start()
    me = lax.axis_index("brick")
    edge = (me == 0) | (me == brick_count - 1)
    keep = jnp.where(edge, 0.0, 1.0).astype(jnp.float32)
    conds = [jnp.full((1, LANES), cond_ref[m], jnp.float32) for m in range(cond_ref.shape[0])]
    padded(pad, lambda h, y: t0[h, pl.ds(PAD + base + y, STRIP), :], ny)
    for copy in copies:
        copy.wait()

    def faces(y):
        for h in HALVES:
            other = keep * pick(halo[1, h, pl.ds(y, STRIP), :].astype(jnp.int32), conds)
            mine = pick(tags[h, pl.ds(y, STRIP), :], conds)
            gxb[h, pl.ds(y, STRIP), :] = face_mean(mine, other)

    rows_loop(ny, faces)

    def emit(y, new):
        for h in HALVES:
            tb[h, pl.ds(y, STRIP), :] = new[h]

    def below(h, y):
        return t0[h, pl.ds(PAD + base - ny + y, STRIP), :]

    last_plane(pad, below, halo.at[0], gxb, gxm, gy, gz, coeff, ny, emit)


def next_last_kernel(tm, tb_old, halo, gxb, gxm, gy, gz, coeff, tb, pad):
    ny = tb.shape[1]
    planes = gz.shape[1] // ny
    padded(pad, lambda h, y: tb_old[h, pl.ds(y, STRIP), :], ny)

    def emit(y, new):
        for h in HALVES:
            tb[h, pl.ds(y, STRIP), :] = new[h]

    def below(h, y):
        return tm[h, pl.ds(PAD + (planes - 2) * ny + y, STRIP), :]

    last_plane(pad, below, halo, gxb, gxm, gy, gz, coeff, ny, emit)


def next_main_kernel(tm, tb_old, halo, gxa, gxm, gy, gz, coeff, out, ta):
    ny = ta.shape[1]
    planes = gz.shape[1] // ny
    zero = jnp.zeros((PAD, LANES), jnp.float32)
    for h in HALVES:
        out[h, pl.ds(0, PAD), :] = zero
        out[h, pl.ds(out.shape[1] - PAD, PAD), :] = zero

    def emit(j, y, new, first):
        for h in HALVES:
            out[h, pl.ds(PAD + j * ny + y, STRIP), :] = new[h]
            if first:
                ta[h, pl.ds(y, STRIP), :] = new[h]

    def last(h, y):
        return tb_old[h, pl.ds(y, STRIP), :]

    main_planes(tm, last, halo, gxa, gxm, gy, gz, coeff, planes, ny, emit)


def bin_rows(heat, owner, start, count, totals, lines):
    def turn(s, acc):
        r = pl.multiple_of(start + s * 8, 8)
        own = owner[pl.ds(r, 8), :]
        hot = heat[pl.ds(r, 8), :]
        return tuple(acc[k] + jnp.where(own == k, hot, 0.0) for k in range(lines))

    acc = lax.fori_loop(0, count // 8, turn, tuple(totals[k] for k in range(lines)), unroll=4)
    for k in range(lines):
        totals[k] = acc[k]


def final_main_kernel(tm, tb_old, halo, gxa, gxm, gy, gz, coeff, owner, heat, totals):
    ny = tb_old.shape[1]
    planes = gz.shape[1] // ny
    rows = planes * ny

    def emit(j, y, new, first):
        for h in HALVES:
            heat[pl.ds(h * rows + plane_of(j, planes) * ny + y, STRIP), :] = new[h]

    def last(h, y):
        return tb_old[h, pl.ds(y, STRIP), :]

    main_planes(tm, last, halo, gxa, gxm, gy, gz, coeff, planes, ny, emit)
    totals[...] = jnp.zeros_like(totals)
    for h in HALVES:
        first = jnp.where(plane_of(planes - 1, planes) == 0, ny, 0)
        bin_rows(heat, owner, h * rows + first, rows - ny, totals, totals.shape[0])


def unpack(entry):
    row = lax.shift_right_logical(entry, 20)
    lane = lax.shift_right_logical(entry, 13) & (LANES - 1)
    return row, lane


def walls_kernel(
    wall, tm, tb_old, halo, gxb, gxm, gy, gz, coeff, owner, extra, extra_n, totals_in, film, ratio, heat_in, heat, send, pad, totals, sums
):
    ny = tb_old.shape[1]
    rows = gz.shape[1]
    planes = rows // ny
    lines = totals.shape[0]
    at = plane_of(planes - 1, planes) * ny
    padded(pad, lambda h, y: tb_old[h, pl.ds(y, STRIP), :], ny)

    def emit(y, new):
        for h in HALVES:
            heat[pl.ds(h * rows + at + y, STRIP), :] = new[h]

    def below(h, y):
        return tm[h, pl.ds(PAD + (planes - 2) * ny + y, STRIP), :]

    last_plane(pad, below, halo, gxb, gxm, gy, gz, coeff, ny, emit)
    totals[...] = totals_in[...]
    for h in HALVES:
        bin_rows(heat, owner, h * rows + at, ny, totals, lines)
    sums[...] = jnp.sum(totals[...], axis=1)
    lane = lanes_iota(1)

    def more(n, carry):
        entry = extra[n]
        row, col = unpack(entry)
        line = lax.shift_right_logical(entry, wall.bit_length() - 1) & (lines - 1)
        hit = jnp.where(lane == col, heat[pl.ds(row, 1), :], 0.0)
        sums[pl.ds(line, 1), :] = sums[pl.ds(line, 1), :] + hit
        return carry

    lax.fori_loop(0, extra_n[0], more, 0)
    mean = lax.dot_general(
        jnp.ones((8, LANES), jnp.float32),
        sums[...],
        (((1,), (1,)), ((), ())),
        precision=lax.Precision.HIGHEST,
        preferred_element_type=jnp.float32,
    )[0:1] * (1.0 / wall)
    keep = jnp.exp(-ratio[...] * film[...])
    gain = (1.0 - keep) * mean
    count = send.shape[0]
    send[...] = jnp.zeros_like(send)
    send[:, 0:lines] = jnp.broadcast_to(keep, (count, lines))
    send[:, lines : 2 * lines] = jnp.broadcast_to(gain, (count, lines))


def owners_kernel(wall, keys, packed, ordered, owner, extra, extra_n, words, words_s, sem):
    rows, total = owner.shape[0], keys.shape[0]
    lines = total // wall
    bits = 32
    one = packed[...]
    depth = one.shape[0]
    nxt = pltpu.roll(one, LANES - 1, 1)
    wrap = pltpu.roll(nxt, depth - 1, 0)
    lane = lanes_iota(depth)
    place = lax.broadcasted_iota(jnp.int32, (depth, LANES), 0)
    after = jnp.where(lane == LANES - 1, wrap, nxt)
    same = lax.shift_right_logical(one ^ after, 13) == 0
    same = same & ((lane < LANES - 1) | (place < depth - 1))
    flag = jnp.where(same, lax.shift_left(jnp.int32(1), place & (bits - 1)), 0)
    words[...] = jnp.zeros_like(words)
    for g in range(depth // bits):
        words[pl.ds(g, 1), :] = jnp.sum(flag[g * bits : (g + 1) * bits], axis=0, keepdims=True)
    copy = pltpu.make_async_copy(words, words_s, sem)
    copy.start()

    def clear(r):
        owner[pl.ds(r, 64), :] = jnp.full((64, LANES), LANES - 1, jnp.int32)

    rows_loop(rows, clear, 64)
    ones = lanes_iota(1)
    unroll = 32

    def line(k, carry):
        value = jnp.full((1, LANES), k, jnp.int32)

        def body(s, inner):
            for u in range(unroll):
                key = keys[k * wall + s * unroll + u]
                row = lax.shift_right_logical(key, 7)
                pltpu.store(owner.at[pl.ds(row, 1), :], value, mask=ones == (key & (LANES - 1)))
            return inner

        return lax.fori_loop(0, wall // unroll, body, carry)

    lax.fori_loop(0, lines, line, 0)
    copy.wait()

    def lane_turn(c, n):
        for g in range(depth // bits):

            def go(state):
                word, n = state
                low = word & (-word)
                bit = 31 - lax.clz(low)
                extra[n] = ordered[(g * bits + bit) * LANES + c]
                return word ^ low, n + 1

            _, n = lax.while_loop(lambda state: state[0] != 0, go, (words_s[g, c], n))
        return n

    extra_n[0] = lax.fori_loop(0, LANES, lane_turn, 0)


def finish_kernel(
    wall, heat, owner, extra, extra_n, rows_all, film, ratio, direction, entry, out, mid, final, table, splat, sem
):
    planes, ny = out.shape[0], out.shape[1]
    rows = planes * ny
    count, lines = rows_all.shape[0], mid.shape[1]
    me = lax.axis_index("brick")

    def pass_on(k, water):
        row = rows_all[pl.ds(k, 1), :]
        return row[:, 0:lines] * water + row[:, lines : 2 * lines]

    start = entry[...]
    ahead = lax.fori_loop(0, me, pass_on, start)
    behind = lax.fori_loop(0, count - 1 - me, lambda k, w: pass_on(count - 1 - k, w), start)
    inflow = jnp.where(direction[...] == 0, ahead, behind)
    own = rows_all[pl.ds(me, 1), :]
    keep, gain = own[:, 0:lines], own[:, lines : 2 * lines]
    coolant = 0.5 * (inflow + keep * inflow + gain)
    mid[...] = coolant
    table[...] = jnp.zeros_like(table)
    table[0:1, 0:lines] = 0.5 * (1.0 - keep)
    table[1:2, 0:lines] = coolant
    eye = lax.broadcasted_iota(jnp.int32, (lines, LANES), 0) == lanes_iota(lines)
    for k in range(2):
        spread = jnp.broadcast_to(table[k : k + 1, :], (lines, LANES))
        column = jnp.sum(jnp.where(eye, spread, 0.0), axis=1, keepdims=True)
        splat[k] = jnp.broadcast_to(column, (lines, LANES))
    pull = jnp.broadcast_to(table[0:1, :], (8, LANES))
    cool = jnp.broadcast_to(table[1:2, :], (8, LANES))

    def dense(r):
        own = owner[pl.ds(r, 8), :]
        hot = heat[pl.ds(r, 8), :]
        a = jnp.take_along_axis(pull, own, axis=1)
        c = jnp.take_along_axis(cool, own, axis=1)
        final[pl.ds(r, 8), :] = hot + a * (c - hot)

    rows_loop(2 * rows, dense, 8, unroll=16)
    lane = lanes_iota(1)

    def more(n, carry):
        item = extra[n]
        row, col = unpack(item)
        line = lax.shift_right_logical(item, wall.bit_length() - 1) & (lines - 1)
        a = splat[0, pl.ds(line, 1), :]
        c = splat[1, pl.ds(line, 1), :]
        hot = heat[pl.ds(row, 1), :]
        final[pl.ds(row, 1), :] = final[pl.ds(row, 1), :] + jnp.where(lane == col, a * (c - hot), 0.0)
        return carry

    lax.fori_loop(0, extra_n[0], more, 0)
    copies = []
    for x in range(planes):
        for h in HALVES:
            copies.append(
                pltpu.make_async_copy(
                    final.at[pl.ds(h * rows + x * ny, ny), :],
                    out.at[x, :, pl.ds(h * LANES, LANES)],
                    sem.at[x, h],
                )
            )
    for copy in copies:
        copy.start()
    for copy in copies:
        copy.wait()


def per_device(
    initial_voxel_degrees,
    alloy_tag_per_voxel,
    thermal_conductance_per_alloy,
    specific_storage_per_alloy,
    bore_boundary_positions,
    surface_transfer_coefficient,
    surface_over_flow_ratio,
    flow_direction_flag,
    entry_coolant_degrees,
):
    planes, ny, nz = initial_voxel_degrees.shape
    _, lines, wall = bore_boundary_positions.shape
    rows, hits = planes * ny, lines * wall
    count = lax.axis_size("brick")
    dma = pltpu.SemaphoreType.DMA
    on_chip = [(i, i ^ 1) for i in range(count)]
    across = [(i, (i + 1) % count) for i in range(1, count, 2)]
    across = across + [(b, a) for a, b in across]

    def swap(value, pairs):
        return lax.ppermute(value, "brick", pairs)

    initial_voxel_degrees = pltpu.with_memory_space_constraint(initial_voxel_degrees, pltpu.HBM)
    alloy_tag_per_voxel = pltpu.with_memory_space_constraint(alloy_tag_per_voxel, pltpu.HBM)

    plane = f32(2, ny, LANES)
    pair = f32(2, 2, ny, LANES)
    ta, tb = call(
        send_kernel,
        (initial_voxel_degrees, alloy_tag_per_voxel),
        [HBM, HBM],
        (pair, pair),
        (VMEM, VMEM),
        [pltpu.VMEM((2, 2, ny, LANES), jnp.int32), dma((8,))],
    )
    halo_b = swap(tb, across)
    halo_a = swap(ta, on_chip)

    cell = bore_boundary_positions.reshape(hits)
    keys = ((cell & LANES) * (rows * LANES // LANES)) | ((cell >> 8) << 7) | (cell & (LANES - 1))
    packed = lax.sort(keys * 8192 + lax.iota(jnp.int32, hits), is_stable=False)
    halo_a, keys, packed = lax.optimization_barrier((halo_a, keys, packed))
    owner, extra, extra_n = call(
        lambda *refs: owners_kernel(wall, *refs),
        (keys, packed.reshape(hits // LANES, LANES), packed),
        [SMEM, VMEM, SMEM],
        (i32(2 * rows, LANES), i32(hits), i32(1)),
        (VMEM, SMEM, SMEM),
        [pltpu.VMEM((8, LANES), jnp.int32), pltpu.SMEM((8, LANES), jnp.int32), dma],
        cost=20_000_000,
    )

    full = f32(2, rows + 2 * PAD, LANES)
    most = f32(2, rows - ny + 2 * PAD, LANES)
    t0, gxa, gxm, gy, gz, coeff, t1, ta = call(
        prepare_kernel,
        (
            initial_voxel_degrees,
            alloy_tag_per_voxel,
            thermal_conductance_per_alloy,
            specific_storage_per_alloy,
            halo_a,
        ),
        [HBM, HBM, SMEM, SMEM, VMEM],
        (full, plane, f32(2, rows - ny, LANES), full, f32(4, rows, LANES), f32(2, rows, LANES), most, plane),
        (VMEM,) * 8,
        [
            pltpu.VMEM((2, rows, LANES), jnp.int32),
            pltpu.VMEM((2, rows + 2 * PAD, LANES), jnp.float32),
            dma((2, planes, 2)),
        ],
        cost=10_000_000,
    )
    pad = pltpu.VMEM((2, ny + 2 * PAD, LANES), jnp.float32)
    gxb, tb = call(
        lambda *refs: first_last_kernel(count, *refs),
        (alloy_tag_per_voxel, thermal_conductance_per_alloy, t0, halo_b, gxm, gy, gz, coeff),
        [HBM, SMEM] + [VMEM] * 6,
        (plane, plane),
        (VMEM, VMEM),
        [pad, pltpu.VMEM((2, ny, LANES), jnp.int32), dma((2,))],
    )
    halo_b = swap(tb, across)
    halo_a = swap(ta, on_chip)

    t2, ta = call(
        next_main_kernel,
        (t1, tb, halo_a, gxa, gxm, gy, gz, coeff),
        [VMEM] * 8,
        (most, plane),
        (VMEM, VMEM),
        cost=4_000_000,
    )
    tb2 = call(
        next_last_kernel,
        (t1, tb, halo_b, gxb, gxm, gy, gz, coeff),
        [VMEM] * 8,
        plane,
        VMEM,
        [pad],
    )
    halo_b = swap(tb2, across)
    halo_a = swap(ta, on_chip)

    heat, totals = call(
        final_main_kernel,
        (t2, tb2, halo_a, gxa, gxm, gy, gz, coeff, owner),
        [VMEM] * 9,
        (f32(2 * rows, LANES), f32(lines, 8, LANES)),
        (VMEM, VMEM),
        cost=10_000_000,
    )
    ratio = surface_over_flow_ratio.reshape(1, lines)
    heat, send = call(
        lambda *refs: walls_kernel(wall, *refs),
        (t2, tb2, halo_b, gxb, gxm, gy, gz, coeff, owner, extra, extra_n, totals, surface_transfer_coefficient, ratio, heat),
        [VMEM] * 9 + [SMEM, SMEM] + [VMEM] * 4,
        (f32(2 * rows, LANES), f32(count, LANES)),
        (VMEM, VMEM),
        [pad, pltpu.VMEM((lines, 8, LANES), jnp.float32), pltpu.VMEM((lines, LANES), jnp.float32)],
        input_output_aliases={14: 0},
    )
    rows_all = lax.all_to_all(send, "brick", 0, 0, tiled=True)
    final, mid = call(
        lambda *refs: finish_kernel(wall, *refs),
        (
            heat,
            owner,
            extra,
            extra_n,
            rows_all,
            surface_transfer_coefficient,
            ratio,
            flow_direction_flag.reshape(1, lines),
            entry_coolant_degrees.reshape(1, lines),
        ),
        [VMEM, VMEM, SMEM, SMEM] + [VMEM] * 5,
        (f32(planes, ny, nz), f32(1, lines)),
        (HBM, VMEM),
        [
            pltpu.VMEM((2 * rows, LANES), jnp.float32),
            pltpu.VMEM((8, LANES), jnp.float32),
            pltpu.VMEM((2, lines, LANES), jnp.float32),
            dma((planes, 2)),
        ],
    )
    return final, mid


def solution(mesh):
    return jax.shard_map(
        per_device,
        mesh=mesh,
        in_specs=(
            P(("pour", "brick"), None, None),
            P("brick", None, None),
            P(),
            P(),
            P("brick", None, None),
            P("brick", None),
            P(),
            P(),
            P("pour"),
        ),
        out_specs=(P(("pour", "brick"), None, None), P(("pour", "brick"), None)),
        check_vma=False,
    )
```

```python
import jax
import jax.numpy as jnp
from jax import lax
from jax.experimental import pallas as pl
from jax.experimental.pallas import tpu as pltpu
from jax.sharding import PartitionSpec as P

LANES = 128
PAD = 8
STRIP = 16
WINDOW = 96
VMEM = pl.BlockSpec(memory_space=pltpu.VMEM)
SMEM = pl.BlockSpec(memory_space=pltpu.SMEM)
HBM = pl.BlockSpec(memory_space=pltpu.HBM)
HALVES = (0, 1)


def f32(*shape):
    return jax.ShapeDtypeStruct(shape, jnp.float32)


def i32(*shape):
    return jax.ShapeDtypeStruct(shape, jnp.int32)


def call(kernel, args, in_specs, out_shape, out_specs, scratch=(), cost=2_000_000, **kw):
    return pl.pallas_call(
        kernel,
        out_shape=out_shape,
        in_specs=in_specs,
        out_specs=out_specs,
        scratch_shapes=list(scratch),
        cost_estimate=pl.CostEstimate(flops=cost, bytes_accessed=cost, transcendentals=0),
        compiler_params=pltpu.CompilerParams(vmem_limit_bytes=12 << 20),
        **kw,
    )(*args)


def plane_of(j, planes):
    odd = lax.rem(lax.axis_index("brick"), 2)
    return jnp.where(odd == 1, j, planes - 1 - j)


def lanes_iota(rows):
    return lax.broadcasted_iota(jnp.int32, (rows, LANES), 1)


def pick(tag, table):
    level = [jnp.broadcast_to(v, tag.shape) for v in table]
    bit = 0
    while len(level) > 1:
        on = (tag & (1 << bit)) != 0
        if len(level) % 2:
            level.append(level[-1])
        level = [jnp.where(on, level[k + 1], level[k]) for k in range(0, len(level), 2)]
        bit += 1
    return level[0]


def face_mean(left, right):
    return 2.0 * left * right / (left + right + 1e-30)


def rows_loop(count, body, step=STRIP, unroll=4):
    def turn(s, carry):
        body(pl.multiple_of(s * step, step))
        return carry

    lax.fori_loop(0, count // step, turn, 0, unroll=unroll)


def advance_rows(cur, r, up, down, gx_up, gx_down, gy, ry, gz, coeff, rz):
    n = STRIP
    lane = lanes_iota(n)
    t = [cur[h, pl.ds(r, n), :] for h in HALVES]
    nxt = [pltpu.roll(t[h], LANES - 1, 1) for h in HALVES]
    ahead = [jnp.where(lane == LANES - 1, nxt[1], nxt[0]), nxt[1]]
    prv = [pltpu.roll(t[h], 1, 1) for h in HALVES]
    behind = [prv[0], jnp.where(lane == 0, prv[0], prv[1])]
    new = []
    for h in HALVES:
        c = t[h]
        flux = gx_up(h) * (up(h) - c) + gx_down(h) * (down(h) - c)
        flux = flux + gy[h, pl.ds(ry, n), :] * (cur[h, pl.ds(r + 1, n), :] - c)
        flux = flux + gy[h, pl.ds(ry - 1, n), :] * (cur[h, pl.ds(r - 1, n), :] - c)
        flux = flux + gz[h, pl.ds(rz, n), :] * (ahead[h] - c)
        flux = flux + gz[2 + h, pl.ds(rz, n), :] * (behind[h] - c)
        new.append(c + coeff[h, pl.ds(rz, n), :] * flux)
    return new


def main_planes(cur, last, halo, gxa, gxm, gy, gz, coeff, planes, ny, emit):
    def plane(j, first, final):
        def body(y):
            r = PAD + j * ny + y
            rz = j * ny + y

            def down(h):
                return halo[h, pl.ds(y, STRIP), :] if first else cur[h, pl.ds(r - ny, STRIP), :]

            def gx_down(h):
                return gxa[h, pl.ds(y, STRIP), :] if first else gxm[h, pl.ds(rz - ny, STRIP), :]

            def up(h):
                return last(h, y) if final else cur[h, pl.ds(r + ny, STRIP), :]

            def gx_up(h):
                return gxm[h, pl.ds(rz, STRIP), :]

            new = advance_rows(cur, r, up, down, gx_up, gx_down, gy, PAD + rz, gz, coeff, rz)
            emit(j, y, new, first)

        rows_loop(ny, body, unroll=8)

    plane(0, True, planes == 2)

    def inner(j, carry):
        plane(j, False, False)
        return carry

    lax.fori_loop(1, planes - 2, inner, 0)
    plane(planes - 2, False, True)


def send_kernel(t_ref, tag_ref, a_ref, b_ref, tags, sem):
    planes = t_ref.shape[0]
    copies = []
    for side, out in ((1, b_ref), (0, a_ref)):
        x = plane_of(0 if side == 0 else planes - 1, planes)
        for h in HALVES:
            part = pl.ds(h * LANES, LANES)
            copies.append(
                pltpu.make_async_copy(t_ref.at[x, :, part], out.at[0, h], sem.at[len(copies)])
            )
            copies.append(
                pltpu.make_async_copy(tag_ref.at[x, :, part], tags.at[side, h], sem.at[len(copies)])
            )
    for copy in copies:
        copy.start()
    for copy in copies:
        copy.wait()
    for side, out in ((1, b_ref), (0, a_ref)):
        for h in HALVES:
            out[1, h] = tags[side, h].astype(jnp.float32)


def prepare_kernel(
    t_ref, tag_ref, cond_ref, store_ref, halo, t0, gxa, gxm, gy, gz, coeff, t1, ta, tags, cond, sem
):
    planes, ny = t_ref.shape[0], t_ref.shape[1]
    copies = []
    for j in range(planes):
        x = plane_of(j, planes)
        for h in HALVES:
            part = pl.ds(h * LANES, LANES)
            rows = pl.ds(PAD + j * ny, ny)
            copies.append(pltpu.make_async_copy(tag_ref.at[x, :, part], tags.at[h, pl.ds(j * ny, ny)], sem.at[0, j, h]))
            copies.append(pltpu.make_async_copy(t_ref.at[x, :, part], t0.at[h, rows], sem.at[1, j, h]))
    for copy in copies:
        copy.start()
    zero = jnp.zeros((PAD, LANES), jnp.float32)
    for h in HALVES:
        for ref in (t0, t1, cond):
            ref[h, pl.ds(0, PAD), :] = zero
            ref[h, pl.ds(ref.shape[1] - PAD, PAD), :] = zero
        gy[h, pl.ds(0, PAD), :] = zero
    shape = (STRIP, LANES)
    lane = lanes_iota(STRIP)
    conds = [jnp.full((1, LANES), cond_ref[m], jnp.float32) for m in range(cond_ref.shape[0])]
    scales = [0.16 / jnp.full((1, LANES), store_ref[m], jnp.float32) for m in range(store_ref.shape[0])]
    for copy in copies:
        copy.wait()

    def materials(r):
        for h in HALVES:
            tag = tags[h, pl.ds(r, STRIP), :]
            cond[h, pl.ds(PAD + r, STRIP), :] = pick(tag, conds)
            coeff[h, pl.ds(r, STRIP), :] = pick(tag, scales)

    rows_loop(planes * ny, materials)

    def halo_face(y):
        for h in HALVES:
            other = pick(halo[1, h, pl.ds(y, STRIP), :].astype(jnp.int32), conds)
            gxa[h, pl.ds(y, STRIP), :] = face_mean(cond[h, pl.ds(PAD + y, STRIP), :], other)

    rows_loop(ny, halo_face)

    def x_faces(r):
        for h in HALVES:
            mine = cond[h, pl.ds(PAD + r, STRIP), :]
            gxm[h, pl.ds(r, STRIP), :] = face_mean(mine, cond[h, pl.ds(PAD + r + ny, STRIP), :])

    rows_loop((planes - 1) * ny, x_faces)

    def yz_faces(r):
        y = lax.rem(r, ny) + lax.broadcasted_iota(jnp.int32, shape, 0)
        mine = [cond[h, pl.ds(PAD + r, STRIP), :] for h in HALVES]
        nxt = [pltpu.roll(mine[h], LANES - 1, 1) for h in HALVES]
        ahead = [jnp.where(lane == LANES - 1, nxt[1], nxt[0]), nxt[1]]
        prv = [pltpu.roll(mine[h], 1, 1) for h in HALVES]
        behind = [prv[0], jnp.where(lane == 0, prv[0], prv[1])]
        for h in HALVES:
            below = face_mean(mine[h], cond[h, pl.ds(PAD + r + 1, STRIP), :])
            gy[h, pl.ds(PAD + r, STRIP), :] = jnp.where(y == ny - 1, 0.0, below)
            right = face_mean(mine[h], ahead[h])
            gz[h, pl.ds(r, STRIP), :] = jnp.where(lane == LANES - 1, 0.0, right) if h else right
            left = face_mean(behind[h], mine[h])
            gz[2 + h, pl.ds(r, STRIP), :] = left if h else jnp.where(lane == 0, 0.0, left)

    rows_loop(planes * ny, yz_faces)

    def emit(j, y, new, first):
        for h in HALVES:
            t1[h, pl.ds(PAD + j * ny + y, STRIP), :] = new[h]
            if first:
                ta[h, pl.ds(y, STRIP), :] = new[h]

    def last(h, y):
        return t0[h, pl.ds(PAD + (planes - 1) * ny + y, STRIP), :]

    main_planes(t0, last, halo.at[0], gxa, gxm, gy, gz, coeff, planes, ny, emit)


def last_plane(cur, below, halo, gxb, gxm, gy, gz, coeff, ny, emit):
    rows = gz.shape[1]
    base = rows - ny

    def body(y):
        new = advance_rows(
            cur,
            PAD + y,
            lambda h: halo[h, pl.ds(y, STRIP), :],
            lambda h: below(h, y),
            lambda h: gxb[h, pl.ds(y, STRIP), :],
            lambda h: gxm[h, pl.ds(base - ny + y, STRIP), :],
            gy,
            PAD + base + y,
            gz,
            coeff,
            base + y,
        )
        emit(y, new)

    rows_loop(ny, body, unroll=8)


def padded(pad, rows_of, ny):
    zero = jnp.zeros((PAD, LANES), jnp.float32)
    for h in HALVES:
        pad[h, pl.ds(0, PAD), :] = zero
        pad[h, pl.ds(PAD + ny, PAD), :] = zero

    def body(y):
        for h in HALVES:
            pad[h, pl.ds(PAD + y, STRIP), :] = rows_of(h, y)

    rows_loop(ny, body)


def first_last_kernel(brick_count, tag_ref, cond_ref, t0, halo, gxm, gy, gz, coeff, gxb, tb, pad, tags, sem):
    ny = tb.shape[1]
    planes = gz.shape[1] // ny
    base = (planes - 1) * ny
    x = plane_of(planes - 1, planes)
    copies = [
        pltpu.make_async_copy(tag_ref.at[x, :, pl.ds(h * LANES, LANES)], tags.at[h], sem.at[h])
        for h in HALVES
    ]
    for copy in copies:
        copy.start()
    me = lax.axis_index("brick")
    edge = (me == 0) | (me == brick_count - 1)
    keep = jnp.where(edge, 0.0, 1.0).astype(jnp.float32)
    conds = [jnp.full((1, LANES), cond_ref[m], jnp.float32) for m in range(cond_ref.shape[0])]
    padded(pad, lambda h, y: t0[h, pl.ds(PAD + base + y, STRIP), :], ny)
    for copy in copies:
        copy.wait()

    def faces(y):
        for h in HALVES:
            other = keep * pick(halo[1, h, pl.ds(y, STRIP), :].astype(jnp.int32), conds)
            mine = pick(tags[h, pl.ds(y, STRIP), :], conds)
            gxb[h, pl.ds(y, STRIP), :] = face_mean(mine, other)

    rows_loop(ny, faces)

    def emit(y, new):
        for h in HALVES:
            tb[h, pl.ds(y, STRIP), :] = new[h]

    def below(h, y):
        return t0[h, pl.ds(PAD + base - ny + y, STRIP), :]

    last_plane(pad, below, halo.at[0], gxb, gxm, gy, gz, coeff, ny, emit)


def next_last_kernel(tm, tb_old, halo, gxb, gxm, gy, gz, coeff, tb, pad):
    ny = tb.shape[1]
    planes = gz.shape[1] // ny
    padded(pad, lambda h, y: tb_old[h, pl.ds(y, STRIP), :], ny)

    def emit(y, new):
        for h in HALVES:
            tb[h, pl.ds(y, STRIP), :] = new[h]

    def below(h, y):
        return tm[h, pl.ds(PAD + (planes - 2) * ny + y, STRIP), :]

    last_plane(pad, below, halo, gxb, gxm, gy, gz, coeff, ny, emit)


def next_main_kernel(tm, tb_old, halo, gxa, gxm, gy, gz, coeff, out, ta):
    ny = ta.shape[1]
    planes = gz.shape[1] // ny
    zero = jnp.zeros((PAD, LANES), jnp.float32)
    for h in HALVES:
        out[h, pl.ds(0, PAD), :] = zero
        out[h, pl.ds(out.shape[1] - PAD, PAD), :] = zero

    def emit(j, y, new, first):
        for h in HALVES:
            out[h, pl.ds(PAD + j * ny + y, STRIP), :] = new[h]
            if first:
                ta[h, pl.ds(y, STRIP), :] = new[h]

    def last(h, y):
        return tb_old[h, pl.ds(y, STRIP), :]

    main_planes(tm, last, halo, gxa, gxm, gy, gz, coeff, planes, ny, emit)


def bin_rows(heat, owner, start, count, totals, lines):
    def turn(s, acc):
        r = pl.multiple_of(start + s * 8, 8)
        own = owner[pl.ds(r, 8), :]
        hot = heat[pl.ds(r, 8), :]
        return tuple(acc[k] + jnp.where(own == k + 1.0, hot, 0.0) for k in range(lines))

    acc = lax.fori_loop(0, count // 8, turn, tuple(totals[k] for k in range(lines)), unroll=4)
    for k in range(lines):
        totals[k] = acc[k]


def final_main_kernel(tm, tb_old, halo, gxa, gxm, gy, gz, coeff, owner, heat, totals):
    ny = tb_old.shape[1]
    planes = gz.shape[1] // ny
    rows = planes * ny

    def emit(j, y, new, first):
        for h in HALVES:
            heat[pl.ds(h * rows + plane_of(j, planes) * ny + y, STRIP), :] = new[h]

    def last(h, y):
        return tb_old[h, pl.ds(y, STRIP), :]

    main_planes(tm, last, halo, gxa, gxm, gy, gz, coeff, planes, ny, emit)
    totals[...] = jnp.zeros_like(totals)
    for h in HALVES:
        first = jnp.where(plane_of(planes - 1, planes) == 0, ny, 0)
        bin_rows(heat, owner, h * rows + first, rows - ny, totals, totals.shape[0])


def unpack(entry, half_rows):
    row = lax.shift_right_arithmetic(entry, 20) + half_rows
    lane = lax.shift_right_logical(entry, 13) & (LANES - 1)
    return row, lane


def walls_kernel(
    wall, tm, tb_old, halo, gxb, gxm, gy, gz, coeff, owner, extra, extra_n, totals_in, film, ratio, heat_in, heat, send, pad, totals, sums
):
    ny = tb_old.shape[1]
    rows = gz.shape[1]
    planes = rows // ny
    lines = totals.shape[0]
    at = plane_of(planes - 1, planes) * ny
    padded(pad, lambda h, y: tb_old[h, pl.ds(y, STRIP), :], ny)

    def emit(y, new):
        for h in HALVES:
            heat[pl.ds(h * rows + at + y, STRIP), :] = new[h]

    def below(h, y):
        return tm[h, pl.ds(PAD + (planes - 2) * ny + y, STRIP), :]

    last_plane(pad, below, halo, gxb, gxm, gy, gz, coeff, ny, emit)
    totals[...] = totals_in[...]
    for h in HALVES:
        bin_rows(heat, owner, h * rows + at, ny, totals, lines)
    sums[...] = jnp.sum(totals[...], axis=1)
    lane = lanes_iota(1)

    def more(n, carry):
        entry = extra[n]
        row, col = unpack(entry, rows)
        line = lax.shift_right_logical(entry, wall.bit_length() - 1) & (lines - 1)
        hit = jnp.where(lane == col, heat[pl.ds(row, 1), :], 0.0)
        sums[pl.ds(line, 1), :] = sums[pl.ds(line, 1), :] + hit
        return carry

    lax.fori_loop(0, extra_n[0], more, 0)
    mean = lax.dot_general(
        jnp.ones((8, LANES), jnp.float32),
        sums[...],
        (((1,), (1,)), ((), ())),
        precision=lax.Precision.HIGHEST,
        preferred_element_type=jnp.float32,
    )[0:1] * (1.0 / wall)
    keep = jnp.exp(-ratio[...] * film[...])
    gain = (1.0 - keep) * mean
    count = send.shape[0]
    send[...] = jnp.zeros_like(send)
    send[:, 0:lines] = jnp.broadcast_to(keep, (count, lines))
    send[:, lines : 2 * lines] = jnp.broadcast_to(gain, (count, lines))


def owners_kernel(wall, packed, ordered, owner, extra, extra_n, row_of, col_of, value, words, words_s, sem):
    bits = 32
    window = WINDOW
    rows = owner.shape[0] - window
    one = packed[...]
    depth = one.shape[0]
    nxt = pltpu.roll(one, LANES - 1, 1)
    wrap = pltpu.roll(nxt, depth - 1, 0)
    lane = lanes_iota(depth)
    place = lax.broadcasted_iota(jnp.int32, (depth, LANES), 0)
    after = jnp.where(lane == LANES - 1, wrap, nxt)
    same = lax.shift_right_logical(one ^ after, 13) == 0
    same = same & ((lane < LANES - 1) | (place < depth - 1))
    flag = jnp.where(same, lax.shift_left(jnp.int32(1), place & (bits - 1)), 0)
    words[...] = jnp.zeros_like(words)
    for g in range(depth // bits):
        words[pl.ds(g, 1), :] = jnp.sum(flag[g * bits : (g + 1) * bits], axis=0, keepdims=True)
    copy = pltpu.make_async_copy(words, words_s, sem)
    copy.start()
    row_of[...] = lax.shift_right_arithmetic(one, 20) + rows // 2
    col_of[...] = lax.shift_right_logical(one, 13) & (LANES - 1)
    line = lax.shift_right_logical(one & 8191, wall.bit_length() - 1)
    value[...] = jnp.where(same, 0, line + 1).astype(jnp.float32)

    def clear(r):
        owner[pl.ds(r, 32), :] = jnp.zeros((32, LANES), jnp.float32)

    rows_loop(rows + window, clear, 32)
    tall = lax.broadcasted_iota(jnp.int32, (window, LANES), 0)
    square = lax.broadcasted_iota(jnp.int32, (LANES, LANES), 0)

    def row_at(i):
        return lax.shift_right_arithmetic(ordered[i], 20) + rows // 2

    def block(c, base):
        at = jnp.where(tall == row_of[pl.ds(c, 1), :] - base, 1.0, 0.0).astype(jnp.bfloat16)
        what = jnp.where(square == col_of[pl.ds(c, 1), :], value[pl.ds(c, 1), :], 0.0)
        return lax.dot_general(
            at,
            what.astype(jnp.bfloat16),
            (((1,), (1,)), ((), ())),
            preferred_element_type=jnp.float32,
        )

    def first_base(c):
        return pl.multiple_of(row_at(c * LANES) & -8, 8)

    group = 8

    def turn(g, carry):
        chunks = [g * group + u for u in range(group)]
        bases = [first_base(c) for c in chunks]
        blocks = [block(c, base) for c, base in zip(chunks, bases)]
        for base, found in zip(bases, blocks):
            owner[pl.ds(base, window), :] = owner[pl.ds(base, window), :] + found
        return carry

    lax.fori_loop(0, depth // group, turn, 0)

    def rest(c, carry):
        last = row_at(c * LANES + LANES - 1)

        def go(base):
            base = pl.multiple_of(base, 8)
            owner[pl.ds(base, window), :] = owner[pl.ds(base, window), :] + block(c, base)
            return base + window

        lax.while_loop(lambda base: base <= last, go, first_base(c) + window)
        return carry

    lax.fori_loop(0, depth, rest, 0)
    copy.wait()

    def lane_turn(c, n):
        for g in range(depth // bits):

            def go(state):
                word, n = state
                low = word & (-word)
                bit = 31 - lax.clz(low)
                extra[n] = ordered[(g * bits + bit) * LANES + c]
                return word ^ low, n + 1

            _, n = lax.while_loop(lambda state: state[0] != 0, go, (words_s[g, c], n))
        return n

    extra_n[0] = lax.fori_loop(0, LANES, lane_turn, 0)


def finish_kernel(
    wall, heat, owner, extra, extra_n, rows_all, film, ratio, direction, entry, out, mid, final, table, splat, sem
):
    planes, ny = out.shape[0], out.shape[1]
    rows = planes * ny
    count, lines = rows_all.shape[0], mid.shape[1]
    me = lax.axis_index("brick")

    def pass_on(k, water):
        row = rows_all[pl.ds(k, 1), :]
        return row[:, 0:lines] * water + row[:, lines : 2 * lines]

    start = entry[...]
    ahead = lax.fori_loop(0, me, pass_on, start)
    behind = lax.fori_loop(0, count - 1 - me, lambda k, w: pass_on(count - 1 - k, w), start)
    inflow = jnp.where(direction[...] == 0, ahead, behind)
    own = rows_all[pl.ds(me, 1), :]
    keep, gain = own[:, 0:lines], own[:, lines : 2 * lines]
    coolant = 0.5 * (inflow + keep * inflow + gain)
    mid[...] = coolant
    table[...] = jnp.zeros_like(table)
    table[0:1, 1 : lines + 1] = 0.5 * (1.0 - keep)
    table[1:2, 1 : lines + 1] = coolant
    eye = lax.broadcasted_iota(jnp.int32, (lines, LANES), 0) + 1 == lanes_iota(lines)
    for k in range(2):
        spread = jnp.broadcast_to(table[k : k + 1, :], (lines, LANES))
        column = jnp.sum(jnp.where(eye, spread, 0.0), axis=1, keepdims=True)
        splat[k] = jnp.broadcast_to(column, (lines, LANES))
    pull = jnp.broadcast_to(table[0:1, :], (8, LANES))
    cool = jnp.broadcast_to(table[1:2, :], (8, LANES))

    def dense(r):
        own = owner[pl.ds(r, 8), :].astype(jnp.int32)
        hot = heat[pl.ds(r, 8), :]
        a = jnp.take_along_axis(pull, own, axis=1)
        c = jnp.take_along_axis(cool, own, axis=1)
        final[pl.ds(r, 8), :] = hot + a * (c - hot)

    rows_loop(2 * rows, dense, 8, unroll=16)
    lane = lanes_iota(1)

    def more(n, carry):
        item = extra[n]
        row, col = unpack(item, rows)
        line = lax.shift_right_logical(item, wall.bit_length() - 1) & (lines - 1)
        a = splat[0, pl.ds(line, 1), :]
        c = splat[1, pl.ds(line, 1), :]
        hot = heat[pl.ds(row, 1), :]
        final[pl.ds(row, 1), :] = final[pl.ds(row, 1), :] + jnp.where(lane == col, a * (c - hot), 0.0)
        return carry

    lax.fori_loop(0, extra_n[0], more, 0)
    copies = []
    for x in range(planes):
        for h in HALVES:
            copies.append(
                pltpu.make_async_copy(
                    final.at[pl.ds(h * rows + x * ny, ny), :],
                    out.at[x, :, pl.ds(h * LANES, LANES)],
                    sem.at[x, h],
                )
            )
    for copy in copies:
        copy.start()
    for copy in copies:
        copy.wait()


def per_device(
    initial_voxel_degrees,
    alloy_tag_per_voxel,
    thermal_conductance_per_alloy,
    specific_storage_per_alloy,
    bore_boundary_positions,
    surface_transfer_coefficient,
    surface_over_flow_ratio,
    flow_direction_flag,
    entry_coolant_degrees,
):
    planes, ny, nz = initial_voxel_degrees.shape
    _, lines, wall = bore_boundary_positions.shape
    rows, hits = planes * ny, lines * wall
    count = lax.axis_size("brick")
    dma = pltpu.SemaphoreType.DMA
    on_chip = [(i, i ^ 1) for i in range(count)]
    across = [(i, (i + 1) % count) for i in range(1, count, 2)]
    across = across + [(b, a) for a, b in across]

    def swap(value, pairs):
        return lax.ppermute(value, "brick", pairs)

    initial_voxel_degrees = pltpu.with_memory_space_constraint(initial_voxel_degrees, pltpu.HBM)
    alloy_tag_per_voxel = pltpu.with_memory_space_constraint(alloy_tag_per_voxel, pltpu.HBM)

    plane = f32(2, ny, LANES)
    pair = f32(2, 2, ny, LANES)
    ta, tb = call(
        send_kernel,
        (initial_voxel_degrees, alloy_tag_per_voxel),
        [HBM, HBM],
        (pair, pair),
        (VMEM, VMEM),
        [pltpu.VMEM((2, 2, ny, LANES), jnp.int32), dma((8,))],
    )
    halo_b = swap(tb, across)
    halo_a = swap(ta, on_chip)

    cell = bore_boundary_positions.reshape(hits)
    keys = ((cell & LANES) * (rows * LANES // LANES)) | ((cell >> 8) << 7) | (cell & (LANES - 1))
    keys = keys ^ (rows * LANES)
    packed = lax.sort(keys * 8192 + lax.iota(jnp.int32, hits), is_stable=False)
    halo_a, packed = lax.optimization_barrier((halo_a, packed))
    owner, extra, extra_n = call(
        lambda *refs: owners_kernel(wall, *refs),
        (packed.reshape(hits // LANES, LANES), packed),
        [VMEM, SMEM],
        (f32(2 * rows + WINDOW, LANES), i32(hits), i32(1)),
        (VMEM, SMEM, SMEM),
        [pltpu.VMEM((hits // LANES, LANES), jnp.int32)] * 2
        + [pltpu.VMEM((hits // LANES, LANES), jnp.float32)]
        + [pltpu.VMEM((8, LANES), jnp.int32), pltpu.SMEM((8, LANES), jnp.int32), dma],
        cost=20_000_000,
    )

    full = f32(2, rows + 2 * PAD, LANES)
    most = f32(2, rows - ny + 2 * PAD, LANES)
    t0, gxa, gxm, gy, gz, coeff, t1, ta = call(
        prepare_kernel,
        (
            initial_voxel_degrees,
            alloy_tag_per_voxel,
            thermal_conductance_per_alloy,
            specific_storage_per_alloy,
            halo_a,
        ),
        [HBM, HBM, SMEM, SMEM, VMEM],
        (full, plane, f32(2, rows - ny, LANES), full, f32(4, rows, LANES), f32(2, rows, LANES), most, plane),
        (VMEM,) * 8,
        [
            pltpu.VMEM((2, rows, LANES), jnp.int32),
            pltpu.VMEM((2, rows + 2 * PAD, LANES), jnp.float32),
            dma((2, planes, 2)),
        ],
        cost=10_000_000,
    )
    pad = pltpu.VMEM((2, ny + 2 * PAD, LANES), jnp.float32)
    gxb, tb = call(
        lambda *refs: first_last_kernel(count, *refs),
        (alloy_tag_per_voxel, thermal_conductance_per_alloy, t0, halo_b, gxm, gy, gz, coeff),
        [HBM, SMEM] + [VMEM] * 6,
        (plane, plane),
        (VMEM, VMEM),
        [pad, pltpu.VMEM((2, ny, LANES), jnp.int32), dma((2,))],
    )
    halo_b = swap(tb, across)
    halo_a = swap(ta, on_chip)

    t2, ta = call(
        next_main_kernel,
        (t1, tb, halo_a, gxa, gxm, gy, gz, coeff),
        [VMEM] * 8,
        (most, plane),
        (VMEM, VMEM),
        cost=4_000_000,
    )
    tb2 = call(
        next_last_kernel,
        (t1, tb, halo_b, gxb, gxm, gy, gz, coeff),
        [VMEM] * 8,
        plane,
        VMEM,
        [pad],
    )
    halo_b = swap(tb2, across)
    halo_a = swap(ta, on_chip)

    heat, totals = call(
        final_main_kernel,
        (t2, tb2, halo_a, gxa, gxm, gy, gz, coeff, owner),
        [VMEM] * 9,
        (f32(2 * rows, LANES), f32(lines, 8, LANES)),
        (VMEM, VMEM),
        cost=10_000_000,
    )
    ratio = surface_over_flow_ratio.reshape(1, lines)
    heat, send = call(
        lambda *refs: walls_kernel(wall, *refs),
        (t2, tb2, halo_b, gxb, gxm, gy, gz, coeff, owner, extra, extra_n, totals, surface_transfer_coefficient, ratio, heat),
        [VMEM] * 9 + [SMEM, SMEM] + [VMEM] * 4,
        (f32(2 * rows, LANES), f32(count, LANES)),
        (VMEM, VMEM),
        [pad, pltpu.VMEM((lines, 8, LANES), jnp.float32), pltpu.VMEM((lines, LANES), jnp.float32)],
        input_output_aliases={14: 0},
    )
    rows_all = lax.all_to_all(send, "brick", 0, 0, tiled=True)
    final, mid = call(
        lambda *refs: finish_kernel(wall, *refs),
        (
            heat,
            owner,
            extra,
            extra_n,
            rows_all,
            surface_transfer_coefficient,
            ratio,
            flow_direction_flag.reshape(1, lines),
            entry_coolant_degrees.reshape(1, lines),
        ),
        [VMEM, VMEM, SMEM, SMEM] + [VMEM] * 5,
        (f32(planes, ny, nz), f32(1, lines)),
        (HBM, VMEM),
        [
            pltpu.VMEM((2 * rows, LANES), jnp.float32),
            pltpu.VMEM((8, LANES), jnp.float32),
            pltpu.VMEM((2, lines, LANES), jnp.float32),
            dma((planes, 2)),
        ],
    )
    return final, mid


def solution(mesh):
    return jax.shard_map(
        per_device,
        mesh=mesh,
        in_specs=(
            P(("pour", "brick"), None, None),
            P("brick", None, None),
            P(),
            P(),
            P("brick", None, None),
            P("brick", None),
            P(),
            P(),
            P("pour"),
        ),
        out_specs=(P(("pour", "brick"), None, None), P(("pour", "brick"), None)),
        check_vma=False,
    )
```

```python
import jax
import jax.numpy as jnp
from jax import lax
from jax.experimental import pallas as pl
from jax.experimental.pallas import tpu as pltpu
from jax.sharding import PartitionSpec as P

LANES = 128
PAD = 8
STRIP = 16
WINDOW = 96
READ_GROUP = 4
WRITE_GROUP = 8
VMEM = pl.BlockSpec(memory_space=pltpu.VMEM)
SMEM = pl.BlockSpec(memory_space=pltpu.SMEM)
HBM = pl.BlockSpec(memory_space=pltpu.HBM)
HALVES = (0, 1)


def f32(*shape):
    return jax.ShapeDtypeStruct(shape, jnp.float32)


def i32(*shape):
    return jax.ShapeDtypeStruct(shape, jnp.int32)


def call(kernel, args, in_specs, out_shape, out_specs, scratch=(), cost=2_000_000, **kw):
    return pl.pallas_call(
        kernel,
        out_shape=out_shape,
        in_specs=in_specs,
        out_specs=out_specs,
        scratch_shapes=list(scratch),
        cost_estimate=pl.CostEstimate(flops=cost, bytes_accessed=cost, transcendentals=0),
        compiler_params=pltpu.CompilerParams(vmem_limit_bytes=12 << 20),
        **kw,
    )(*args)


def plane_of(j, planes):
    odd = lax.rem(lax.axis_index("brick"), 2)
    return jnp.where(odd == 1, j, planes - 1 - j)


def lanes_iota(rows):
    return lax.broadcasted_iota(jnp.int32, (rows, LANES), 1)


def pick(tag, table):
    level = [jnp.broadcast_to(v, tag.shape) for v in table]
    bit = 0
    while len(level) > 1:
        on = (tag & (1 << bit)) != 0
        if len(level) % 2:
            level.append(level[-1])
        level = [jnp.where(on, level[k + 1], level[k]) for k in range(0, len(level), 2)]
        bit += 1
    return level[0]


def face_mean(left, right):
    return 2.0 * left * right / (left + right + 1e-30)


def rows_loop(count, body, step=STRIP, unroll=4):
    def turn(s, carry):
        body(pl.multiple_of(s * step, step))
        return carry

    lax.fori_loop(0, count // step, turn, 0, unroll=unroll)


def advance_rows(cur, r, up, down, gx_up, gx_down, gy, ry, gz, coeff, rz):
    n = STRIP
    lane = lanes_iota(n)
    t = [cur[h, pl.ds(r, n), :] for h in HALVES]
    nxt = [pltpu.roll(t[h], LANES - 1, 1) for h in HALVES]
    ahead = [jnp.where(lane == LANES - 1, nxt[1], nxt[0]), nxt[1]]
    prv = [pltpu.roll(t[h], 1, 1) for h in HALVES]
    behind = [prv[0], jnp.where(lane == 0, prv[0], prv[1])]
    new = []
    for h in HALVES:
        c = t[h]
        flux = gx_up(h) * (up(h) - c) + gx_down(h) * (down(h) - c)
        flux = flux + gy[h, pl.ds(ry, n), :] * (cur[h, pl.ds(r + 1, n), :] - c)
        flux = flux + gy[h, pl.ds(ry - 1, n), :] * (cur[h, pl.ds(r - 1, n), :] - c)
        flux = flux + gz[h, pl.ds(rz, n), :] * (ahead[h] - c)
        flux = flux + gz[2 + h, pl.ds(rz, n), :] * (behind[h] - c)
        new.append(c + coeff[h, pl.ds(rz, n), :] * flux)
    return new


def main_planes(cur, last, halo, gxa, gxm, gy, gz, coeff, planes, ny, emit):
    def plane(j, first, final):
        def body(y):
            r = PAD + j * ny + y
            rz = j * ny + y

            def down(h):
                return halo[h, pl.ds(y, STRIP), :] if first else cur[h, pl.ds(r - ny, STRIP), :]

            def gx_down(h):
                return gxa[h, pl.ds(y, STRIP), :] if first else gxm[h, pl.ds(rz - ny, STRIP), :]

            def up(h):
                return last(h, y) if final else cur[h, pl.ds(r + ny, STRIP), :]

            def gx_up(h):
                return gxm[h, pl.ds(rz, STRIP), :]

            new = advance_rows(cur, r, up, down, gx_up, gx_down, gy, PAD + rz, gz, coeff, rz)
            emit(j, y, new, first)

        rows_loop(ny, body, unroll=8)

    plane(0, True, planes == 2)

    def inner(j, carry):
        plane(j, False, False)
        return carry

    lax.fori_loop(1, planes - 2, inner, 0)
    plane(planes - 2, False, True)


def send_kernel(t_ref, tag_ref, a_ref, b_ref, tags, sem):
    planes = t_ref.shape[0]
    copies = []
    for side, out in ((1, b_ref), (0, a_ref)):
        x = plane_of(0 if side == 0 else planes - 1, planes)
        for h in HALVES:
            part = pl.ds(h * LANES, LANES)
            copies.append(
                pltpu.make_async_copy(t_ref.at[x, :, part], out.at[0, h], sem.at[len(copies)])
            )
            copies.append(
                pltpu.make_async_copy(tag_ref.at[x, :, part], tags.at[side, h], sem.at[len(copies)])
            )
    for copy in copies:
        copy.start()
    for copy in copies:
        copy.wait()
    for side, out in ((1, b_ref), (0, a_ref)):
        for h in HALVES:
            out[1, h] = tags[side, h].astype(jnp.float32)


def prepare_kernel(
    t_ref, tag_ref, cond_ref, store_ref, halo, t0, gxa, gxm, gy, gz, coeff, t1, ta, tags, cond, sem
):
    planes, ny = t_ref.shape[0], t_ref.shape[1]
    copies = []
    for j in range(planes):
        x = plane_of(j, planes)
        for h in HALVES:
            part = pl.ds(h * LANES, LANES)
            rows = pl.ds(PAD + j * ny, ny)
            copies.append(pltpu.make_async_copy(tag_ref.at[x, :, part], tags.at[h, pl.ds(j * ny, ny)], sem.at[0, j, h]))
            copies.append(pltpu.make_async_copy(t_ref.at[x, :, part], t0.at[h, rows], sem.at[1, j, h]))
    for copy in copies:
        copy.start()
    zero = jnp.zeros((PAD, LANES), jnp.float32)
    for h in HALVES:
        for ref in (t0, t1, cond):
            ref[h, pl.ds(0, PAD), :] = zero
            ref[h, pl.ds(ref.shape[1] - PAD, PAD), :] = zero
        gy[h, pl.ds(0, PAD), :] = zero
    shape = (STRIP, LANES)
    lane = lanes_iota(STRIP)
    conds = [jnp.full((1, LANES), cond_ref[m], jnp.float32) for m in range(cond_ref.shape[0])]
    scales = [0.16 / jnp.full((1, LANES), store_ref[m], jnp.float32) for m in range(store_ref.shape[0])]
    for copy in copies:
        copy.wait()

    def materials(r):
        for h in HALVES:
            tag = tags[h, pl.ds(r, STRIP), :]
            cond[h, pl.ds(PAD + r, STRIP), :] = pick(tag, conds)
            coeff[h, pl.ds(r, STRIP), :] = pick(tag, scales)

    rows_loop(planes * ny, materials)

    def halo_face(y):
        for h in HALVES:
            other = pick(halo[1, h, pl.ds(y, STRIP), :].astype(jnp.int32), conds)
            gxa[h, pl.ds(y, STRIP), :] = face_mean(cond[h, pl.ds(PAD + y, STRIP), :], other)

    rows_loop(ny, halo_face)

    def x_faces(r):
        for h in HALVES:
            mine = cond[h, pl.ds(PAD + r, STRIP), :]
            gxm[h, pl.ds(r, STRIP), :] = face_mean(mine, cond[h, pl.ds(PAD + r + ny, STRIP), :])

    rows_loop((planes - 1) * ny, x_faces)

    def yz_faces(r):
        y = lax.rem(r, ny) + lax.broadcasted_iota(jnp.int32, shape, 0)
        mine = [cond[h, pl.ds(PAD + r, STRIP), :] for h in HALVES]
        nxt = [pltpu.roll(mine[h], LANES - 1, 1) for h in HALVES]
        ahead = [jnp.where(lane == LANES - 1, nxt[1], nxt[0]), nxt[1]]
        right = [face_mean(mine[h], ahead[h]) for h in HALVES]
        right[1] = jnp.where(lane == LANES - 1, 0.0, right[1])
        back = [pltpu.roll(right[h], 1, 1) for h in HALVES]
        left = [jnp.where(lane == 0, back[1], back[0]), jnp.where(lane == 0, back[0], back[1])]
        for h in HALVES:
            below = face_mean(mine[h], cond[h, pl.ds(PAD + r + 1, STRIP), :])
            gy[h, pl.ds(PAD + r, STRIP), :] = jnp.where(y == ny - 1, 0.0, below)
            gz[h, pl.ds(r, STRIP), :] = right[h]
            gz[2 + h, pl.ds(r, STRIP), :] = left[h]

    rows_loop(planes * ny, yz_faces)

    def emit(j, y, new, first):
        for h in HALVES:
            t1[h, pl.ds(PAD + j * ny + y, STRIP), :] = new[h]
            if first:
                ta[h, pl.ds(y, STRIP), :] = new[h]

    def last(h, y):
        return t0[h, pl.ds(PAD + (planes - 1) * ny + y, STRIP), :]

    main_planes(t0, last, halo.at[0], gxa, gxm, gy, gz, coeff, planes, ny, emit)


def last_plane(cur, below, halo, gxb, gxm, gy, gz, coeff, ny, emit):
    rows = gz.shape[1]
    base = rows - ny

    def body(y):
        new = advance_rows(
            cur,
            PAD + y,
            lambda h: halo[h, pl.ds(y, STRIP), :],
            lambda h: below(h, y),
            lambda h: gxb[h, pl.ds(y, STRIP), :],
            lambda h: gxm[h, pl.ds(base - ny + y, STRIP), :],
            gy,
            PAD + base + y,
            gz,
            coeff,
            base + y,
        )
        emit(y, new)

    rows_loop(ny, body, unroll=8)


def padded(pad, rows_of, ny):
    zero = jnp.zeros((PAD, LANES), jnp.float32)
    for h in HALVES:
        pad[h, pl.ds(0, PAD), :] = zero
        pad[h, pl.ds(PAD + ny, PAD), :] = zero

    def body(y):
        for h in HALVES:
            pad[h, pl.ds(PAD + y, STRIP), :] = rows_of(h, y)

    rows_loop(ny, body)


def first_last_kernel(brick_count, tag_ref, cond_ref, t0, halo, gxm, gy, gz, coeff, gxb, tb, pad, tags, sem):
    ny = tb.shape[1]
    planes = gz.shape[1] // ny
    base = (planes - 1) * ny
    x = plane_of(planes - 1, planes)
    copies = [
        pltpu.make_async_copy(tag_ref.at[x, :, pl.ds(h * LANES, LANES)], tags.at[h], sem.at[h])
        for h in HALVES
    ]
    for copy in copies:
        copy.start()
    me = lax.axis_index("brick")
    edge = (me == 0) | (me == brick_count - 1)
    keep = jnp.where(edge, 0.0, 1.0).astype(jnp.float32)
    conds = [jnp.full((1, LANES), cond_ref[m], jnp.float32) for m in range(cond_ref.shape[0])]
    padded(pad, lambda h, y: t0[h, pl.ds(PAD + base + y, STRIP), :], ny)
    for copy in copies:
        copy.wait()

    def faces(y):
        for h in HALVES:
            other = keep * pick(halo[1, h, pl.ds(y, STRIP), :].astype(jnp.int32), conds)
            mine = pick(tags[h, pl.ds(y, STRIP), :], conds)
            gxb[h, pl.ds(y, STRIP), :] = face_mean(mine, other)

    rows_loop(ny, faces)

    def emit(y, new):
        for h in HALVES:
            tb[h, pl.ds(y, STRIP), :] = new[h]

    def below(h, y):
        return t0[h, pl.ds(PAD + base - ny + y, STRIP), :]

    last_plane(pad, below, halo.at[0], gxb, gxm, gy, gz, coeff, ny, emit)


def next_last_kernel(tm, tb_old, halo, gxb, gxm, gy, gz, coeff, tb, pad):
    ny = tb.shape[1]
    planes = gz.shape[1] // ny
    padded(pad, lambda h, y: tb_old[h, pl.ds(y, STRIP), :], ny)

    def emit(y, new):
        for h in HALVES:
            tb[h, pl.ds(y, STRIP), :] = new[h]

    def below(h, y):
        return tm[h, pl.ds(PAD + (planes - 2) * ny + y, STRIP), :]

    last_plane(pad, below, halo, gxb, gxm, gy, gz, coeff, ny, emit)


def next_main_kernel(tm, tb_old, halo, gxa, gxm, gy, gz, coeff, out, ta):
    ny = ta.shape[1]
    planes = gz.shape[1] // ny
    zero = jnp.zeros((PAD, LANES), jnp.float32)
    for h in HALVES:
        out[h, pl.ds(0, PAD), :] = zero
        out[h, pl.ds(out.shape[1] - PAD, PAD), :] = zero

    def emit(j, y, new, first):
        for h in HALVES:
            out[h, pl.ds(PAD + j * ny + y, STRIP), :] = new[h]
            if first:
                ta[h, pl.ds(y, STRIP), :] = new[h]

    def last(h, y):
        return tb_old[h, pl.ds(y, STRIP), :]

    main_planes(tm, last, halo, gxa, gxm, gy, gz, coeff, planes, ny, emit)


def unpack(packed, ordered, row_of, col_of, sem, half):
    copy = pltpu.make_async_copy(packed, ordered, sem)
    copy.start()
    one = packed[...]
    row_of[...] = lax.shift_right_arithmetic(one, 20) + half
    col_of[...] = lax.shift_right_logical(one, 13) & (LANES - 1)
    return copy


def line_of(packed, wall):
    return lax.shift_right_logical(packed & 8191, wall.bit_length() - 1)


def row_at(ordered, c, place, half):
    return lax.shift_right_arithmetic(ordered[c, place], 20) + half


def windows(first, last, group, ordered, half, work, commit, after=None):
    def base_of(c):
        return pl.multiple_of(row_at(ordered, c, 0, half) & -8, 8)

    def turn(g, carry):
        chunks = [g * group + u for u in range(group)]
        bases = [base_of(c) for c in chunks]
        made = [work(c, base) for c, base in zip(chunks, bases)]
        for c, base, item in zip(chunks, bases, made):
            commit(c, base, item)
        ends = [row_at(ordered, c, LANES - 1, half) - base for c, base in zip(chunks, bases)]
        longest = ends[0]
        for end in ends[1:]:
            longest = jnp.maximum(longest, end)

        @pl.when(longest >= WINDOW)
        def _():
            def chunk(u, inner):
                c = g * group + u
                end = row_at(ordered, c, LANES - 1, half)

                def go(base):
                    base = pl.multiple_of(base, 8)
                    commit(c, base, work(c, base))
                    return base + WINDOW

                lax.while_loop(lambda base: base <= end, go, base_of(c) + WINDOW)
                return inner

            lax.fori_loop(0, group, chunk, 0)

        return carry if after is None else after(g, carry)

    return lax.fori_loop(first, last, turn, 0)


def split(x):
    high = x.astype(jnp.bfloat16)
    return high, (x - high.astype(jnp.float32)).astype(jnp.bfloat16)


def read_walls(first, last, ordered, row_of, col_of, heat, found, half):
    tall = lax.broadcasted_iota(jnp.int32, (WINDOW, LANES), 0)
    square = lax.broadcasted_iota(jnp.int32, (LANES, LANES), 0)

    def work(c, base):
        lanes = jnp.where(square == col_of[pl.ds(c, 1), :], 1.0, 0.0).astype(jnp.bfloat16)
        high, low = split(heat[pl.ds(base, WINDOW), :])
        values = jnp.dot(high, lanes, preferred_element_type=jnp.float32)
        values = values + jnp.dot(low, lanes, preferred_element_type=jnp.float32)
        here = tall == row_of[pl.ds(c, 1), :] - base
        return jnp.sum(jnp.where(here, values, 0.0), axis=0, keepdims=True)

    def commit(c, base, item):
        found[pl.ds(c, 1), :] = found[pl.ds(c, 1), :] + item

    windows(first, last, READ_GROUP, ordered, half, work, commit)


def early_groups(ordered, rows_before, half):
    depth = ordered.shape[0]
    count = jnp.int32(0)
    for g in range(depth // READ_GROUP):
        end = row_at(ordered, (g + 1) * READ_GROUP - 1, LANES - 1, half)
        count = count + jnp.where(end < rows_before, 1, 0)
    return count


def final_main_kernel(tm, tb_old, halo, gxa, gxm, gy, gz, coeff, packed, heat, found, ordered, row_of, col_of, sem):
    ny = tb_old.shape[1]
    rows = gz.shape[1]
    planes = rows // ny
    copy = unpack(packed, ordered, row_of, col_of, sem, rows)

    def emit(j, y, new, first):
        for h in HALVES:
            heat[pl.ds((2 * j + h) * ny + y, STRIP), :] = new[h]

    def last(h, y):
        return tb_old[h, pl.ds(y, STRIP), :]

    main_planes(tm, last, halo, gxa, gxm, gy, gz, coeff, planes, ny, emit)
    heat[pl.ds(2 * rows, WINDOW), :] = jnp.zeros((WINDOW, LANES), jnp.float32)
    heat[pl.ds(2 * (rows - ny), 2 * ny), :] = jnp.zeros((2 * ny, LANES), jnp.float32)
    found[...] = jnp.zeros_like(found)
    copy.wait()
    early = early_groups(ordered, 2 * (rows - ny), rows)
    read_walls(0, early, ordered, row_of, col_of, heat, found, rows)


def walls_kernel(
    wall, tm, tb_old, halo, gxb, gxm, gy, gz, coeff, packed, found_in, film, ratio, heat_in, heat, found, send, pad, sums, ordered, row_of, col_of, sem
):
    ny = tb_old.shape[1]
    rows = gz.shape[1]
    planes = rows // ny
    lines = film.shape[1]
    copy = unpack(packed, ordered, row_of, col_of, sem, rows)
    padded(pad, lambda h, y: tb_old[h, pl.ds(y, STRIP), :], ny)

    def emit(y, new):
        for h in HALVES:
            heat[pl.ds((2 * (planes - 1) + h) * ny + y, STRIP), :] = new[h]

    def below(h, y):
        return tm[h, pl.ds(PAD + (planes - 2) * ny + y, STRIP), :]

    last_plane(pad, below, halo, gxb, gxm, gy, gz, coeff, ny, emit)
    found[...] = found_in[...]
    copy.wait()
    early = early_groups(ordered, 2 * (rows - ny), rows)
    read_walls(early, ordered.shape[0] // READ_GROUP, ordered, row_of, col_of, heat, found, rows)
    owner = line_of(packed[...], wall)
    hot = found[...]
    for k in range(lines):
        part = jnp.where(owner == k, hot, 0.0)
        sums[k : k + 1, :] = jnp.sum(part, axis=0, keepdims=True)
    mean = lax.dot_general(
        jnp.ones((8, LANES), jnp.float32),
        sums[...],
        (((1,), (1,)), ((), ())),
        precision=lax.Precision.HIGHEST,
        preferred_element_type=jnp.float32,
    )[0:1] * (1.0 / wall)
    keep = jnp.exp(-ratio[...] * film[...])
    gain = (1.0 - keep) * mean
    count = send.shape[0]
    send[...] = jnp.zeros_like(send)
    send[:, 0:lines] = jnp.broadcast_to(keep, (count, lines))
    send[:, lines : 2 * lines] = jnp.broadcast_to(gain, (count, lines))


def finish_kernel(
    wall, packed, found, rows_all, direction, entry, heat_in, out, mid, heat, table, change, ordered, row_of, col_of, sem, sems
):
    planes, ny = out.shape[0], out.shape[1]
    rows = planes * ny
    count, lines = rows_all.shape[0], mid.shape[1]
    me = lax.axis_index("brick")
    copy = unpack(packed, ordered, row_of, col_of, sem, rows)

    def pass_on(k, water):
        row = rows_all[pl.ds(k, 1), :]
        return row[:, 0:lines] * water + row[:, lines : 2 * lines]

    start = entry[...]
    ahead = lax.fori_loop(0, me, pass_on, start)
    behind = lax.fori_loop(0, count - 1 - me, lambda k, w: pass_on(count - 1 - k, w), start)
    inflow = jnp.where(direction[...] == 0, ahead, behind)
    own = rows_all[pl.ds(me, 1), :]
    keep, gain = own[:, 0:lines], own[:, lines : 2 * lines]
    coolant = 0.5 * (inflow + keep * inflow + gain)
    mid[...] = coolant
    table[...] = jnp.zeros_like(table)
    table[0:1, 0:lines] = 0.5 * (1.0 - keep)
    table[1:2, 0:lines] = coolant
    pull = jnp.broadcast_to(table[0:1, :], (8, LANES))
    cool = jnp.broadcast_to(table[1:2, :], (8, LANES))
    depth = change.shape[0]
    for k in range(0, depth, 8):
        owner = line_of(packed[k : k + 8, :], wall)
        a = jnp.take_along_axis(pull, owner, axis=1)
        c = jnp.take_along_axis(cool, owner, axis=1)
        change[k : k + 8, :] = a * (c - found[k : k + 8, :])
    tall = lax.broadcasted_iota(jnp.int32, (WINDOW, LANES), 0)
    square = lax.broadcasted_iota(jnp.int32, (LANES, LANES), 0)

    def work(c, base):
        at = jnp.where(tall == row_of[pl.ds(c, 1), :] - base, 1.0, 0.0).astype(jnp.bfloat16)
        amount = jnp.where(square == col_of[pl.ds(c, 1), :], change[pl.ds(c, 1), :], 0.0)
        high, low = split(amount)
        dims = (((1,), (1,)), ((), ()))
        return lax.dot_general(at, high, dims, preferred_element_type=jnp.float32) + lax.dot_general(
            at, low, dims, preferred_element_type=jnp.float32
        )

    def commit(c, base, item):
        heat[pl.ds(base, WINDOW), :] = heat[pl.ds(base, WINDOW), :] + item

    def copies(j):
        x = plane_of(j, planes)
        return [
            pltpu.make_async_copy(
                heat.at[pl.ds((2 * j + h) * ny, ny), :],
                out.at[x, :, pl.ds(h * LANES, LANES)],
                sems.at[j, h],
            )
            for h in HALVES
        ]

    groups = depth // WRITE_GROUP

    def after(g, sent):
        following = row_at(ordered, jnp.minimum((g + 1) * WRITE_GROUP, depth - 1), 0, rows) & -8
        ready = jnp.where(g == groups - 1, 2 * rows, following)

        def send(j):
            for item in copies(j):
                item.start()
            return j + 1

        return lax.while_loop(lambda j: (j + 1) * 2 * ny <= ready, send, sent)

    copy.wait()
    windows(0, groups, WRITE_GROUP, ordered, rows, work, commit, after)
    for j in range(planes):
        for item in copies(j):
            item.wait()


def per_device(
    initial_voxel_degrees,
    alloy_tag_per_voxel,
    thermal_conductance_per_alloy,
    specific_storage_per_alloy,
    bore_boundary_positions,
    surface_transfer_coefficient,
    surface_over_flow_ratio,
    flow_direction_flag,
    entry_coolant_degrees,
):
    planes, ny, nz = initial_voxel_degrees.shape
    _, lines, wall = bore_boundary_positions.shape
    rows, hits = planes * ny, lines * wall
    count = lax.axis_size("brick")
    dma = pltpu.SemaphoreType.DMA
    on_chip = [(i, i ^ 1) for i in range(count)]
    across = [(i, (i + 1) % count) for i in range(1, count, 2)]
    across = across + [(b, a) for a, b in across]

    def swap(value, pairs):
        return lax.ppermute(value, "brick", pairs)

    initial_voxel_degrees = pltpu.with_memory_space_constraint(initial_voxel_degrees, pltpu.HBM)
    alloy_tag_per_voxel = pltpu.with_memory_space_constraint(alloy_tag_per_voxel, pltpu.HBM)

    plane = f32(2, ny, LANES)
    pair = f32(2, 2, ny, LANES)
    ta, tb = call(
        send_kernel,
        (initial_voxel_degrees, alloy_tag_per_voxel),
        [HBM, HBM],
        (pair, pair),
        (VMEM, VMEM),
        [pltpu.VMEM((2, 2, ny, LANES), jnp.int32), dma((8,))],
    )
    halo_b = swap(tb, across)
    halo_a = swap(ta, on_chip)

    cell = bore_boundary_positions.reshape(hits)
    cell = cell ^ jnp.where(lax.rem(lax.axis_index("brick"), 2) == 1, 0, (planes - 1) * ny * nz)
    row = (cell // (ny * nz) * 2 + (cell // LANES) % 2) * ny + (cell // nz) % ny
    cell = (row * LANES + cell % LANES) ^ (rows * LANES)
    packed = lax.sort(cell * 8192 + lax.iota(jnp.int32, hits), is_stable=False)
    halo_a, packed = lax.optimization_barrier((halo_a, packed))
    packed = packed.reshape(hits // LANES, LANES)

    full = f32(2, rows + 2 * PAD, LANES)
    most = f32(2, rows - ny + 2 * PAD, LANES)
    t0, gxa, gxm, gy, gz, coeff, t1, ta = call(
        prepare_kernel,
        (
            initial_voxel_degrees,
            alloy_tag_per_voxel,
            thermal_conductance_per_alloy,
            specific_storage_per_alloy,
            halo_a,
        ),
        [HBM, HBM, SMEM, SMEM, VMEM],
        (full, plane, f32(2, rows - ny, LANES), full, f32(4, rows, LANES), f32(2, rows, LANES), most, plane),
        (VMEM,) * 8,
        [
            pltpu.VMEM((2, rows, LANES), jnp.int32),
            pltpu.VMEM((2, rows + 2 * PAD, LANES), jnp.float32),
            dma((2, planes, 2)),
        ],
        cost=10_000_000,
    )
    pad = pltpu.VMEM((2, ny + 2 * PAD, LANES), jnp.float32)
    gxb, tb = call(
        lambda *refs: first_last_kernel(count, *refs),
        (alloy_tag_per_voxel, thermal_conductance_per_alloy, t0, halo_b, gxm, gy, gz, coeff),
        [HBM, SMEM] + [VMEM] * 6,
        (plane, plane),
        (VMEM, VMEM),
        [pad, pltpu.VMEM((2, ny, LANES), jnp.int32), dma((2,))],
    )
    halo_b = swap(tb, across)
    halo_a = swap(ta, on_chip)

    t2, ta = call(
        next_main_kernel,
        (t1, tb, halo_a, gxa, gxm, gy, gz, coeff),
        [VMEM] * 8,
        (most, plane),
        (VMEM, VMEM),
        cost=4_000_000,
    )
    tb2 = call(
        next_last_kernel,
        (t1, tb, halo_b, gxb, gxm, gy, gz, coeff),
        [VMEM] * 8,
        plane,
        VMEM,
        [pad],
    )
    halo_b = swap(tb2, across)
    halo_a = swap(ta, on_chip)

    depth = hits // LANES
    listing = [
        pltpu.SMEM((depth, LANES), jnp.int32),
        pltpu.VMEM((depth, LANES), jnp.int32),
        pltpu.VMEM((depth, LANES), jnp.int32),
        dma,
    ]
    heat, found = call(
        lambda *refs: final_main_kernel(*refs),
        (t2, tb2, halo_a, gxa, gxm, gy, gz, coeff, packed),
        [VMEM] * 9,
        (f32(2 * rows + WINDOW, LANES), f32(depth, LANES)),
        (VMEM, VMEM),
        listing,
        cost=10_000_000,
    )
    ratio = surface_over_flow_ratio.reshape(1, lines)
    heat, found, send = call(
        lambda *refs: walls_kernel(wall, *refs),
        (t2, tb2, halo_b, gxb, gxm, gy, gz, coeff, packed, found, surface_transfer_coefficient, ratio, heat),
        [VMEM] * 13,
        (f32(2 * rows + WINDOW, LANES), f32(depth, LANES), f32(count, LANES)),
        (VMEM, VMEM, VMEM),
        [pad, pltpu.VMEM((lines, LANES), jnp.float32)] + listing,
        input_output_aliases={12: 0},
    )
    rows_all = lax.all_to_all(send, "brick", 0, 0, tiled=True)
    final, mid, _ = call(
        lambda *refs: finish_kernel(wall, *refs),
        (
            packed,
            found,
            rows_all,
            flow_direction_flag.reshape(1, lines),
            entry_coolant_degrees.reshape(1, lines),
            heat,
        ),
        [VMEM] * 6,
        (f32(planes, ny, nz), f32(1, lines), f32(2 * rows + WINDOW, LANES)),
        (HBM, VMEM, VMEM),
        [pltpu.VMEM((8, LANES), jnp.float32), pltpu.VMEM((depth, LANES), jnp.float32)]
        + listing
        + [dma((planes, 2))],
        input_output_aliases={5: 2},
    )
    return final, mid


def solution(mesh):
    return jax.shard_map(
        per_device,
        mesh=mesh,
        in_specs=(
            P(("pour", "brick"), None, None),
            P("brick", None, None),
            P(),
            P(),
            P("brick", None, None),
            P("brick", None),
            P(),
            P(),
            P("pour"),
        ),
        out_specs=(P(("pour", "brick"), None, None), P(("pour", "brick"), None)),
        check_vma=False,
    )
```

```python
import jax
import jax.numpy as jnp
from jax import lax
from jax.experimental import pallas as pl
from jax.experimental.pallas import tpu as pltpu
from jax.sharding import PartitionSpec as P

LANES = 128
PAD = 8
STRIP = 16
WINDOW = 96
READ_GROUP = 4
WRITE_GROUP = 8
VMEM = pl.BlockSpec(memory_space=pltpu.VMEM)
SMEM = pl.BlockSpec(memory_space=pltpu.SMEM)
HBM = pl.BlockSpec(memory_space=pltpu.HBM)
HALVES = (0, 1)


def f32(*shape):
    return jax.ShapeDtypeStruct(shape, jnp.float32)


def i32(*shape):
    return jax.ShapeDtypeStruct(shape, jnp.int32)


def call(kernel, args, in_specs, out_shape, out_specs, scratch=(), cost=2_000_000, **kw):
    return pl.pallas_call(
        kernel,
        out_shape=out_shape,
        in_specs=in_specs,
        out_specs=out_specs,
        scratch_shapes=list(scratch),
        cost_estimate=pl.CostEstimate(flops=cost, bytes_accessed=cost, transcendentals=0),
        compiler_params=pltpu.CompilerParams(vmem_limit_bytes=12 << 20),
        **kw,
    )(*args)


def plane_of(j, planes):
    odd = lax.rem(lax.axis_index("brick"), 2)
    return jnp.where(odd == 1, j, planes - 1 - j)


def lanes_iota(rows):
    return lax.broadcasted_iota(jnp.int32, (rows, LANES), 1)


def pick(tag, table):
    level = [jnp.broadcast_to(v, tag.shape) for v in table]
    bit = 0
    while len(level) > 1:
        on = (tag & (1 << bit)) != 0
        if len(level) % 2:
            level.append(level[-1])
        level = [jnp.where(on, level[k + 1], level[k]) for k in range(0, len(level), 2)]
        bit += 1
    return level[0]


def face_mean(left, right):
    return 2.0 * left * right / (left + right + 1e-30)


def rows_loop(count, body, step=STRIP, unroll=4):
    def turn(s, carry):
        body(pl.multiple_of(s * step, step))
        return carry

    lax.fori_loop(0, count // step, turn, 0, unroll=unroll)


def advance_rows(cur, r, up, down, gx_up, gx_down, gy, ry, gz, coeff, rz):
    n = STRIP
    lane = lanes_iota(n)
    t = [cur[h, pl.ds(r, n), :] for h in HALVES]
    nxt = [pltpu.roll(t[h], LANES - 1, 1) for h in HALVES]
    ahead = [jnp.where(lane == LANES - 1, nxt[1], nxt[0]), nxt[1]]
    prv = [pltpu.roll(t[h], 1, 1) for h in HALVES]
    behind = [prv[0], jnp.where(lane == 0, prv[0], prv[1])]
    new = []
    for h in HALVES:
        c = t[h]
        flux = gx_up(h) * (up(h) - c) + gx_down(h) * (down(h) - c)
        flux = flux + gy[h, pl.ds(ry, n), :] * (cur[h, pl.ds(r + 1, n), :] - c)
        flux = flux + gy[h, pl.ds(ry - 1, n), :] * (cur[h, pl.ds(r - 1, n), :] - c)
        flux = flux + gz[h, pl.ds(rz, n), :] * (ahead[h] - c)
        flux = flux + gz[2 + h, pl.ds(rz, n), :] * (behind[h] - c)
        new.append(c + coeff[h, pl.ds(rz, n), :] * flux)
    return new


def main_planes(cur, last, halo, gxa, gxm, gy, gz, coeff, planes, ny, emit):
    def plane(j, first, final):
        def body(y):
            r = PAD + j * ny + y
            rz = j * ny + y

            def down(h):
                return halo[h, pl.ds(y, STRIP), :] if first else cur[h, pl.ds(r - ny, STRIP), :]

            def gx_down(h):
                return gxa[h, pl.ds(y, STRIP), :] if first else gxm[h, pl.ds(rz - ny, STRIP), :]

            def up(h):
                return last(h, y) if final else cur[h, pl.ds(r + ny, STRIP), :]

            def gx_up(h):
                return gxm[h, pl.ds(rz, STRIP), :]

            new = advance_rows(cur, r, up, down, gx_up, gx_down, gy, PAD + rz, gz, coeff, rz)
            emit(j, y, new, first)

        rows_loop(ny, body, unroll=8)

    plane(0, True, planes == 2)

    def inner(j, carry):
        plane(j, False, False)
        return carry

    lax.fori_loop(1, planes - 2, inner, 0)
    plane(planes - 2, False, True)


def send_kernel(t_ref, tag_ref, a_ref, b_ref, tags, sem):
    planes = t_ref.shape[0]
    copies = []
    for side, out in ((1, b_ref), (0, a_ref)):
        x = plane_of(0 if side == 0 else planes - 1, planes)
        for h in HALVES:
            part = pl.ds(h * LANES, LANES)
            copies.append(
                pltpu.make_async_copy(t_ref.at[x, :, part], out.at[0, h], sem.at[len(copies)])
            )
            copies.append(
                pltpu.make_async_copy(tag_ref.at[x, :, part], tags.at[side, h], sem.at[len(copies)])
            )
    for copy in copies:
        copy.start()
    for copy in copies:
        copy.wait()
    for side, out in ((1, b_ref), (0, a_ref)):
        for h in HALVES:
            out[1, h] = tags[side, h].astype(jnp.float32)


def prepare_kernel(t_ref, tag_ref, cond_ref, store_ref, halo, t0, tb, cond_b, gxa, gxm, gy, gz, coeff, cond):
    planes, ny = t_ref.shape[0], t_ref.shape[1]
    zero = jnp.zeros((PAD, LANES), jnp.float32)
    for h in HALVES:
        for ref in (t0, cond):
            ref[h, pl.ds(0, PAD), :] = zero
            ref[h, pl.ds(ref.shape[1] - PAD, PAD), :] = zero
        gy[h, pl.ds(0, PAD), :] = zero
    shape = (STRIP, LANES)
    lane = lanes_iota(STRIP)
    conds = [jnp.full((1, LANES), cond_ref[m], jnp.float32) for m in range(cond_ref.shape[0])]
    scales = [0.16 / jnp.full((1, LANES), store_ref[m], jnp.float32) for m in range(store_ref.shape[0])]

    def materials(j, final):
        x = plane_of(j, planes)

        def body(y):
            for h in HALVES:
                part = slice(h * LANES, (h + 1) * LANES)
                tag = tag_ref[x, pl.ds(y, STRIP), part]
                kind = pick(tag, conds)
                cond[h, pl.ds(PAD + j * ny + y, STRIP), :] = kind
                coeff[h, pl.ds(j * ny + y, STRIP), :] = pick(tag, scales)
                if final:
                    cond_b[h, pl.ds(y, STRIP), :] = kind
                    tb[h, pl.ds(y, STRIP), :] = t_ref[x, pl.ds(y, STRIP), part]
                else:
                    t0[h, pl.ds(PAD + j * ny + y, STRIP), :] = t_ref[x, pl.ds(y, STRIP), part]

        rows_loop(ny, body)

    def main(j, carry):
        materials(j, False)
        return carry

    lax.fori_loop(0, planes - 1, main, 0)
    materials(planes - 1, True)

    def halo_face(y):
        for h in HALVES:
            other = pick(halo[1, h, pl.ds(y, STRIP), :].astype(jnp.int32), conds)
            gxa[h, pl.ds(y, STRIP), :] = face_mean(cond[h, pl.ds(PAD + y, STRIP), :], other)

    rows_loop(ny, halo_face)

    def x_faces(r):
        for h in HALVES:
            mine = cond[h, pl.ds(PAD + r, STRIP), :]
            gxm[h, pl.ds(r, STRIP), :] = face_mean(mine, cond[h, pl.ds(PAD + r + ny, STRIP), :])

    rows_loop((planes - 1) * ny, x_faces)

    def yz_faces(r):
        y = lax.rem(r, ny) + lax.broadcasted_iota(jnp.int32, shape, 0)
        mine = [cond[h, pl.ds(PAD + r, STRIP), :] for h in HALVES]
        nxt = [pltpu.roll(mine[h], LANES - 1, 1) for h in HALVES]
        ahead = [jnp.where(lane == LANES - 1, nxt[1], nxt[0]), nxt[1]]
        prv = [pltpu.roll(mine[h], 1, 1) for h in HALVES]
        behind = [prv[0], jnp.where(lane == 0, prv[0], prv[1])]
        for h in HALVES:
            below = face_mean(mine[h], cond[h, pl.ds(PAD + r + 1, STRIP), :])
            gy[h, pl.ds(PAD + r, STRIP), :] = jnp.where(y == ny - 1, 0.0, below)
            right = face_mean(mine[h], ahead[h])
            gz[h, pl.ds(r, STRIP), :] = jnp.where(lane == LANES - 1, 0.0, right) if h else right
            left = face_mean(behind[h], mine[h])
            gz[2 + h, pl.ds(r, STRIP), :] = left if h else jnp.where(lane == 0, 0.0, left)

    rows_loop(planes * ny, yz_faces, unroll=8)


def last_plane(cur, below, halo, gxb, gxm, gy, gz, coeff, ny, emit):
    rows = gz.shape[1]
    base = rows - ny

    def body(y):
        new = advance_rows(
            cur,
            PAD + y,
            lambda h: halo[h, pl.ds(y, STRIP), :],
            lambda h: below(h, y),
            lambda h: gxb[h, pl.ds(y, STRIP), :],
            lambda h: gxm[h, pl.ds(base - ny + y, STRIP), :],
            gy,
            PAD + base + y,
            gz,
            coeff,
            base + y,
        )
        emit(y, new)

    rows_loop(ny, body, unroll=8)


def padded(pad, rows_of, ny):
    zero = jnp.zeros((PAD, LANES), jnp.float32)
    for h in HALVES:
        pad[h, pl.ds(0, PAD), :] = zero
        pad[h, pl.ds(PAD + ny, PAD), :] = zero

    def body(y):
        for h in HALVES:
            pad[h, pl.ds(PAD + y, STRIP), :] = rows_of(h, y)

    rows_loop(ny, body)


def first_last_kernel(brick_count, cond_ref, tm, tb_old, cond_b, halo, gxm, gy, gz, coeff, gxb, tb, pad):
    ny = tb.shape[1]
    me = lax.axis_index("brick")
    edge = (me == 0) | (me == brick_count - 1)
    keep = jnp.where(edge, 0.0, 1.0).astype(jnp.float32)
    conds = [keep * jnp.full((1, LANES), cond_ref[m], jnp.float32) for m in range(cond_ref.shape[0])]

    def faces(y):
        for h in HALVES:
            other = pick(halo[1, h, pl.ds(y, STRIP), :].astype(jnp.int32), conds)
            gxb[h, pl.ds(y, STRIP), :] = face_mean(cond_b[h, pl.ds(y, STRIP), :], other)

    rows_loop(ny, faces)
    next_last_kernel(tm, tb_old, halo.at[0], gxb, gxm, gy, gz, coeff, tb, pad)


def next_last_kernel(tm, tb_old, halo, gxb, gxm, gy, gz, coeff, tb, pad):
    ny = tb.shape[1]
    planes = gz.shape[1] // ny
    padded(pad, lambda h, y: tb_old[h, pl.ds(y, STRIP), :], ny)

    def emit(y, new):
        for h in HALVES:
            tb[h, pl.ds(y, STRIP), :] = new[h]

    def below(h, y):
        return tm[h, pl.ds(PAD + (planes - 2) * ny + y, STRIP), :]

    last_plane(pad, below, halo, gxb, gxm, gy, gz, coeff, ny, emit)


def next_main_kernel(tm, tb_old, halo, gxa, gxm, gy, gz, coeff, out, ta):
    ny = ta.shape[1]
    planes = gz.shape[1] // ny
    zero = jnp.zeros((PAD, LANES), jnp.float32)
    for h in HALVES:
        out[h, pl.ds(0, PAD), :] = zero
        out[h, pl.ds(out.shape[1] - PAD, PAD), :] = zero

    def emit(j, y, new, first):
        for h in HALVES:
            out[h, pl.ds(PAD + j * ny + y, STRIP), :] = new[h]
            if first:
                ta[h, pl.ds(y, STRIP), :] = new[h]

    def last(h, y):
        return tb_old[h, pl.ds(y, STRIP), :]

    main_planes(tm, last, halo, gxa, gxm, gy, gz, coeff, planes, ny, emit)


def unpack(packed, ordered, row_of, col_of, sem, half):
    copy = pltpu.make_async_copy(packed, ordered, sem)
    copy.start()
    one = packed[...]
    row_of[...] = lax.shift_right_arithmetic(one, 20) + half
    col_of[...] = lax.shift_right_logical(one, 13) & (LANES - 1)
    return copy


def line_of(packed, wall):
    return lax.shift_right_logical(packed & 8191, wall.bit_length() - 1)


def row_at(ordered, c, place, half):
    return lax.shift_right_arithmetic(ordered[c, place], 20) + half


def windows(first, last, group, ordered, half, work, commit, after=None):
    def base_of(c):
        return pl.multiple_of(row_at(ordered, c, 0, half) & -8, 8)

    def turn(g, carry):
        chunks = [g * group + u for u in range(group)]
        bases = [base_of(c) for c in chunks]
        made = [work(c, base) for c, base in zip(chunks, bases)]
        for c, base, item in zip(chunks, bases, made):
            commit(c, base, item)
        ends = [row_at(ordered, c, LANES - 1, half) - base for c, base in zip(chunks, bases)]
        longest = ends[0]
        for end in ends[1:]:
            longest = jnp.maximum(longest, end)

        @pl.when(longest >= WINDOW)
        def _():
            def chunk(u, inner):
                c = g * group + u
                end = row_at(ordered, c, LANES - 1, half)

                def go(base):
                    base = pl.multiple_of(base, 8)
                    commit(c, base, work(c, base))
                    return base + WINDOW

                lax.while_loop(lambda base: base <= end, go, base_of(c) + WINDOW)
                return inner

            lax.fori_loop(0, group, chunk, 0)

        return carry if after is None else after(g, carry)

    return lax.fori_loop(first, last, turn, 0)


def split(x):
    high = x.astype(jnp.bfloat16)
    return high, (x - high.astype(jnp.float32)).astype(jnp.bfloat16)


def read_walls(first, last, ordered, row_of, col_of, heat, found, half):
    tall = lax.broadcasted_iota(jnp.int32, (WINDOW, LANES), 0)
    square = lax.broadcasted_iota(jnp.int32, (LANES, LANES), 0)

    def work(c, base):
        lanes = jnp.where(square == col_of[pl.ds(c, 1), :], 1.0, 0.0).astype(jnp.bfloat16)
        high, low = split(heat[pl.ds(base, WINDOW), :])
        values = jnp.dot(high, lanes, preferred_element_type=jnp.float32)
        values = values + jnp.dot(low, lanes, preferred_element_type=jnp.float32)
        here = tall == row_of[pl.ds(c, 1), :] - base
        return jnp.sum(jnp.where(here, values, 0.0), axis=0, keepdims=True)

    def commit(c, base, item):
        found[pl.ds(c, 1), :] = found[pl.ds(c, 1), :] + item

    windows(first, last, READ_GROUP, ordered, half, work, commit)


def early_groups(ordered, rows_before, half):
    depth = ordered.shape[0]
    count = jnp.int32(0)
    for g in range(depth // READ_GROUP):
        end = row_at(ordered, (g + 1) * READ_GROUP - 1, LANES - 1, half)
        count = count + jnp.where(end < rows_before, 1, 0)
    return count


def final_main_kernel(tm, tb_old, halo, gxa, gxm, gy, gz, coeff, packed, heat, found, ordered, row_of, col_of, sem):
    ny = tb_old.shape[1]
    rows = gz.shape[1]
    planes = rows // ny
    copy = unpack(packed, ordered, row_of, col_of, sem, rows)

    def emit(j, y, new, first):
        for h in HALVES:
            heat[pl.ds((2 * j + h) * ny + y, STRIP), :] = new[h]

    def last(h, y):
        return tb_old[h, pl.ds(y, STRIP), :]

    main_planes(tm, last, halo, gxa, gxm, gy, gz, coeff, planes, ny, emit)
    heat[pl.ds(2 * rows, WINDOW), :] = jnp.zeros((WINDOW, LANES), jnp.float32)
    heat[pl.ds(2 * (rows - ny), 2 * ny), :] = jnp.zeros((2 * ny, LANES), jnp.float32)
    found[...] = jnp.zeros_like(found)
    copy.wait()
    early = early_groups(ordered, 2 * (rows - ny), rows)
    read_walls(0, early, ordered, row_of, col_of, heat, found, rows)


def walls_kernel(
    wall, tm, tb_old, halo, gxb, gxm, gy, gz, coeff, packed, found_in, film, ratio, heat_in, heat, found, send, pad, sums, ordered, row_of, col_of, sem
):
    ny = tb_old.shape[1]
    rows = gz.shape[1]
    planes = rows // ny
    lines = film.shape[1]
    copy = unpack(packed, ordered, row_of, col_of, sem, rows)
    padded(pad, lambda h, y: tb_old[h, pl.ds(y, STRIP), :], ny)

    def emit(y, new):
        for h in HALVES:
            heat[pl.ds((2 * (planes - 1) + h) * ny + y, STRIP), :] = new[h]

    def below(h, y):
        return tm[h, pl.ds(PAD + (planes - 2) * ny + y, STRIP), :]

    last_plane(pad, below, halo, gxb, gxm, gy, gz, coeff, ny, emit)
    found[...] = found_in[...]
    copy.wait()
    early = early_groups(ordered, 2 * (rows - ny), rows)
    read_walls(early, ordered.shape[0] // READ_GROUP, ordered, row_of, col_of, heat, found, rows)
    owner = line_of(packed[...], wall)
    hot = found[...]
    for k in range(lines):
        part = jnp.where(owner == k, hot, 0.0)
        sums[k : k + 1, :] = jnp.sum(part, axis=0, keepdims=True)
    mean = lax.dot_general(
        jnp.ones((8, LANES), jnp.float32),
        sums[...],
        (((1,), (1,)), ((), ())),
        precision=lax.Precision.HIGHEST,
        preferred_element_type=jnp.float32,
    )[0:1] * (1.0 / wall)
    keep = jnp.exp(-ratio[...] * film[...])
    gain = (1.0 - keep) * mean
    count = send.shape[0]
    send[...] = jnp.zeros_like(send)
    send[:, 0:lines] = jnp.broadcast_to(keep, (count, lines))
    send[:, lines : 2 * lines] = jnp.broadcast_to(gain, (count, lines))


def finish_kernel(
    wall, packed, found, rows_all, direction, entry, heat_in, out, mid, heat, gains, table, change, ordered, row_of, col_of, sem, sems
):
    planes, ny = out.shape[0], out.shape[1]
    rows = planes * ny
    count, lines = rows_all.shape[0], mid.shape[1]
    me = lax.axis_index("brick")
    copy = unpack(packed, ordered, row_of, col_of, sem, rows)

    def pass_on(k, water):
        return rows_all[pl.ds(k, 1), :] * water + gains[pl.ds(k, 1), :]

    gains[...] = pltpu.roll(rows_all[...], LANES - lines, 1)
    table[...] = jnp.zeros_like(table)
    table[0:1, 0:lines] = entry[...]
    start = table[0:1, :]
    ahead = lax.fori_loop(0, me, pass_on, start)
    behind = lax.fori_loop(0, count - 1 - me, lambda k, w: pass_on(count - 1 - k, w), start)
    inflow = jnp.where(direction[...] == 0, ahead[:, 0:lines], behind[:, 0:lines])
    keep = rows_all[pl.ds(me, 1), :][:, 0:lines]
    coolant = 0.5 * (inflow + keep * inflow + gains[pl.ds(me, 1), :][:, 0:lines])
    mid[...] = coolant
    table[0:1, 0:lines] = 0.5 * (1.0 - keep)
    table[1:2, 0:lines] = coolant
    pull = jnp.broadcast_to(table[0:1, :], (8, LANES))
    cool = jnp.broadcast_to(table[1:2, :], (8, LANES))
    depth = change.shape[0]
    for k in range(0, depth, 8):
        owner = line_of(packed[k : k + 8, :], wall)
        a = jnp.take_along_axis(pull, owner, axis=1)
        c = jnp.take_along_axis(cool, owner, axis=1)
        change[k : k + 8, :] = a * (c - found[k : k + 8, :])
    tall = lax.broadcasted_iota(jnp.int32, (WINDOW, LANES), 0)
    square = lax.broadcasted_iota(jnp.int32, (LANES, LANES), 0)

    def work(c, base):
        at = jnp.where(tall == row_of[pl.ds(c, 1), :] - base, 1.0, 0.0).astype(jnp.bfloat16)
        amount = jnp.where(square == col_of[pl.ds(c, 1), :], change[pl.ds(c, 1), :], 0.0)
        high, low = split(amount)
        dims = (((1,), (1,)), ((), ()))
        return lax.dot_general(at, high, dims, preferred_element_type=jnp.float32) + lax.dot_general(
            at, low, dims, preferred_element_type=jnp.float32
        )

    def commit(c, base, item):
        heat[pl.ds(base, WINDOW), :] = heat[pl.ds(base, WINDOW), :] + item

    def copies(j):
        x = plane_of(j, planes)
        return [
            pltpu.make_async_copy(
                heat.at[pl.ds((2 * j + h) * ny, ny), :],
                out.at[x, :, pl.ds(h * LANES, LANES)],
                sems.at[j, h],
            )
            for h in HALVES
        ]

    groups = depth // WRITE_GROUP

    def after(g, sent):
        following = row_at(ordered, jnp.minimum((g + 1) * WRITE_GROUP, depth - 1), 0, rows) & -8
        ready = jnp.where(g == groups - 1, 2 * rows, following)

        def send(j):
            for item in copies(j):
                item.start()
            return j + 1

        return lax.while_loop(lambda j: (j + 1) * 2 * ny <= ready, send, sent)

    copy.wait()
    windows(0, groups, WRITE_GROUP, ordered, rows, work, commit, after)
    for j in range(planes):
        for item in copies(j):
            item.wait()


def per_device(
    initial_voxel_degrees,
    alloy_tag_per_voxel,
    thermal_conductance_per_alloy,
    specific_storage_per_alloy,
    bore_boundary_positions,
    surface_transfer_coefficient,
    surface_over_flow_ratio,
    flow_direction_flag,
    entry_coolant_degrees,
):
    planes, ny, nz = initial_voxel_degrees.shape
    _, lines, wall = bore_boundary_positions.shape
    rows, hits = planes * ny, lines * wall
    count = lax.axis_size("brick")
    dma = pltpu.SemaphoreType.DMA
    on_chip = [(i, i ^ 1) for i in range(count)]
    across = [(i, (i + 1) % count) for i in range(1, count, 2)]
    across = across + [(b, a) for a, b in across]

    def swap(value, pairs):
        return lax.ppermute(value, "brick", pairs)

    temperatures, tags = initial_voxel_degrees, alloy_tag_per_voxel
    initial_voxel_degrees = pltpu.with_memory_space_constraint(initial_voxel_degrees, pltpu.HBM)
    alloy_tag_per_voxel = pltpu.with_memory_space_constraint(alloy_tag_per_voxel, pltpu.HBM)

    plane = f32(2, ny, LANES)
    pair = f32(2, 2, ny, LANES)
    ta, tb = call(
        send_kernel,
        (initial_voxel_degrees, alloy_tag_per_voxel),
        [HBM, HBM],
        (pair, pair),
        (VMEM, VMEM),
        [pltpu.VMEM((2, 2, ny, LANES), jnp.int32), dma((8,))],
    )
    halo_b = swap(tb, across)
    halo_a = swap(ta, on_chip)

    cell = bore_boundary_positions.reshape(hits)
    cell = cell ^ jnp.where(lax.rem(lax.axis_index("brick"), 2) == 1, 0, (planes - 1) * ny * nz)
    row = (cell // (ny * nz) * 2 + (cell // LANES) % 2) * ny + (cell // nz) % ny
    cell = (row * LANES + cell % LANES) ^ (rows * LANES)
    packed = lax.sort(cell * 8192 + lax.iota(jnp.int32, hits), is_stable=False)
    halo_a, packed = lax.optimization_barrier((halo_a, packed))
    packed = packed.reshape(hits // LANES, LANES)

    full = f32(2, rows + 2 * PAD, LANES)
    most = f32(2, rows - ny + 2 * PAD, LANES)
    t0, tb0, cond_b, gxa, gxm, gy, gz, coeff = call(
        prepare_kernel,
        (temperatures, tags, thermal_conductance_per_alloy, specific_storage_per_alloy, halo_a),
        [VMEM, VMEM, SMEM, SMEM, VMEM],
        (most, plane, plane, plane, f32(2, rows - ny, LANES), full, f32(4, rows, LANES), f32(2, rows, LANES)),
        (VMEM,) * 8,
        [pltpu.VMEM((2, rows + 2 * PAD, LANES), jnp.float32)],
        cost=10_000_000,
    )
    pad = pltpu.VMEM((2, ny + 2 * PAD, LANES), jnp.float32)
    gxb, tb = call(
        lambda *refs: first_last_kernel(count, *refs),
        (thermal_conductance_per_alloy, t0, tb0, cond_b, halo_b, gxm, gy, gz, coeff),
        [SMEM] + [VMEM] * 8,
        (plane, plane),
        (VMEM, VMEM),
        [pad],
    )
    tb, t0 = lax.optimization_barrier((tb, t0))
    halo_b = swap(tb, across)
    t1, ta = call(
        lambda tm, old, halo, *refs: next_main_kernel(tm, old, halo.at[0], *refs),
        (t0, tb0, halo_a, gxa, gxm, gy, gz, coeff),
        [VMEM] * 8,
        (most, plane),
        (VMEM, VMEM),
        cost=4_000_000,
    )
    halo_a = swap(ta, on_chip)

    t2, ta = call(
        next_main_kernel,
        (t1, tb, halo_a, gxa, gxm, gy, gz, coeff),
        [VMEM] * 8,
        (most, plane),
        (VMEM, VMEM),
        cost=4_000_000,
    )
    tb2 = call(
        next_last_kernel,
        (t1, tb, halo_b, gxb, gxm, gy, gz, coeff),
        [VMEM] * 8,
        plane,
        VMEM,
        [pad],
    )
    halo_b = swap(tb2, across)
    halo_a = swap(ta, on_chip)

    depth = hits // LANES
    listing = [
        pltpu.SMEM((depth, LANES), jnp.int32),
        pltpu.VMEM((depth, LANES), jnp.int32),
        pltpu.VMEM((depth, LANES), jnp.int32),
        dma,
    ]
    heat, found = call(
        lambda *refs: final_main_kernel(*refs),
        (t2, tb2, halo_a, gxa, gxm, gy, gz, coeff, packed),
        [VMEM] * 9,
        (f32(2 * rows + WINDOW, LANES), f32(depth, LANES)),
        (VMEM, VMEM),
        listing,
        cost=10_000_000,
    )
    ratio = surface_over_flow_ratio.reshape(1, lines)
    heat, found, send = call(
        lambda *refs: walls_kernel(wall, *refs),
        (t2, tb2, halo_b, gxb, gxm, gy, gz, coeff, packed, found, surface_transfer_coefficient, ratio, heat),
        [VMEM] * 13,
        (f32(2 * rows + WINDOW, LANES), f32(depth, LANES), f32(count, LANES)),
        (VMEM, VMEM, VMEM),
        [pad, pltpu.VMEM((lines, LANES), jnp.float32)] + listing,
        input_output_aliases={12: 0},
    )
    rows_all = lax.all_to_all(send, "brick", 0, 0, tiled=True)
    final, mid, _ = call(
        lambda *refs: finish_kernel(wall, *refs),
        (
            packed,
            found,
            rows_all,
            flow_direction_flag.reshape(1, lines),
            entry_coolant_degrees.reshape(1, lines),
            heat,
        ),
        [VMEM] * 6,
        (f32(planes, ny, nz), f32(1, lines), f32(2 * rows + WINDOW, LANES)),
        (HBM, VMEM, VMEM),
        [
            pltpu.VMEM((count, LANES), jnp.float32),
            pltpu.VMEM((8, LANES), jnp.float32),
            pltpu.VMEM((depth, LANES), jnp.float32),
        ]
        + listing
        + [dma((planes, 2))],
        input_output_aliases={5: 2},
    )
    return final, mid


def solution(mesh):
    return jax.shard_map(
        per_device,
        mesh=mesh,
        in_specs=(
            P(("pour", "brick"), None, None),
            P("brick", None, None),
            P(),
            P(),
            P("brick", None, None),
            P("brick", None),
            P(),
            P(),
            P("pour"),
        ),
        out_specs=(P(("pour", "brick"), None, None), P(("pour", "brick"), None)),
        check_vma=False,
    )
```

```python
import jax
import jax.numpy as jnp
from jax import lax
from jax.experimental import pallas as pl
from jax.experimental.pallas import tpu as pltpu
from jax.sharding import PartitionSpec as P

LANES = 128
PAD = 8
STRIP = 16
DEEP = 3
WINDOW = 96
READ_GROUP = 16
WRITE_GROUP = 16
VMEM = pl.BlockSpec(memory_space=pltpu.VMEM)
SMEM = pl.BlockSpec(memory_space=pltpu.SMEM)
HBM = pl.BlockSpec(memory_space=pltpu.HBM)
HALVES = (0, 1)


def f32(*shape):
    return jax.ShapeDtypeStruct(shape, jnp.float32)


def i32(*shape):
    return jax.ShapeDtypeStruct(shape, jnp.int32)


def call(kernel, args, in_specs, out_shape, out_specs, scratch=(), cost=2_000_000, **kw):
    return pl.pallas_call(
        kernel,
        out_shape=out_shape,
        in_specs=in_specs,
        out_specs=out_specs,
        scratch_shapes=list(scratch),
        cost_estimate=pl.CostEstimate(flops=cost, bytes_accessed=cost, transcendentals=0),
        compiler_params=pltpu.CompilerParams(vmem_limit_bytes=12 << 20),
        **kw,
    )(*args)


def plane_of(j, planes):
    odd = lax.rem(lax.axis_index("brick"), 2)
    return jnp.where(odd == 1, j, planes - 1 - j)


def lanes_iota(rows):
    return lax.broadcasted_iota(jnp.int32, (rows, LANES), 1)


def pick(tag, table):
    level = [jnp.broadcast_to(v, tag.shape) for v in table]
    bit = 0
    while len(level) > 1:
        on = (tag & (1 << bit)) != 0
        if len(level) % 2:
            level.append(level[-1])
        level = [jnp.where(on, level[k + 1], level[k]) for k in range(0, len(level), 2)]
        bit += 1
    return level[0]


def face_mean(left, right):
    return 2.0 * left * right / (left + right + 1e-30)


def rows_loop(count, body, step=STRIP, unroll=4):
    def turn(s, carry):
        body(pl.multiple_of(s * step, step))
        return carry

    lax.fori_loop(0, count // step, turn, 0, unroll=unroll)


def advance_rows(cur, r, up, down, gx_up, gx_down, gy, ry, gz, coeff, rz):
    n = STRIP
    lane = lanes_iota(n)
    t = [cur[h, pl.ds(r, n), :] for h in HALVES]
    nxt = [pltpu.roll(t[h], LANES - 1, 1) for h in HALVES]
    ahead = [jnp.where(lane == LANES - 1, nxt[1], nxt[0]), nxt[1]]
    prv = [pltpu.roll(t[h], 1, 1) for h in HALVES]
    behind = [prv[0], jnp.where(lane == 0, prv[0], prv[1])]
    new = []
    for h in HALVES:
        c = t[h]
        flux = gx_up(h) * (up(h) - c) + gx_down(h) * (down(h) - c)
        flux = flux + gy[h, pl.ds(ry, n), :] * (cur[h, pl.ds(r + 1, n), :] - c)
        flux = flux + gy[h, pl.ds(ry - 1, n), :] * (cur[h, pl.ds(r - 1, n), :] - c)
        flux = flux + gz[h, pl.ds(rz, n), :] * (ahead[h] - c)
        flux = flux + gz[2 + h, pl.ds(rz, n), :] * (behind[h] - c)
        new.append(c + coeff[h, pl.ds(rz, n), :] * flux)
    return new


def step_plane(cur, r, up, down, gx_up, gx_down, gy, ry, gz, coeff, rz, ny, emit):
    def body(y):
        new = advance_rows(
            cur,
            r + y,
            lambda h: up(h, y),
            lambda h: down(h, y),
            lambda h: gx_up(h, y),
            lambda h: gx_down(h, y),
            gy,
            ry + y,
            gz,
            coeff,
            rz + y,
        )
        emit(y, new)

    rows_loop(ny, body, unroll=16)


def rows_of(ref, start=0):
    return lambda h, y: ref[h, pl.ds(start + y, STRIP), :]


def main_planes(cur, last, halo, gxa, gxm, gy, gz, coeff, planes, ny, emit):
    def plane(j, first, final):
        r, rz = PAD + j * ny, j * ny
        step_plane(
            cur,
            r,
            rows_of(last) if final else rows_of(cur, r + ny),
            halo if first else rows_of(cur, r - ny),
            rows_of(gxm, rz),
            rows_of(gxa) if first else rows_of(gxm, rz - ny),
            gy,
            PAD + rz,
            gz,
            coeff,
            rz,
            ny,
            lambda y, new: emit(j, y, new),
        )

    def inner(j, carry):
        plane(j, False, False)
        return carry

    plane(0, True, planes == 2)
    lax.fori_loop(1, planes - 2, inner, 0)
    plane(planes - 2, False, True)


def send_kernel(t_ref, tag_ref, a_ref, b_ref, tags, sem):
    planes = t_ref.shape[0]
    parts = [(b_ref, 0, planes - 1)] + [(a_ref, k, k) for k in range(DEEP)]
    copies = []
    for n, (out, k, j) in enumerate(parts):
        x = plane_of(j, planes)
        for h in HALVES:
            part = pl.ds(h * LANES, LANES)
            copies.append(pltpu.make_async_copy(tag_ref.at[x, :, part], tags.at[n, h], sem.at[1, n, h]))
            copies.append(pltpu.make_async_copy(t_ref.at[x, :, part], out.at[0, k, h], sem.at[0, n, h]))
    for copy in copies:
        copy.start()
    for copy in copies:
        copy.wait()
    for n, (out, k, j) in enumerate(parts):
        for h in HALVES:
            out[1, k, h] = tags[n, h].astype(jnp.float32)


def tables(cond_ref, store_ref):
    conds = [jnp.full((1, LANES), cond_ref[m], jnp.float32) for m in range(cond_ref.shape[0])]
    scales = [0.16 / jnp.full((1, LANES), store_ref[m], jnp.float32) for m in range(store_ref.shape[0])]
    return conds, scales


def plane_faces(cond, gy, gz, planes, ny):
    lane = lanes_iota(STRIP)

    def body(r):
        y = lax.rem(r, ny) + lax.broadcasted_iota(jnp.int32, (STRIP, LANES), 0)
        mine = [cond[h, pl.ds(PAD + r, STRIP), :] for h in HALVES]
        nxt = [pltpu.roll(mine[h], LANES - 1, 1) for h in HALVES]
        ahead = [jnp.where(lane == LANES - 1, nxt[1], nxt[0]), nxt[1]]
        prv = [pltpu.roll(mine[h], 1, 1) for h in HALVES]
        behind = [prv[0], jnp.where(lane == 0, prv[0], prv[1])]
        for h in HALVES:
            below = face_mean(mine[h], cond[h, pl.ds(PAD + r + 1, STRIP), :])
            gy[h, pl.ds(PAD + r, STRIP), :] = jnp.where(y == ny - 1, 0.0, below)
            right = face_mean(mine[h], ahead[h])
            gz[h, pl.ds(r, STRIP), :] = jnp.where(lane == LANES - 1, 0.0, right) if h else right
            left = face_mean(behind[h], mine[h])
            gz[2 + h, pl.ds(r, STRIP), :] = left if h else jnp.where(lane == 0, 0.0, left)

    rows_loop(planes * ny, body, unroll=16)


def prepare_kernel(t_ref, tag_ref, cond_ref, store_ref, t0, tb, cond_a, cond_b, gxm, gy, gz, coeff, cond, tags, sem):
    planes, ny = t_ref.shape[0], t_ref.shape[1]

    def fetch(j):
        return pltpu.make_async_copy(tag_ref.at[plane_of(j, planes)], tags.at[j], sem.at[j])

    for j in range(planes):
        fetch(j).start()
    zero = jnp.zeros((PAD, LANES), jnp.float32)
    for h in HALVES:
        for ref in (t0, cond):
            ref[h, pl.ds(0, PAD), :] = zero
            ref[h, pl.ds(ref.shape[1] - PAD, PAD), :] = zero
        gy[h, pl.ds(0, PAD), :] = zero
    conds, scales = tables(cond_ref, store_ref)

    def materials(j, final):
        x = plane_of(j, planes)
        fetch(j).wait()

        def body(y):
            for h in HALVES:
                part = slice(h * LANES, (h + 1) * LANES)
                tag = tags[j, pl.ds(y, STRIP), part]
                kind = pick(tag, conds)
                cond[h, pl.ds(PAD + j * ny + y, STRIP), :] = kind
                coeff[h, pl.ds(j * ny + y, STRIP), :] = pick(tag, scales)
                if final:
                    cond_b[h, pl.ds(y, STRIP), :] = kind
                    tb[h, pl.ds(y, STRIP), :] = t_ref[x, pl.ds(y, STRIP), part]
                else:
                    t0[h, pl.ds(PAD + j * ny + y, STRIP), :] = t_ref[x, pl.ds(y, STRIP), part]

        rows_loop(ny, body)

    def main(j, carry):
        materials(j, False)
        return carry

    lax.fori_loop(0, planes - 1, main, 0)
    materials(planes - 1, True)

    def x_faces(r):
        for h in HALVES:
            mine = cond[h, pl.ds(PAD + r, STRIP), :]
            gxm[h, pl.ds(r, STRIP), :] = face_mean(mine, cond[h, pl.ds(PAD + r + ny, STRIP), :])

    rows_loop((planes - 1) * ny, x_faces)

    def first_conds(y):
        for h in HALVES:
            cond_a[h, pl.ds(y, STRIP), :] = cond[h, pl.ds(PAD + y, STRIP), :]

    rows_loop(ny, first_conds)

    plane_faces(cond, gy, gz, planes, ny)


def clear_pads(ref):
    zero = jnp.zeros((PAD, LANES), jnp.float32)
    for h in HALVES:
        ref[h, pl.ds(0, PAD), :] = zero
        ref[h, pl.ds(ref.shape[1] - PAD, PAD), :] = zero


def last_plane(pad, old, below, halo, gxb, gxm, gy, gz, coeff, emit):
    ny = gxb.shape[1]
    base = gz.shape[1] - ny
    clear_pads(pad)

    def body(y):
        for h in HALVES:
            pad[h, pl.ds(PAD + y, STRIP), :] = old[h, pl.ds(y, STRIP), :]

    rows_loop(ny, body)
    step_plane(
        pad,
        PAD,
        halo,
        below,
        rows_of(gxb),
        rows_of(gxm, base - ny),
        gy,
        PAD + base,
        gz,
        coeff,
        base,
        ny,
        emit,
    )


def keep_rows(ref):
    def emit(y, new):
        for h in HALVES:
            ref[h, pl.ds(y, STRIP), :] = new[h]

    return emit


def first_last_kernel(brick_count, cond_ref, t0, tb_old, cond_b, halo, gxm, gy, gz, coeff, gxb, tb, pad):
    ny = tb.shape[1]
    me = lax.axis_index("brick")
    edge = (me == 0) | (me == brick_count - 1)
    keep = jnp.where(edge, 0.0, 1.0).astype(jnp.float32)
    conds = [keep * jnp.full((1, LANES), cond_ref[m], jnp.float32) for m in range(cond_ref.shape[0])]

    def faces(y):
        for h in HALVES:
            other = pick(halo[1, 0, h, pl.ds(y, STRIP), :].astype(jnp.int32), conds)
            gxb[h, pl.ds(y, STRIP), :] = face_mean(cond_b[h, pl.ds(y, STRIP), :], other)

    rows_loop(ny, faces)
    below = rows_of(t0, t0.shape[1] - PAD - ny)
    last_plane(pad, tb_old, below, rows_of(halo.at[0, 0]), gxb, gxm, gy, gz, coeff, keep_rows(tb))


def next_last_kernel(below, tb_old, halo, gxb, gxm, gy, gz, coeff, tb, pad):
    last_plane(pad, tb_old, rows_of(below), rows_of(halo), gxb, gxm, gy, gz, coeff, keep_rows(tb))


def two_steps_kernel(
    cond_ref, store_ref, t0, tb0, tb1, cond_a, halo, gxm, gy, gz, coeff, t1_last, t2, t2_before, gxa, t1, t0x, t1x, condx, gxx, gyx, gzx, coeffx
):
    ny = tb0.shape[1]
    planes = gz.shape[1] // ny
    conds, scales = tables(cond_ref, store_ref)
    for ref in (t0x, t1x, condx, gyx, t1, t2):
        clear_pads(ref)

    def material(k, y):
        return [halo[1, k, h, pl.ds(y, STRIP), :].astype(jnp.int32) for h in HALVES]

    def beside(y):
        far, mid, near = material(2, y), material(1, y), material(0, y)
        for h in HALVES:
            kinds = [pick(far[h], conds), pick(mid[h], conds), pick(near[h], conds), cond_a[h, pl.ds(y, STRIP), :]]
            for n, tag in enumerate((mid[h], near[h])):
                rows = pl.ds(n * ny + y, STRIP)
                condx[h, pl.ds(PAD + n * ny + y, STRIP), :] = kinds[n + 1]
                coeffx[h, rows, :] = pick(tag, scales)
                t0x[h, pl.ds(PAD + n * ny + y, STRIP), :] = halo[0, 1 - n, h, pl.ds(y, STRIP), :]
                gxx[h, rows, :] = face_mean(kinds[n], kinds[n + 1])
            gxa[h, pl.ds(y, STRIP), :] = face_mean(kinds[2], kinds[3])

    rows_loop(ny, beside, unroll=2)
    plane_faces(condx, gyx, gzx, 2, ny)

    def beside_step(cur, n, up, down, emit):
        step_plane(
            cur,
            PAD + n * ny,
            up,
            down,
            rows_of(gxx, ny) if n == 0 else rows_of(gxa),
            rows_of(gxx, n * ny),
            gyx,
            PAD + n * ny,
            gzx,
            coeffx,
            n * ny,
            ny,
            emit,
        )

    def into(ref, start):
        def emit(y, new):
            for h in HALVES:
                ref[h, pl.ds(start + y, STRIP), :] = new[h]

        return emit

    beside_step(t0x, 0, rows_of(t0x, PAD + ny), rows_of(halo.at[0, 2]), into(t1x, PAD))
    beside_step(t0x, 1, rows_of(t0, PAD), rows_of(t0x, PAD), into(t1x, PAD + ny))
    main_planes(
        t0, tb0, rows_of(t0x, PAD + ny), gxa, gxm, gy, gz, coeff, planes, ny, lambda j, y, new: into(t1, PAD + j * ny)(y, new)
    )

    def out_last(y):
        for h in HALVES:
            t1_last[h, pl.ds(y, STRIP), :] = t1[h, pl.ds(PAD + (planes - 2) * ny + y, STRIP), :]

    rows_loop(ny, out_last)
    beside_step(t1x, 1, rows_of(t1, PAD), rows_of(t1x, PAD), keep_rows(t2_before))
    main_planes(
        t1, tb1, rows_of(t1x, PAD + ny), gxa, gxm, gy, gz, coeff, planes, ny, lambda j, y, new: into(t2, PAD + j * ny)(y, new)
    )


def unpack(packed, ordered, row_of, col_of, sem, half):
    copy = pltpu.make_async_copy(packed, ordered, sem)
    copy.start()
    one = packed[...]
    row_of[...] = lax.shift_right_arithmetic(one, 20) + half
    col_of[...] = lax.shift_right_logical(one, 13) & (LANES - 1)
    return copy


def line_of(packed, wall):
    return lax.shift_right_logical(packed & 8191, wall.bit_length() - 1)


def row_at(ordered, c, place, half):
    return lax.shift_right_arithmetic(ordered[c, place], 20) + half


def windows(first, last, group, ordered, half, work, commit, after=None):
    def base_of(c):
        return pl.multiple_of(row_at(ordered, c, 0, half) & -8, 8)

    def turn(g, carry):
        chunks = [g * group + u for u in range(group)]
        bases = [base_of(c) for c in chunks]
        made = [work(c, base) for c, base in zip(chunks, bases)]
        for c, base, item in zip(chunks, bases, made):
            commit(c, base, item)
        ends = [row_at(ordered, c, LANES - 1, half) - base for c, base in zip(chunks, bases)]
        longest = ends[0]
        for end in ends[1:]:
            longest = jnp.maximum(longest, end)

        @pl.when(longest >= WINDOW)
        def _():
            def chunk(u, inner):
                c = g * group + u
                end = row_at(ordered, c, LANES - 1, half)

                def go(base):
                    base = pl.multiple_of(base, 8)
                    commit(c, base, work(c, base))
                    return base + WINDOW

                lax.while_loop(lambda base: base <= end, go, base_of(c) + WINDOW)
                return inner

            lax.fori_loop(0, group, chunk, 0)

        return carry if after is None else after(g, carry)

    return lax.fori_loop(first, last, turn, 0)


def split(x):
    high = x.astype(jnp.bfloat16)
    return high, (x - high.astype(jnp.float32)).astype(jnp.bfloat16)


def read_walls(first, last, ordered, row_of, col_of, heat, found, half):
    tall = lax.broadcasted_iota(jnp.int32, (WINDOW, LANES), 0)
    square = lax.broadcasted_iota(jnp.int32, (LANES, LANES), 0)

    def work(c, base):
        lanes = jnp.where(square == col_of[pl.ds(c, 1), :], 1.0, 0.0).astype(jnp.bfloat16)
        high, low = split(heat[pl.ds(base, WINDOW), :])
        values = jnp.dot(high, lanes, preferred_element_type=jnp.float32)
        values = values + jnp.dot(low, lanes, preferred_element_type=jnp.float32)
        here = tall == row_of[pl.ds(c, 1), :] - base
        return jnp.sum(jnp.where(here, values, 0.0), axis=0, keepdims=True)

    def commit(c, base, item):
        found[pl.ds(c, 1), :] = found[pl.ds(c, 1), :] + item

    windows(first, last, READ_GROUP, ordered, half, work, commit)


def early_groups(ordered, rows_before, half):
    depth = ordered.shape[0]
    count = jnp.int32(0)
    for g in range(depth // READ_GROUP):
        end = row_at(ordered, (g + 1) * READ_GROUP - 1, LANES - 1, half)
        count = count + jnp.where(end < rows_before, 1, 0)
    return count


def final_main_kernel(tm, tb_old, halo, gxa, gxm, gy, gz, coeff, packed, heat, found, ordered, row_of, col_of, sem):
    ny = tb_old.shape[1]
    rows = gz.shape[1]
    planes = rows // ny
    copy = unpack(packed, ordered, row_of, col_of, sem, rows)

    def emit(j, y, new):
        for h in HALVES:
            heat[pl.ds((2 * j + h) * ny + y, STRIP), :] = new[h]

    main_planes(tm, tb_old, rows_of(halo), gxa, gxm, gy, gz, coeff, planes, ny, emit)
    heat[pl.ds(2 * rows, WINDOW), :] = jnp.zeros((WINDOW, LANES), jnp.float32)
    heat[pl.ds(2 * (rows - ny), 2 * ny), :] = jnp.zeros((2 * ny, LANES), jnp.float32)
    found[...] = jnp.zeros_like(found)
    copy.wait()
    early = early_groups(ordered, 2 * (rows - ny), rows)
    read_walls(0, early, ordered, row_of, col_of, heat, found, rows)


def walls_kernel(
    wall, tm, tb_old, halo, gxb, gxm, gy, gz, coeff, packed, found_in, film, ratio, heat_in, heat, found, send, pad, sums, ordered, row_of, col_of, sem
):
    ny = tb_old.shape[1]
    rows = gz.shape[1]
    planes = rows // ny
    lines = film.shape[1]
    copy = unpack(packed, ordered, row_of, col_of, sem, rows)

    def emit(y, new):
        for h in HALVES:
            heat[pl.ds((2 * (planes - 1) + h) * ny + y, STRIP), :] = new[h]

    below = rows_of(tm, PAD + (planes - 2) * ny)
    last_plane(pad, tb_old, below, rows_of(halo), gxb, gxm, gy, gz, coeff, emit)
    found[...] = found_in[...]
    copy.wait()
    early = early_groups(ordered, 2 * (rows - ny), rows)
    read_walls(early, ordered.shape[0] // READ_GROUP, ordered, row_of, col_of, heat, found, rows)
    owner = line_of(packed[...], wall)
    hot = found[...]
    for k in range(lines):
        part = jnp.where(owner == k, hot, 0.0)
        sums[k : k + 1, :] = jnp.sum(part, axis=0, keepdims=True)
    mean = lax.dot_general(
        jnp.ones((8, LANES), jnp.float32),
        sums[...],
        (((1,), (1,)), ((), ())),
        precision=lax.Precision.HIGHEST,
        preferred_element_type=jnp.float32,
    )[0:1] * (1.0 / wall)
    keep = jnp.exp(-ratio[...] * film[...])
    gain = (1.0 - keep) * mean
    count = send.shape[0]
    send[...] = jnp.zeros_like(send)
    send[:, 0:lines] = jnp.broadcast_to(keep, (count, lines))
    send[:, lines : 2 * lines] = jnp.broadcast_to(gain, (count, lines))


def finish_kernel(
    wall, packed, found, rows_all, direction, entry, heat_in, out, mid, heat, gains, table, change, ordered, row_of, col_of, sem, sems
):
    planes, ny = out.shape[0], out.shape[1]
    rows = planes * ny
    count, lines = rows_all.shape[0], mid.shape[1]
    me = lax.axis_index("brick")
    copy = unpack(packed, ordered, row_of, col_of, sem, rows)

    def pass_on(k, water):
        return rows_all[pl.ds(k, 1), :] * water + gains[pl.ds(k, 1), :]

    gains[...] = pltpu.roll(rows_all[...], LANES - lines, 1)
    table[...] = jnp.zeros_like(table)
    table[0:1, 0:lines] = entry[...]
    start = table[0:1, :]
    ahead = lax.fori_loop(0, me, pass_on, start)
    behind = lax.fori_loop(0, count - 1 - me, lambda k, w: pass_on(count - 1 - k, w), start)
    inflow = jnp.where(direction[...] == 0, ahead[:, 0:lines], behind[:, 0:lines])
    keep = rows_all[pl.ds(me, 1), :][:, 0:lines]
    coolant = 0.5 * (inflow + keep * inflow + gains[pl.ds(me, 1), :][:, 0:lines])
    mid[...] = coolant
    table[0:1, 0:lines] = 0.5 * (1.0 - keep)
    table[1:2, 0:lines] = coolant
    pull = jnp.broadcast_to(table[0:1, :], (8, LANES))
    cool = jnp.broadcast_to(table[1:2, :], (8, LANES))
    depth = change.shape[0]
    for k in range(0, depth, 8):
        owner = line_of(packed[k : k + 8, :], wall)
        a = jnp.take_along_axis(pull, owner, axis=1)
        c = jnp.take_along_axis(cool, owner, axis=1)
        change[k : k + 8, :] = a * (c - found[k : k + 8, :])
    tall = lax.broadcasted_iota(jnp.int32, (WINDOW, LANES), 0)
    square = lax.broadcasted_iota(jnp.int32, (LANES, LANES), 0)

    def work(c, base):
        at = jnp.where(tall == row_of[pl.ds(c, 1), :] - base, 1.0, 0.0).astype(jnp.bfloat16)
        amount = jnp.where(square == col_of[pl.ds(c, 1), :], change[pl.ds(c, 1), :], 0.0)
        high, low = split(amount)
        dims = (((1,), (1,)), ((), ()))
        return lax.dot_general(at, high, dims, preferred_element_type=jnp.float32) + lax.dot_general(
            at, low, dims, preferred_element_type=jnp.float32
        )

    def commit(c, base, item):
        heat[pl.ds(base, WINDOW), :] = heat[pl.ds(base, WINDOW), :] + item

    def copies(j):
        x = plane_of(j, planes)
        return [
            pltpu.make_async_copy(
                heat.at[pl.ds((2 * j + h) * ny, ny), :],
                out.at[x, :, pl.ds(h * LANES, LANES)],
                sems.at[j, h],
            )
            for h in HALVES
        ]

    groups = depth // WRITE_GROUP

    def after(g, sent):
        following = row_at(ordered, jnp.minimum((g + 1) * WRITE_GROUP, depth - 1), 0, rows) & -8
        ready = jnp.where(g == groups - 1, 2 * rows, following)

        def send(j):
            for item in copies(j):
                item.start()
            return j + 1

        return lax.while_loop(lambda j: (j + 1) * 2 * ny <= ready, send, sent)

    copy.wait()
    windows(0, groups, WRITE_GROUP, ordered, rows, work, commit, after)
    for j in range(planes):
        for item in copies(j):
            item.wait()


def per_device(
    initial_voxel_degrees,
    alloy_tag_per_voxel,
    thermal_conductance_per_alloy,
    specific_storage_per_alloy,
    bore_boundary_positions,
    surface_transfer_coefficient,
    surface_over_flow_ratio,
    flow_direction_flag,
    entry_coolant_degrees,
):
    planes, ny, nz = initial_voxel_degrees.shape
    _, lines, wall = bore_boundary_positions.shape
    rows, hits = planes * ny, lines * wall
    count = lax.axis_size("brick")
    dma = pltpu.SemaphoreType.DMA
    axes = ("pour", "brick")
    pours = lax.axis_size("pour")
    on_chip, across = [], []
    for p in range(pours):
        for i in range(count):
            on_chip.append((p * count + i, p * count + (i ^ 1)))
            to = i + 1 if i % 2 else i - 1
            other = p ^ 1 if (p ^ 1) < pours else p
            inside = 0 <= to < count
            across.append((p * count + i, p * count + to if inside else other * count + i))

    def swap(value, pairs):
        return lax.ppermute(value, axes, pairs)

    temperatures = initial_voxel_degrees
    initial_voxel_degrees = pltpu.with_memory_space_constraint(initial_voxel_degrees, pltpu.HBM)
    alloy_tag_per_voxel = pltpu.with_memory_space_constraint(alloy_tag_per_voxel, pltpu.HBM)

    plane = f32(2, ny, LANES)
    ta, tb = call(
        send_kernel,
        (initial_voxel_degrees, alloy_tag_per_voxel),
        [HBM, HBM],
        (f32(2, DEEP, 2, ny, LANES), f32(2, 1, 2, ny, LANES)),
        (VMEM, VMEM),
        [pltpu.VMEM((DEEP + 1, 2, ny, LANES), jnp.int32), dma((2, DEEP + 1, 2))],
    )
    halo_b = swap(tb, across)
    halo_a = swap(ta, on_chip)

    cell = bore_boundary_positions.reshape(hits)
    cell = cell ^ jnp.where(lax.rem(lax.axis_index("brick"), 2) == 1, 0, (planes - 1) * ny * nz)
    row = (cell // (ny * nz) * 2 + (cell // LANES) % 2) * ny + (cell // nz) % ny
    cell = (row * LANES + cell % LANES) ^ (rows * LANES)
    packed = lax.sort(cell * 8192 + lax.iota(jnp.int32, hits), is_stable=False)
    specific_storage_per_alloy, packed = lax.optimization_barrier((specific_storage_per_alloy, packed))
    packed = packed.reshape(hits // LANES, LANES)

    full = f32(2, rows + 2 * PAD, LANES)
    most = f32(2, rows - ny + 2 * PAD, LANES)
    t0, tb0, cond_a, cond_b, gxm, gy, gz, coeff = call(
        prepare_kernel,
        (temperatures, alloy_tag_per_voxel, thermal_conductance_per_alloy, specific_storage_per_alloy),
        [VMEM, HBM, SMEM, SMEM],
        (most, plane, plane, plane, f32(2, rows - ny, LANES), full, f32(4, rows, LANES), f32(2, rows, LANES)),
        (VMEM,) * 8,
        [
            pltpu.VMEM((2, rows + 2 * PAD, LANES), jnp.float32),
            pltpu.VMEM((planes, ny, nz), jnp.int32),
            dma((planes,)),
        ],
    )
    pad = pltpu.VMEM((2, ny + 2 * PAD, LANES), jnp.float32)
    gxb, tb1 = call(
        lambda *refs: first_last_kernel(count, *refs),
        (thermal_conductance_per_alloy, t0, tb0, cond_b, halo_b, gxm, gy, gz, coeff),
        [SMEM] + [VMEM] * 8,
        (plane, plane),
        (VMEM, VMEM),
        [pad],
    )
    halo_b = swap(tb1, across)
    two = pltpu.VMEM((2, 2 * ny + 2 * PAD, LANES), jnp.float32)
    flat = pltpu.VMEM((2, 2 * ny, LANES), jnp.float32)
    t1_last, t2, t2_before, gxa = call(
        two_steps_kernel,
        (thermal_conductance_per_alloy, specific_storage_per_alloy, t0, tb0, tb1, cond_a, halo_a, gxm, gy, gz, coeff),
        [SMEM, SMEM] + [VMEM] * 9,
        (plane, most, plane, plane),
        (VMEM,) * 4,
        [
            pltpu.VMEM(most.shape, jnp.float32),
            two,
            two,
            two,
            flat,
            two,
            pltpu.VMEM((4, 2 * ny, LANES), jnp.float32),
            flat,
        ],
    )
    tb2 = call(
        next_last_kernel,
        (t1_last, tb1, halo_b, gxb, gxm, gy, gz, coeff),
        [VMEM] * 8,
        plane,
        VMEM,
        [pad],
    )
    halo_b = swap(tb2, across)

    depth = hits // LANES
    listing = [
        pltpu.SMEM((depth, LANES), jnp.int32),
        pltpu.VMEM((depth, LANES), jnp.int32),
        pltpu.VMEM((depth, LANES), jnp.int32),
        dma,
    ]
    heat, found = call(
        lambda *refs: final_main_kernel(*refs),
        (t2, tb2, t2_before, gxa, gxm, gy, gz, coeff, packed),
        [VMEM] * 9,
        (f32(2 * rows + WINDOW, LANES), f32(depth, LANES)),
        (VMEM, VMEM),
        listing,
        cost=10_000_000,
    )
    ratio = surface_over_flow_ratio.reshape(1, lines)
    heat, found, send = call(
        lambda *refs: walls_kernel(wall, *refs),
        (t2, tb2, halo_b, gxb, gxm, gy, gz, coeff, packed, found, surface_transfer_coefficient, ratio, heat),
        [VMEM] * 13,
        (f32(2 * rows + WINDOW, LANES), f32(depth, LANES), f32(count, LANES)),
        (VMEM, VMEM, VMEM),
        [pad, pltpu.VMEM((lines, LANES), jnp.float32)] + listing,
        input_output_aliases={12: 0},
    )
    rows_all = lax.all_to_all(send, "brick", 0, 0, tiled=True)
    final, mid, _ = call(
        lambda *refs: finish_kernel(wall, *refs),
        (
            packed,
            found,
            rows_all,
            flow_direction_flag.reshape(1, lines),
            entry_coolant_degrees.reshape(1, lines),
            heat,
        ),
        [VMEM] * 6,
        (f32(planes, ny, nz), f32(1, lines), f32(2 * rows + WINDOW, LANES)),
        (HBM, VMEM, VMEM),
        [
            pltpu.VMEM((count, LANES), jnp.float32),
            pltpu.VMEM((8, LANES), jnp.float32),
            pltpu.VMEM((depth, LANES), jnp.float32),
        ]
        + listing
        + [dma((planes, 2))],
        input_output_aliases={5: 2},
    )
    return final, mid


def solution(mesh):
    return jax.shard_map(
        per_device,
        mesh=mesh,
        in_specs=(
            P(("pour", "brick"), None, None),
            P("brick", None, None),
            P(),
            P(),
            P("brick", None, None),
            P("brick", None),
            P(),
            P(),
            P("pour"),
        ),
        out_specs=(P(("pour", "brick"), None, None), P(("pour", "brick"), None)),
        check_vma=False,
    )
```

```python
import jax
import jax.numpy as jnp
from jax import lax
from jax.experimental import pallas as pl
from jax.experimental.pallas import tpu as pltpu
from jax.sharding import PartitionSpec as P

LANES = 128
PAD = 8
STRIP = 16
DEEP = 3
WINDOW = 96
READ_GROUP = 16
WRITE_GROUP = 16
VMEM = pl.BlockSpec(memory_space=pltpu.VMEM)
SMEM = pl.BlockSpec(memory_space=pltpu.SMEM)
HBM = pl.BlockSpec(memory_space=pltpu.HBM)
HALVES = (0, 1)


def f32(*shape):
    return jax.ShapeDtypeStruct(shape, jnp.float32)


def i32(*shape):
    return jax.ShapeDtypeStruct(shape, jnp.int32)


def call(kernel, args, in_specs, out_shape, out_specs, scratch=(), cost=2_000_000, **kw):
    return pl.pallas_call(
        kernel,
        out_shape=out_shape,
        in_specs=in_specs,
        out_specs=out_specs,
        scratch_shapes=list(scratch),
        cost_estimate=pl.CostEstimate(flops=cost, bytes_accessed=cost, transcendentals=0),
        compiler_params=pltpu.CompilerParams(vmem_limit_bytes=12 << 20),
        **kw,
    )(*args)


def plane_of(j, planes):
    odd = lax.rem(lax.axis_index("brick"), 2)
    return jnp.where(odd == 1, j, planes - 1 - j)


def lanes_iota(rows):
    return lax.broadcasted_iota(jnp.int32, (rows, LANES), 1)


def pick(tag, table):
    level = [jnp.broadcast_to(v, tag.shape) for v in table]
    bit = 0
    while len(level) > 1:
        on = (tag & (1 << bit)) != 0
        if len(level) % 2:
            level.append(level[-1])
        level = [jnp.where(on, level[k + 1], level[k]) for k in range(0, len(level), 2)]
        bit += 1
    return level[0]


def face_mean(left, right):
    return 2.0 * left * right / (left + right + 1e-30)


def rows_loop(count, body, step=STRIP, unroll=4):
    def turn(s, carry):
        body(pl.multiple_of(s * step, step))
        return carry

    lax.fori_loop(0, count // step, turn, 0, unroll=unroll)


def advance_rows(cur, r, up, down, gx_up, gx_down, gy, ry, gz, coeff, rz):
    n = STRIP
    lane = lanes_iota(n)
    t = [cur[h, pl.ds(r, n), :] for h in HALVES]
    nxt = [pltpu.roll(t[h], LANES - 1, 1) for h in HALVES]
    ahead = [jnp.where(lane == LANES - 1, nxt[1], nxt[0]), nxt[1]]
    prv = [pltpu.roll(t[h], 1, 1) for h in HALVES]
    behind = [prv[0], jnp.where(lane == 0, prv[0], prv[1])]
    new = []
    for h in HALVES:
        c = t[h]
        flux = gx_up(h) * (up(h) - c) + gx_down(h) * (down(h) - c)
        flux = flux + gy[h, pl.ds(ry, n), :] * (cur[h, pl.ds(r + 1, n), :] - c)
        flux = flux + gy[h, pl.ds(ry - 1, n), :] * (cur[h, pl.ds(r - 1, n), :] - c)
        flux = flux + gz[h, pl.ds(rz, n), :] * (ahead[h] - c)
        flux = flux + gz[2 + h, pl.ds(rz, n), :] * (behind[h] - c)
        new.append(c + coeff[h, pl.ds(rz, n), :] * flux)
    return new


def step_plane(cur, r, up, down, gx_up, gx_down, gy, ry, gz, coeff, rz, ny, emit):
    def body(y):
        new = advance_rows(
            cur,
            r + y,
            lambda h: up(h, y),
            lambda h: down(h, y),
            lambda h: gx_up(h, y),
            lambda h: gx_down(h, y),
            gy,
            ry + y,
            gz,
            coeff,
            rz + y,
        )
        emit(y, new)

    rows_loop(ny, body, unroll=16)


def rows_of(ref, start=0):
    return lambda h, y: ref[h, pl.ds(start + y, STRIP), :]


def main_planes(cur, last, halo, gxa, gxm, gy, gz, coeff, planes, ny, emit):
    def plane(j, first, final):
        r, rz = PAD + j * ny, j * ny
        step_plane(
            cur,
            r,
            rows_of(last) if final else rows_of(cur, r + ny),
            halo if first else rows_of(cur, r - ny),
            rows_of(gxm, rz),
            rows_of(gxa) if first else rows_of(gxm, rz - ny),
            gy,
            PAD + rz,
            gz,
            coeff,
            rz,
            ny,
            lambda y, new: emit(j, y, new),
        )

    def inner(j, carry):
        plane(j, False, False)
        return carry

    plane(0, True, planes == 2)
    lax.fori_loop(1, planes - 2, inner, 0)
    plane(planes - 2, False, True)


def send_kernel(t_ref, tag_ref, a_ref, b_ref, tags, sem):
    planes = t_ref.shape[0]
    parts = [(b_ref, 0, planes - 1)] + [(a_ref, k, k) for k in range(DEEP)]
    copies = []
    for n, (out, k, j) in enumerate(parts):
        x = plane_of(j, planes)
        for h in HALVES:
            part = pl.ds(h * LANES, LANES)
            copies.append(pltpu.make_async_copy(tag_ref.at[x, :, part], tags.at[n, h], sem.at[1, n, h]))
            copies.append(pltpu.make_async_copy(t_ref.at[x, :, part], out.at[0, k, h], sem.at[0, n, h]))
    for copy in copies:
        copy.start()
    for n, (out, k, j) in enumerate(parts):
        for copy in copies[4 * n : 4 * n + 4]:
            copy.wait()
        for h in HALVES:
            out[1, k, h] = tags[n, h].astype(jnp.float32)


def tables(cond_ref, store_ref):
    conds = [jnp.full((1, LANES), cond_ref[m], jnp.float32) for m in range(cond_ref.shape[0])]
    scales = [0.16 / jnp.full((1, LANES), store_ref[m], jnp.float32) for m in range(store_ref.shape[0])]
    return conds, scales


def plane_faces(cond, gy, gz, planes, ny):
    lane = lanes_iota(STRIP)

    def body(r):
        y = lax.rem(r, ny) + lax.broadcasted_iota(jnp.int32, (STRIP, LANES), 0)
        mine = [cond[h, pl.ds(PAD + r, STRIP), :] for h in HALVES]
        nxt = [pltpu.roll(mine[h], LANES - 1, 1) for h in HALVES]
        ahead = [jnp.where(lane == LANES - 1, nxt[1], nxt[0]), nxt[1]]
        prv = [pltpu.roll(mine[h], 1, 1) for h in HALVES]
        behind = [prv[0], jnp.where(lane == 0, prv[0], prv[1])]
        for h in HALVES:
            below = face_mean(mine[h], cond[h, pl.ds(PAD + r + 1, STRIP), :])
            gy[h, pl.ds(PAD + r, STRIP), :] = jnp.where(y == ny - 1, 0.0, below)
            right = face_mean(mine[h], ahead[h])
            gz[h, pl.ds(r, STRIP), :] = jnp.where(lane == LANES - 1, 0.0, right) if h else right
            left = face_mean(behind[h], mine[h])
            gz[2 + h, pl.ds(r, STRIP), :] = left if h else jnp.where(lane == 0, 0.0, left)

    rows_loop(planes * ny, body, unroll=16)


def prepare_kernel(t_ref, tag_ref, cond_ref, store_ref, t0, tb, cond_a, cond_b, gxm, gy, gz, coeff, cond, tags, sem, sems):
    planes, ny = t_ref.shape[0], t_ref.shape[1]

    def fetch(j):
        return pltpu.make_async_copy(tag_ref.at[plane_of(j, planes)], tags.at[j], sem.at[j])

    def bring(j):
        x = plane_of(j, planes)
        for h in HALVES:
            to = tb.at[h] if j == planes - 1 else t0.at[h, pl.ds(PAD + j * ny, ny)]
            yield pltpu.make_async_copy(t_ref.at[x, :, pl.ds(h * LANES, LANES)], to, sems.at[j, h])

    for j in range(planes):
        fetch(j).start()
    for j in range(planes):
        for copy in bring(j):
            copy.start()
    zero = jnp.zeros((PAD, LANES), jnp.float32)
    for h in HALVES:
        for ref in (t0, cond):
            ref[h, pl.ds(0, PAD), :] = zero
            ref[h, pl.ds(ref.shape[1] - PAD, PAD), :] = zero
        gy[h, pl.ds(0, PAD), :] = zero
    conds, scales = tables(cond_ref, store_ref)

    def materials(j, final):
        fetch(j).wait()

        def body(y):
            for h in HALVES:
                part = slice(h * LANES, (h + 1) * LANES)
                tag = tags[j, pl.ds(y, STRIP), part]
                kind = pick(tag, conds)
                cond[h, pl.ds(PAD + j * ny + y, STRIP), :] = kind
                coeff[h, pl.ds(j * ny + y, STRIP), :] = pick(tag, scales)
                if final:
                    cond_b[h, pl.ds(y, STRIP), :] = kind

        rows_loop(ny, body)

    def main(j, carry):
        materials(j, False)
        return carry

    lax.fori_loop(0, planes - 1, main, 0)
    materials(planes - 1, True)

    def x_faces(r):
        for h in HALVES:
            mine = cond[h, pl.ds(PAD + r, STRIP), :]
            gxm[h, pl.ds(r, STRIP), :] = face_mean(mine, cond[h, pl.ds(PAD + r + ny, STRIP), :])

    rows_loop((planes - 1) * ny, x_faces)

    def first_conds(y):
        for h in HALVES:
            cond_a[h, pl.ds(y, STRIP), :] = cond[h, pl.ds(PAD + y, STRIP), :]

    rows_loop(ny, first_conds)

    plane_faces(cond, gy, gz, planes, ny)
    for j in range(planes):
        for copy in bring(j):
            copy.wait()


def clear_pads(ref):
    zero = jnp.zeros((PAD, LANES), jnp.float32)
    for h in HALVES:
        ref[h, pl.ds(0, PAD), :] = zero
        ref[h, pl.ds(ref.shape[1] - PAD, PAD), :] = zero


def last_plane(pad, old, below, halo, gxb, gxm, gy, gz, coeff, emit):
    ny = gxb.shape[1]
    base = gz.shape[1] - ny
    clear_pads(pad)

    def body(y):
        for h in HALVES:
            pad[h, pl.ds(PAD + y, STRIP), :] = old[h, pl.ds(y, STRIP), :]

    rows_loop(ny, body)
    step_plane(
        pad,
        PAD,
        halo,
        below,
        rows_of(gxb),
        rows_of(gxm, base - ny),
        gy,
        PAD + base,
        gz,
        coeff,
        base,
        ny,
        emit,
    )


def keep_rows(ref):
    def emit(y, new):
        for h in HALVES:
            ref[h, pl.ds(y, STRIP), :] = new[h]

    return emit


def first_last_kernel(brick_count, cond_ref, t0, tb_old, cond_b, halo, gxm, gy, gz, coeff, gxb, tb, pad):
    ny = tb.shape[1]
    me = lax.axis_index("brick")
    edge = (me == 0) | (me == brick_count - 1)
    keep = jnp.where(edge, 0.0, 1.0).astype(jnp.float32)
    conds = [keep * jnp.full((1, LANES), cond_ref[m], jnp.float32) for m in range(cond_ref.shape[0])]

    def faces(y):
        for h in HALVES:
            other = pick(halo[1, 0, h, pl.ds(y, STRIP), :].astype(jnp.int32), conds)
            gxb[h, pl.ds(y, STRIP), :] = face_mean(cond_b[h, pl.ds(y, STRIP), :], other)

    rows_loop(ny, faces)
    below = rows_of(t0, t0.shape[1] - PAD - ny)
    last_plane(pad, tb_old, below, rows_of(halo.at[0, 0]), gxb, gxm, gy, gz, coeff, keep_rows(tb))


def next_last_kernel(below, tb_old, halo, gxb, gxm, gy, gz, coeff, tb, pad):
    last_plane(pad, tb_old, rows_of(below), rows_of(halo), gxb, gxm, gy, gz, coeff, keep_rows(tb))


def two_steps_kernel(
    cond_ref, store_ref, t0, tb0, tb1, cond_a, halo, gxm, gy, gz, coeff, t1_last, t2, t2_before, gxa, t1, t0x, t1x, condx, gxx, gyx, gzx, coeffx
):
    ny = tb0.shape[1]
    planes = gz.shape[1] // ny
    conds, scales = tables(cond_ref, store_ref)
    for ref in (t0x, t1x, condx, gyx, t1, t2):
        clear_pads(ref)

    def material(k, y):
        return [halo[1, k, h, pl.ds(y, STRIP), :].astype(jnp.int32) for h in HALVES]

    def beside(y):
        far, mid, near = material(2, y), material(1, y), material(0, y)
        for h in HALVES:
            kinds = [pick(far[h], conds), pick(mid[h], conds), pick(near[h], conds), cond_a[h, pl.ds(y, STRIP), :]]
            for n, tag in enumerate((mid[h], near[h])):
                rows = pl.ds(n * ny + y, STRIP)
                condx[h, pl.ds(PAD + n * ny + y, STRIP), :] = kinds[n + 1]
                coeffx[h, rows, :] = pick(tag, scales)
                t0x[h, pl.ds(PAD + n * ny + y, STRIP), :] = halo[0, 1 - n, h, pl.ds(y, STRIP), :]
                gxx[h, rows, :] = face_mean(kinds[n], kinds[n + 1])
            gxa[h, pl.ds(y, STRIP), :] = face_mean(kinds[2], kinds[3])

    rows_loop(ny, beside, unroll=2)
    plane_faces(condx, gyx, gzx, 2, ny)

    def beside_step(cur, n, up, down, emit):
        step_plane(
            cur,
            PAD + n * ny,
            up,
            down,
            rows_of(gxx, ny) if n == 0 else rows_of(gxa),
            rows_of(gxx, n * ny),
            gyx,
            PAD + n * ny,
            gzx,
            coeffx,
            n * ny,
            ny,
            emit,
        )

    def into(ref, start):
        def emit(y, new):
            for h in HALVES:
                ref[h, pl.ds(start + y, STRIP), :] = new[h]

        return emit

    beside_step(t0x, 0, rows_of(t0x, PAD + ny), rows_of(halo.at[0, 2]), into(t1x, PAD))
    beside_step(t0x, 1, rows_of(t0, PAD), rows_of(t0x, PAD), into(t1x, PAD + ny))
    main_planes(
        t0, tb0, rows_of(t0x, PAD + ny), gxa, gxm, gy, gz, coeff, planes, ny, lambda j, y, new: into(t1, PAD + j * ny)(y, new)
    )

    def out_last(y):
        for h in HALVES:
            t1_last[h, pl.ds(y, STRIP), :] = t1[h, pl.ds(PAD + (planes - 2) * ny + y, STRIP), :]

    rows_loop(ny, out_last)
    beside_step(t1x, 1, rows_of(t1, PAD), rows_of(t1x, PAD), keep_rows(t2_before))
    main_planes(
        t1, tb1, rows_of(t1x, PAD + ny), gxa, gxm, gy, gz, coeff, planes, ny, lambda j, y, new: into(t2, PAD + j * ny)(y, new)
    )


def unpack(packed, ordered, row_of, sem, half):
    copy = pltpu.make_async_copy(packed, ordered, sem)
    copy.start()
    row_of[...] = lax.shift_right_arithmetic(packed[...], 20) + half
    return copy


def line_of(packed, wall):
    return lax.shift_right_logical(packed & 8191, wall.bit_length() - 1)


def row_at(ordered, c, place, half):
    return lax.shift_right_arithmetic(ordered[c, place], 20) + half


def windows(first, last, group, ordered, half, work, commit, after=None):
    def base_of(c):
        return pl.multiple_of(row_at(ordered, c, 0, half) & -8, 8)

    def turn(g, carry):
        chunks = [g * group + u for u in range(group)]
        bases = [base_of(c) for c in chunks]
        made = [work(c, base) for c, base in zip(chunks, bases)]
        for c, base, item in zip(chunks, bases, made):
            commit(c, base, item)
        ends = [row_at(ordered, c, LANES - 1, half) - base for c, base in zip(chunks, bases)]
        longest = ends[0]
        for end in ends[1:]:
            longest = jnp.maximum(longest, end)

        @pl.when(longest >= WINDOW)
        def _():
            def chunk(u, inner):
                c = g * group + u
                end = row_at(ordered, c, LANES - 1, half)

                def go(base):
                    base = pl.multiple_of(base, 8)
                    commit(c, base, work(c, base))
                    return base + WINDOW

                lax.while_loop(lambda base: base <= end, go, base_of(c) + WINDOW)
                return inner

            lax.fori_loop(0, group, chunk, 0)

        return carry if after is None else after(g, carry)

    return lax.fori_loop(first, last, turn, 0)


def split(x):
    high = x.astype(jnp.bfloat16)
    return high, (x - high.astype(jnp.float32)).astype(jnp.bfloat16)


def lane_masks(col_of, masks):
    square = lax.broadcasted_iota(jnp.int32, (LANES, LANES), 0)

    def turn(c, carry):
        mask = jnp.where(square == col_of[pl.ds(c, 1), :], 1.0, 0.0)
        masks[pl.ds(pl.multiple_of(c * LANES, LANES), LANES), :] = mask.astype(jnp.bfloat16)
        return carry

    lax.fori_loop(0, col_of.shape[0], turn, 0, unroll=8)


def mask_of(masks, c):
    return masks[pl.ds(pl.multiple_of(c * LANES, LANES), LANES), :]


def read_walls(first, last, ordered, row_of, masks, heat, found, half):
    tall = lax.broadcasted_iota(jnp.int32, (WINDOW, LANES), 0)

    def work(c, base):
        lanes = mask_of(masks, c)
        high, low = split(heat[pl.ds(base, WINDOW), :])
        values = jnp.dot(high, lanes, preferred_element_type=jnp.float32)
        values = values + jnp.dot(low, lanes, preferred_element_type=jnp.float32)
        here = tall == row_of[pl.ds(c, 1), :] - base
        return jnp.sum(jnp.where(here, values, 0.0), axis=0, keepdims=True)

    def commit(c, base, item):
        found[pl.ds(c, 1), :] = found[pl.ds(c, 1), :] + item

    windows(first, last, READ_GROUP, ordered, half, work, commit)


def early_groups(ordered, rows_before, half):
    depth = ordered.shape[0]
    count = jnp.int32(0)
    for g in range(depth // READ_GROUP):
        end = row_at(ordered, (g + 1) * READ_GROUP - 1, LANES - 1, half)
        count = count + jnp.where(end < rows_before, 1, 0)
    return count


def final_main_kernel(tm, tb_old, halo, gxa, gxm, gy, gz, coeff, packed, heat, found, masks, ordered, row_of, sem, col_of):
    ny = tb_old.shape[1]
    rows = gz.shape[1]
    planes = rows // ny
    copy = unpack(packed, ordered, row_of, sem, rows)

    def emit(j, y, new):
        for h in HALVES:
            heat[pl.ds((2 * j + h) * ny + y, STRIP), :] = new[h]

    main_planes(tm, tb_old, rows_of(halo), gxa, gxm, gy, gz, coeff, planes, ny, emit)
    heat[pl.ds(2 * rows, WINDOW), :] = jnp.zeros((WINDOW, LANES), jnp.float32)
    heat[pl.ds(2 * (rows - ny), 2 * ny), :] = jnp.zeros((2 * ny, LANES), jnp.float32)
    found[...] = jnp.zeros_like(found)
    col_of[...] = lax.shift_right_logical(packed[...], 13) & (LANES - 1)
    lane_masks(col_of, masks)
    copy.wait()
    early = early_groups(ordered, 2 * (rows - ny), rows)
    read_walls(0, early, ordered, row_of, masks, heat, found, rows)


def walls_kernel(
    wall, tm, tb_old, halo, gxb, gxm, gy, gz, coeff, packed, masks, found_in, film, ratio, heat_in, heat, found, send, pad, sums, ordered, row_of, sem
):
    ny = tb_old.shape[1]
    rows = gz.shape[1]
    planes = rows // ny
    lines = film.shape[1]
    copy = unpack(packed, ordered, row_of, sem, rows)

    def emit(y, new):
        for h in HALVES:
            heat[pl.ds((2 * (planes - 1) + h) * ny + y, STRIP), :] = new[h]

    below = rows_of(tm, PAD + (planes - 2) * ny)
    last_plane(pad, tb_old, below, rows_of(halo), gxb, gxm, gy, gz, coeff, emit)
    found[...] = found_in[...]
    copy.wait()
    early = early_groups(ordered, 2 * (rows - ny), rows)
    read_walls(early, ordered.shape[0] // READ_GROUP, ordered, row_of, masks, heat, found, rows)
    owner = line_of(packed[...], wall)
    hot = found[...]
    for k in range(lines):
        part = jnp.where(owner == k, hot, 0.0)
        sums[k : k + 1, :] = jnp.sum(part, axis=0, keepdims=True)
    mean = lax.dot_general(
        jnp.ones((8, LANES), jnp.float32),
        sums[...],
        (((1,), (1,)), ((), ())),
        precision=lax.Precision.HIGHEST,
        preferred_element_type=jnp.float32,
    )[0:1] * (1.0 / wall)
    keep = jnp.exp(-ratio[...] * film[...])
    gain = (1.0 - keep) * mean
    count = send.shape[0]
    send[...] = jnp.zeros_like(send)
    send[:, 0:lines] = jnp.broadcast_to(keep, (count, lines))
    send[:, lines : 2 * lines] = jnp.broadcast_to(gain, (count, lines))


def finish_kernel(
    wall, packed, masks, found, rows_all, direction, entry, heat_in, out, mid, heat, gains, table, high, low, ordered, row_of, sem, sems
):
    planes, ny = out.shape[0], out.shape[1]
    rows = planes * ny
    count, lines = rows_all.shape[0], mid.shape[1]
    me = lax.axis_index("brick")
    copy = unpack(packed, ordered, row_of, sem, rows)

    def pass_on(k, water):
        return rows_all[pl.ds(k, 1), :] * water + gains[pl.ds(k, 1), :]

    gains[...] = pltpu.roll(rows_all[...], LANES - lines, 1)
    table[...] = jnp.zeros_like(table)
    table[0:1, 0:lines] = entry[...]
    start = table[0:1, :]
    ahead = lax.fori_loop(0, me, pass_on, start)
    behind = lax.fori_loop(0, count - 1 - me, lambda k, w: pass_on(count - 1 - k, w), start)
    inflow = jnp.where(direction[...] == 0, ahead[:, 0:lines], behind[:, 0:lines])
    keep = rows_all[pl.ds(me, 1), :][:, 0:lines]
    coolant = 0.5 * (inflow + keep * inflow + gains[pl.ds(me, 1), :][:, 0:lines])
    mid[...] = coolant
    table[0:1, 0:lines] = 0.5 * (1.0 - keep)
    table[1:2, 0:lines] = coolant
    pull = jnp.broadcast_to(table[0:1, :], (8, LANES))
    cool = jnp.broadcast_to(table[1:2, :], (8, LANES))
    depth = high.shape[0]
    for k in range(0, depth, 8):
        owner = line_of(packed[k : k + 8, :], wall)
        a = jnp.take_along_axis(pull, owner, axis=1)
        c = jnp.take_along_axis(cool, owner, axis=1)
        change = a * (c - found[k : k + 8, :])
        first = change.astype(jnp.bfloat16).astype(jnp.float32)
        high[k : k + 8, :] = first
        low[k : k + 8, :] = change - first
    tall = lax.broadcasted_iota(jnp.int32, (WINDOW, LANES), 0)

    def work(c, base):
        here = tall == row_of[pl.ds(c, 1), :] - base
        pieces = [jnp.where(here, ref[pl.ds(c, 1), :], 0.0).astype(jnp.bfloat16) for ref in (high, low)]
        both = lax.dot_general(
            jnp.concatenate(pieces, axis=0),
            mask_of(masks, c),
            (((1,), (1,)), ((), ())),
            preferred_element_type=jnp.float32,
        )
        return both[:WINDOW] + both[WINDOW:]

    def commit(c, base, item):
        heat[pl.ds(base, WINDOW), :] = heat[pl.ds(base, WINDOW), :] + item

    def copies(j):
        x = plane_of(j, planes)
        return [
            pltpu.make_async_copy(
                heat.at[pl.ds((2 * j + h) * ny, ny), :],
                out.at[x, :, pl.ds(h * LANES, LANES)],
                sems.at[j, h],
            )
            for h in HALVES
        ]

    groups = depth // WRITE_GROUP

    def after(g, sent):
        following = row_at(ordered, jnp.minimum((g + 1) * WRITE_GROUP, depth - 1), 0, rows) & -8
        ready = jnp.where(g == groups - 1, 2 * rows, following)

        def send(j):
            for item in copies(j):
                item.start()
            return j + 1

        return lax.while_loop(lambda j: (j + 1) * 2 * ny <= ready, send, sent)

    copy.wait()
    windows(0, groups, WRITE_GROUP, ordered, rows, work, commit, after)
    for j in range(planes):
        for item in copies(j):
            item.wait()


def per_device(
    initial_voxel_degrees,
    alloy_tag_per_voxel,
    thermal_conductance_per_alloy,
    specific_storage_per_alloy,
    bore_boundary_positions,
    surface_transfer_coefficient,
    surface_over_flow_ratio,
    flow_direction_flag,
    entry_coolant_degrees,
):
    planes, ny, nz = initial_voxel_degrees.shape
    _, lines, wall = bore_boundary_positions.shape
    rows, hits = planes * ny, lines * wall
    count = lax.axis_size("brick")
    dma = pltpu.SemaphoreType.DMA
    axes = ("pour", "brick")
    pours = lax.axis_size("pour")
    on_chip, across = [], []
    for p in range(pours):
        for i in range(count):
            on_chip.append((p * count + i, p * count + (i ^ 1)))
            to = i + 1 if i % 2 else i - 1
            other = p ^ 1 if (p ^ 1) < pours else p
            inside = 0 <= to < count
            across.append((p * count + i, p * count + to if inside else other * count + i))

    def swap(value, pairs):
        return lax.ppermute(value, axes, pairs)

    initial_voxel_degrees = pltpu.with_memory_space_constraint(initial_voxel_degrees, pltpu.HBM)
    alloy_tag_per_voxel = pltpu.with_memory_space_constraint(alloy_tag_per_voxel, pltpu.HBM)

    plane = f32(2, ny, LANES)
    ta, tb = call(
        send_kernel,
        (initial_voxel_degrees, alloy_tag_per_voxel),
        [HBM, HBM],
        (f32(2, DEEP, 2, ny, LANES), f32(2, 1, 2, ny, LANES)),
        (VMEM, VMEM),
        [pltpu.VMEM((DEEP + 1, 2, ny, LANES), jnp.int32), dma((2, DEEP + 1, 2))],
    )
    halo_b = swap(tb, across)
    halo_a = swap(ta, on_chip)

    cell = bore_boundary_positions.reshape(hits)
    cell = cell ^ jnp.where(lax.rem(lax.axis_index("brick"), 2) == 1, 0, (planes - 1) * ny * nz)
    row = (cell // (ny * nz) * 2 + (cell // LANES) % 2) * ny + (cell // nz) % ny
    cell = (row * LANES + cell % LANES) ^ (rows * LANES)
    packed = lax.sort(cell * 8192 + lax.iota(jnp.int32, hits), is_stable=False)
    specific_storage_per_alloy, packed = lax.optimization_barrier((specific_storage_per_alloy, packed))
    packed = packed.reshape(hits // LANES, LANES)

    full = f32(2, rows + 2 * PAD, LANES)
    most = f32(2, rows - ny + 2 * PAD, LANES)
    t0, tb0, cond_a, cond_b, gxm, gy, gz, coeff = call(
        prepare_kernel,
        (initial_voxel_degrees, alloy_tag_per_voxel, thermal_conductance_per_alloy, specific_storage_per_alloy),
        [HBM, HBM, SMEM, SMEM],
        (most, plane, plane, plane, f32(2, rows - ny, LANES), full, f32(4, rows, LANES), f32(2, rows, LANES)),
        (VMEM,) * 8,
        [
            pltpu.VMEM((2, rows + 2 * PAD, LANES), jnp.float32),
            pltpu.VMEM((planes, ny, nz), jnp.int32),
            dma((planes,)),
            dma((planes, 2)),
        ],
    )
    pad = pltpu.VMEM((2, ny + 2 * PAD, LANES), jnp.float32)
    gxb, tb1 = call(
        lambda *refs: first_last_kernel(count, *refs),
        (thermal_conductance_per_alloy, t0, tb0, cond_b, halo_b, gxm, gy, gz, coeff),
        [SMEM] + [VMEM] * 8,
        (plane, plane),
        (VMEM, VMEM),
        [pad],
    )
    halo_b = swap(tb1, across)
    two = pltpu.VMEM((2, 2 * ny + 2 * PAD, LANES), jnp.float32)
    flat = pltpu.VMEM((2, 2 * ny, LANES), jnp.float32)
    t1_last, t2, t2_before, gxa = call(
        two_steps_kernel,
        (thermal_conductance_per_alloy, specific_storage_per_alloy, t0, tb0, tb1, cond_a, halo_a, gxm, gy, gz, coeff),
        [SMEM, SMEM] + [VMEM] * 9,
        (plane, most, plane, plane),
        (VMEM,) * 4,
        [
            pltpu.VMEM(most.shape, jnp.float32),
            two,
            two,
            two,
            flat,
            two,
            pltpu.VMEM((4, 2 * ny, LANES), jnp.float32),
            flat,
        ],
    )
    tb2 = call(
        next_last_kernel,
        (t1_last, tb1, halo_b, gxb, gxm, gy, gz, coeff),
        [VMEM] * 8,
        plane,
        VMEM,
        [pad],
    )
    halo_b = swap(tb2, across)

    depth = hits // LANES
    listing = [
        pltpu.SMEM((depth, LANES), jnp.int32),
        pltpu.VMEM((depth, LANES), jnp.int32),
        dma,
    ]
    heat, found, masks = call(
        lambda *refs: final_main_kernel(*refs),
        (t2, tb2, t2_before, gxa, gxm, gy, gz, coeff, packed),
        [VMEM] * 9,
        (
            f32(2 * rows + WINDOW, LANES),
            f32(depth, LANES),
            jax.ShapeDtypeStruct((hits, LANES), jnp.bfloat16),
        ),
        (VMEM,) * 3,
        listing + [pltpu.VMEM((depth, LANES), jnp.int32)],
        cost=10_000_000,
    )
    ratio = surface_over_flow_ratio.reshape(1, lines)
    heat, found, send = call(
        lambda *refs: walls_kernel(wall, *refs),
        (t2, tb2, halo_b, gxb, gxm, gy, gz, coeff, packed, masks, found, surface_transfer_coefficient, ratio, heat),
        [VMEM] * 14,
        (f32(2 * rows + WINDOW, LANES), f32(depth, LANES), f32(count, LANES)),
        (VMEM, VMEM, VMEM),
        [pad, pltpu.VMEM((lines, LANES), jnp.float32)] + listing,
        input_output_aliases={13: 0},
    )
    rows_all = lax.all_to_all(send, "brick", 0, 0, tiled=True)
    final, mid, _ = call(
        lambda *refs: finish_kernel(wall, *refs),
        (
            packed,
            masks,
            found,
            rows_all,
            flow_direction_flag.reshape(1, lines),
            entry_coolant_degrees.reshape(1, lines),
            heat,
        ),
        [VMEM] * 7,
        (f32(planes, ny, nz), f32(1, lines), f32(2 * rows + WINDOW, LANES)),
        (HBM, VMEM, VMEM),
        [
            pltpu.VMEM((count, LANES), jnp.float32),
            pltpu.VMEM((8, LANES), jnp.float32),
            pltpu.VMEM((depth, LANES), jnp.float32),
            pltpu.VMEM((depth, LANES), jnp.float32),
        ]
        + listing
        + [dma((planes, 2))],
        input_output_aliases={6: 2},
    )
    return final, mid


def solution(mesh):
    return jax.shard_map(
        per_device,
        mesh=mesh,
        in_specs=(
            P(("pour", "brick"), None, None),
            P("brick", None, None),
            P(),
            P(),
            P("brick", None, None),
            P("brick", None),
            P(),
            P(),
            P("pour"),
        ),
        out_specs=(P(("pour", "brick"), None, None), P(("pour", "brick"), None)),
        check_vma=False,
    )
```

```python
import jax
import jax.numpy as jnp
from jax import lax
from jax.experimental import pallas as pl
from jax.experimental.pallas import tpu as pltpu
from jax.sharding import PartitionSpec as P

LANES = 128
PAD = 8
STRIP = 16
DEEP = 3
WINDOW = 96
READ_GROUP = 16
WRITE_GROUP = 16
VMEM = pl.BlockSpec(memory_space=pltpu.VMEM)
SMEM = pl.BlockSpec(memory_space=pltpu.SMEM)
HBM = pl.BlockSpec(memory_space=pltpu.HBM)
HALVES = (0, 1)


def f32(*shape):
    return jax.ShapeDtypeStruct(shape, jnp.float32)


def i32(*shape):
    return jax.ShapeDtypeStruct(shape, jnp.int32)


def call(kernel, args, in_specs, out_shape, out_specs, scratch=(), cost=2_000_000, **kw):
    return pl.pallas_call(
        kernel,
        out_shape=out_shape,
        in_specs=in_specs,
        out_specs=out_specs,
        scratch_shapes=list(scratch),
        cost_estimate=pl.CostEstimate(flops=cost, bytes_accessed=cost, transcendentals=0),
        compiler_params=pltpu.CompilerParams(vmem_limit_bytes=12 << 20),
        **kw,
    )(*args)


def plane_of(j, planes):
    odd = lax.rem(lax.axis_index("brick"), 2)
    return jnp.where(odd == 1, j, planes - 1 - j)


def lanes_iota(rows):
    return lax.broadcasted_iota(jnp.int32, (rows, LANES), 1)


def pick(tag, table):
    level = [jnp.broadcast_to(v, tag.shape) for v in table]
    bit = 0
    while len(level) > 1:
        on = (tag & (1 << bit)) != 0
        if len(level) % 2:
            level.append(level[-1])
        level = [jnp.where(on, level[k + 1], level[k]) for k in range(0, len(level), 2)]
        bit += 1
    return level[0]


def face_mean(left, right):
    return 2.0 * left * right / (left + right + 1e-30)


def rows_loop(count, body, step=STRIP, unroll=4):
    def turn(s, carry):
        body(pl.multiple_of(s * step, step))
        return carry

    lax.fori_loop(0, count // step, turn, 0, unroll=unroll)


def advance_rows(cur, r, up, down, gx_up, gx_down, gy, ry, gz, coeff, rz):
    n = STRIP
    lane = lanes_iota(n)
    t = [cur[h, pl.ds(r, n), :] for h in HALVES]
    nxt = [pltpu.roll(t[h], LANES - 1, 1) for h in HALVES]
    ahead = [jnp.where(lane == LANES - 1, nxt[1], nxt[0]), nxt[1]]
    prv = [pltpu.roll(t[h], 1, 1) for h in HALVES]
    behind = [prv[0], jnp.where(lane == 0, prv[0], prv[1])]
    new = []
    for h in HALVES:
        c = t[h]
        flux = gx_up(h) * (up(h) - c) + gx_down(h) * (down(h) - c)
        flux = flux + gy[h, pl.ds(ry, n), :] * (cur[h, pl.ds(r + 1, n), :] - c)
        flux = flux + gy[h, pl.ds(ry - 1, n), :] * (cur[h, pl.ds(r - 1, n), :] - c)
        flux = flux + gz[h, pl.ds(rz, n), :] * (ahead[h] - c)
        flux = flux + gz[2 + h, pl.ds(rz, n), :] * (behind[h] - c)
        new.append(c + coeff[h, pl.ds(rz, n), :] * flux)
    return new


def step_plane(cur, r, up, down, gx_up, gx_down, gy, ry, gz, coeff, rz, ny, emit):
    def body(y):
        new = advance_rows(
            cur,
            r + y,
            lambda h: up(h, y),
            lambda h: down(h, y),
            lambda h: gx_up(h, y),
            lambda h: gx_down(h, y),
            gy,
            ry + y,
            gz,
            coeff,
            rz + y,
        )
        emit(y, new)

    rows_loop(ny, body, unroll=16)


def rows_of(ref, start=0):
    return lambda h, y: ref[h, pl.ds(start + y, STRIP), :]


def main_planes(cur, last, halo, gxa, gxm, gy, gz, coeff, planes, ny, emit):
    def plane(j, first, final):
        r, rz = PAD + j * ny, j * ny
        step_plane(
            cur,
            r,
            rows_of(last) if final else rows_of(cur, r + ny),
            halo if first else rows_of(cur, r - ny),
            rows_of(gxm, rz),
            rows_of(gxa) if first else rows_of(gxm, rz - ny),
            gy,
            PAD + rz,
            gz,
            coeff,
            rz,
            ny,
            lambda y, new: emit(j, y, new),
        )

    def inner(j, carry):
        plane(j, False, False)
        return carry

    plane(0, True, planes == 2)
    lax.fori_loop(1, planes - 2, inner, 0)
    plane(planes - 2, False, True)


def send_kernel(t_ref, tag_ref, a_ref, b_ref, heat, tags, sem):
    planes, ny = t_ref.shape[0], t_ref.shape[1]
    parts = [(b_ref, 0, planes - 1)] + [(a_ref, k, k) for k in range(DEEP)]
    copies = []
    for n, (_, _, j) in enumerate(parts):
        x = plane_of(j, planes)
        copies.append(pltpu.make_async_copy(tag_ref.at[x], tags.at[n], sem.at[1, n]))
        copies.append(pltpu.make_async_copy(t_ref.at[x], heat.at[n], sem.at[0, n]))
    for copy in copies:
        copy.start()
    for n, (out, k, j) in enumerate(parts):
        for copy in copies[2 * n : 2 * n + 2]:
            copy.wait()

        def body(y, n=n, out=out, k=k):
            for h in HALVES:
                part = slice(h * LANES, (h + 1) * LANES)
                out[0, k, h, pl.ds(y, STRIP), :] = heat[n, pl.ds(y, STRIP), part]
                out[1, k, h, pl.ds(y, STRIP), :] = tags[n, pl.ds(y, STRIP), part].astype(jnp.float32)

        rows_loop(ny, body)


def tables(cond_ref, store_ref):
    conds = [jnp.full((1, LANES), cond_ref[m], jnp.float32) for m in range(cond_ref.shape[0])]
    scales = [0.16 / jnp.full((1, LANES), store_ref[m], jnp.float32) for m in range(store_ref.shape[0])]
    return conds, scales


def plane_faces(cond, gy, gz, planes, ny):
    lane = lanes_iota(STRIP)

    def body(r):
        y = lax.rem(r, ny) + lax.broadcasted_iota(jnp.int32, (STRIP, LANES), 0)
        mine = [cond[h, pl.ds(PAD + r, STRIP), :] for h in HALVES]
        nxt = [pltpu.roll(mine[h], LANES - 1, 1) for h in HALVES]
        ahead = [jnp.where(lane == LANES - 1, nxt[1], nxt[0]), nxt[1]]
        prv = [pltpu.roll(mine[h], 1, 1) for h in HALVES]
        behind = [prv[0], jnp.where(lane == 0, prv[0], prv[1])]
        for h in HALVES:
            below = face_mean(mine[h], cond[h, pl.ds(PAD + r + 1, STRIP), :])
            gy[h, pl.ds(PAD + r, STRIP), :] = jnp.where(y == ny - 1, 0.0, below)
            right = face_mean(mine[h], ahead[h])
            gz[h, pl.ds(r, STRIP), :] = jnp.where(lane == LANES - 1, 0.0, right) if h else right
            left = face_mean(behind[h], mine[h])
            gz[2 + h, pl.ds(r, STRIP), :] = left if h else jnp.where(lane == 0, 0.0, left)

    rows_loop(planes * ny, body, unroll=16)


def prepare_kernel(t_ref, tag_ref, cond_ref, store_ref, t0, tb, cond_a, cond_b, gxm, gy, gz, coeff, cond, tags, sem, sems):
    planes, ny = t_ref.shape[0], t_ref.shape[1]

    def fetch(j):
        return pltpu.make_async_copy(tag_ref.at[plane_of(j, planes)], tags.at[j], sem.at[j])

    def bring(j):
        x = plane_of(j, planes)
        for h in HALVES:
            to = tb.at[h] if j == planes - 1 else t0.at[h, pl.ds(PAD + j * ny, ny)]
            yield pltpu.make_async_copy(t_ref.at[x, :, pl.ds(h * LANES, LANES)], to, sems.at[j, h])

    for j in range(planes):
        fetch(j).start()
    for j in range(planes):
        for copy in bring(j):
            copy.start()
    zero = jnp.zeros((PAD, LANES), jnp.float32)
    for h in HALVES:
        for ref in (t0, cond):
            ref[h, pl.ds(0, PAD), :] = zero
            ref[h, pl.ds(ref.shape[1] - PAD, PAD), :] = zero
        gy[h, pl.ds(0, PAD), :] = zero
    conds, scales = tables(cond_ref, store_ref)

    def materials(j, final):
        fetch(j).wait()

        def body(y):
            for h in HALVES:
                part = slice(h * LANES, (h + 1) * LANES)
                tag = tags[j, pl.ds(y, STRIP), part]
                kind = pick(tag, conds)
                cond[h, pl.ds(PAD + j * ny + y, STRIP), :] = kind
                coeff[h, pl.ds(j * ny + y, STRIP), :] = pick(tag, scales)
                if final:
                    cond_b[h, pl.ds(y, STRIP), :] = kind

        rows_loop(ny, body)

    def main(j, carry):
        materials(j, False)
        return carry

    lax.fori_loop(0, planes - 1, main, 0)
    materials(planes - 1, True)

    def x_faces(r):
        for h in HALVES:
            mine = cond[h, pl.ds(PAD + r, STRIP), :]
            gxm[h, pl.ds(r, STRIP), :] = face_mean(mine, cond[h, pl.ds(PAD + r + ny, STRIP), :])

    rows_loop((planes - 1) * ny, x_faces)

    def first_conds(y):
        for h in HALVES:
            cond_a[h, pl.ds(y, STRIP), :] = cond[h, pl.ds(PAD + y, STRIP), :]

    rows_loop(ny, first_conds)

    plane_faces(cond, gy, gz, planes, ny)
    for j in range(planes):
        for copy in bring(j):
            copy.wait()


def clear_pads(ref):
    zero = jnp.zeros((PAD, LANES), jnp.float32)
    for h in HALVES:
        ref[h, pl.ds(0, PAD), :] = zero
        ref[h, pl.ds(ref.shape[1] - PAD, PAD), :] = zero


def last_plane(pad, old, below, halo, gxb, gxm, gy, gz, coeff, emit):
    ny = gxb.shape[1]
    base = gz.shape[1] - ny
    clear_pads(pad)

    def body(y):
        for h in HALVES:
            pad[h, pl.ds(PAD + y, STRIP), :] = old[h, pl.ds(y, STRIP), :]

    rows_loop(ny, body)
    step_plane(
        pad,
        PAD,
        halo,
        below,
        rows_of(gxb),
        rows_of(gxm, base - ny),
        gy,
        PAD + base,
        gz,
        coeff,
        base,
        ny,
        emit,
    )


def keep_rows(ref):
    def emit(y, new):
        for h in HALVES:
            ref[h, pl.ds(y, STRIP), :] = new[h]

    return emit


def first_last_kernel(brick_count, cond_ref, t0, tb_old, cond_b, halo, gxm, gy, gz, coeff, gxb, tb, pad):
    ny = tb.shape[1]
    me = lax.axis_index("brick")
    edge = (me == 0) | (me == brick_count - 1)
    keep = jnp.where(edge, 0.0, 1.0).astype(jnp.float32)
    conds = [keep * jnp.full((1, LANES), cond_ref[m], jnp.float32) for m in range(cond_ref.shape[0])]

    def faces(y):
        for h in HALVES:
            other = pick(halo[1, 0, h, pl.ds(y, STRIP), :].astype(jnp.int32), conds)
            gxb[h, pl.ds(y, STRIP), :] = face_mean(cond_b[h, pl.ds(y, STRIP), :], other)

    rows_loop(ny, faces)
    below = rows_of(t0, t0.shape[1] - PAD - ny)
    last_plane(pad, tb_old, below, rows_of(halo.at[0, 0]), gxb, gxm, gy, gz, coeff, keep_rows(tb))


def next_last_kernel(below, tb_old, halo, gxb, gxm, gy, gz, coeff, tb, pad):
    last_plane(pad, tb_old, rows_of(below), rows_of(halo), gxb, gxm, gy, gz, coeff, keep_rows(tb))


def two_steps_kernel(
    cond_ref, store_ref, t0, tb0, tb1, cond_a, halo, gxm, gy, gz, coeff, t1_last, t2, t2_before, gxa, t1, t0x, t1x, condx, gxx, gyx, gzx, coeffx
):
    ny = tb0.shape[1]
    planes = gz.shape[1] // ny
    conds, scales = tables(cond_ref, store_ref)
    for ref in (t0x, t1x, condx, gyx, t1, t2):
        clear_pads(ref)

    def material(k, y):
        return [halo[1, k, h, pl.ds(y, STRIP), :].astype(jnp.int32) for h in HALVES]

    def beside(y):
        far, mid, near = material(2, y), material(1, y), material(0, y)
        for h in HALVES:
            kinds = [pick(far[h], conds), pick(mid[h], conds), pick(near[h], conds), cond_a[h, pl.ds(y, STRIP), :]]
            for n, tag in enumerate((mid[h], near[h])):
                rows = pl.ds(n * ny + y, STRIP)
                condx[h, pl.ds(PAD + n * ny + y, STRIP), :] = kinds[n + 1]
                coeffx[h, rows, :] = pick(tag, scales)
                t0x[h, pl.ds(PAD + n * ny + y, STRIP), :] = halo[0, 1 - n, h, pl.ds(y, STRIP), :]
                gxx[h, rows, :] = face_mean(kinds[n], kinds[n + 1])
            gxa[h, pl.ds(y, STRIP), :] = face_mean(kinds[2], kinds[3])

    rows_loop(ny, beside, unroll=2)
    plane_faces(condx, gyx, gzx, 2, ny)

    def beside_step(cur, n, up, down, emit):
        step_plane(
            cur,
            PAD + n * ny,
            up,
            down,
            rows_of(gxx, ny) if n == 0 else rows_of(gxa),
            rows_of(gxx, n * ny),
            gyx,
            PAD + n * ny,
            gzx,
            coeffx,
            n * ny,
            ny,
            emit,
        )

    def into(ref, start):
        def emit(y, new):
            for h in HALVES:
                ref[h, pl.ds(start + y, STRIP), :] = new[h]

        return emit

    beside_step(t0x, 0, rows_of(t0x, PAD + ny), rows_of(halo.at[0, 2]), into(t1x, PAD))
    beside_step(t0x, 1, rows_of(t0, PAD), rows_of(t0x, PAD), into(t1x, PAD + ny))
    main_planes(
        t0, tb0, rows_of(t0x, PAD + ny), gxa, gxm, gy, gz, coeff, planes, ny, lambda j, y, new: into(t1, PAD + j * ny)(y, new)
    )

    def out_last(y):
        for h in HALVES:
            t1_last[h, pl.ds(y, STRIP), :] = t1[h, pl.ds(PAD + (planes - 2) * ny + y, STRIP), :]

    rows_loop(ny, out_last)
    beside_step(t1x, 1, rows_of(t1, PAD), rows_of(t1x, PAD), keep_rows(t2_before))
    main_planes(
        t1, tb1, rows_of(t1x, PAD + ny), gxa, gxm, gy, gz, coeff, planes, ny, lambda j, y, new: into(t2, PAD + j * ny)(y, new)
    )


def unpack(packed, ordered, row_of, sem, half):
    copy = pltpu.make_async_copy(packed, ordered, sem)
    copy.start()
    row_of[...] = lax.shift_right_arithmetic(packed[...], 20) + half
    return copy


def line_of(packed, wall):
    return lax.shift_right_logical(packed & 8191, wall.bit_length() - 1)


def row_at(ordered, c, place, half):
    return lax.shift_right_arithmetic(ordered[c, place], 20) + half


def windows(first, last, group, ordered, half, work, commit, after=None):
    def base_of(c):
        return pl.multiple_of(row_at(ordered, c, 0, half) & -8, 8)

    def turn(g, carry):
        chunks = [g * group + u for u in range(group)]
        bases = [base_of(c) for c in chunks]
        made = [work(c, base) for c, base in zip(chunks, bases)]
        for c, base, item in zip(chunks, bases, made):
            commit(c, base, item)
        ends = [row_at(ordered, c, LANES - 1, half) - base for c, base in zip(chunks, bases)]
        longest = ends[0]
        for end in ends[1:]:
            longest = jnp.maximum(longest, end)

        @pl.when(longest >= WINDOW)
        def _():
            def chunk(u, inner):
                c = g * group + u
                end = row_at(ordered, c, LANES - 1, half)

                def go(base):
                    base = pl.multiple_of(base, 8)
                    commit(c, base, work(c, base))
                    return base + WINDOW

                lax.while_loop(lambda base: base <= end, go, base_of(c) + WINDOW)
                return inner

            lax.fori_loop(0, group, chunk, 0)

        return carry if after is None else after(g, carry)

    return lax.fori_loop(first, last, turn, 0)


def split(x):
    high = x.astype(jnp.bfloat16)
    return high, (x - high.astype(jnp.float32)).astype(jnp.bfloat16)


def lane_masks(col_of, masks):
    square = lax.broadcasted_iota(jnp.int32, (LANES, LANES), 0)

    def turn(c, carry):
        mask = jnp.where(square == col_of[pl.ds(c, 1), :], 1.0, 0.0)
        masks[pl.ds(pl.multiple_of(c * LANES, LANES), LANES), :] = mask.astype(jnp.bfloat16)
        return carry

    lax.fori_loop(0, col_of.shape[0], turn, 0, unroll=8)


def mask_of(masks, c):
    return masks[pl.ds(pl.multiple_of(c * LANES, LANES), LANES), :]


def read_walls(first, last, ordered, row_of, masks, heat, found, half):
    tall = lax.broadcasted_iota(jnp.int32, (WINDOW, LANES), 0)

    def work(c, base):
        lanes = mask_of(masks, c)
        high, low = split(heat[pl.ds(base, WINDOW), :])
        values = jnp.dot(high, lanes, preferred_element_type=jnp.float32)
        values = values + jnp.dot(low, lanes, preferred_element_type=jnp.float32)
        here = tall == row_of[pl.ds(c, 1), :] - base
        return jnp.sum(jnp.where(here, values, 0.0), axis=0, keepdims=True)

    def commit(c, base, item):
        found[pl.ds(c, 1), :] = found[pl.ds(c, 1), :] + item

    windows(first, last, READ_GROUP, ordered, half, work, commit)


def early_groups(ordered, rows_before, half):
    depth = ordered.shape[0]
    count = jnp.int32(0)
    for g in range(depth // READ_GROUP):
        end = row_at(ordered, (g + 1) * READ_GROUP - 1, LANES - 1, half)
        count = count + jnp.where(end < rows_before, 1, 0)
    return count


def final_main_kernel(tm, tb_old, halo, gxa, gxm, gy, gz, coeff, packed, heat, found, masks, ordered, row_of, sem, col_of):
    ny = tb_old.shape[1]
    rows = gz.shape[1]
    planes = rows // ny
    copy = unpack(packed, ordered, row_of, sem, rows)

    def emit(j, y, new):
        for h in HALVES:
            heat[pl.ds((2 * j + h) * ny + y, STRIP), :] = new[h]

    main_planes(tm, tb_old, rows_of(halo), gxa, gxm, gy, gz, coeff, planes, ny, emit)
    heat[pl.ds(2 * rows, WINDOW), :] = jnp.zeros((WINDOW, LANES), jnp.float32)
    heat[pl.ds(2 * (rows - ny), 2 * ny), :] = jnp.zeros((2 * ny, LANES), jnp.float32)
    found[...] = jnp.zeros_like(found)
    col_of[...] = lax.shift_right_logical(packed[...], 13) & (LANES - 1)
    lane_masks(col_of, masks)
    copy.wait()
    early = early_groups(ordered, 2 * (rows - ny), rows)
    read_walls(0, early, ordered, row_of, masks, heat, found, rows)


def walls_kernel(
    wall, tm, tb_old, halo, gxb, gxm, gy, gz, coeff, packed, masks, found_in, film, ratio, heat_in, heat, found, send, pad, sums, ordered, row_of, sem
):
    ny = tb_old.shape[1]
    rows = gz.shape[1]
    planes = rows // ny
    lines = film.shape[1]
    copy = unpack(packed, ordered, row_of, sem, rows)

    def emit(y, new):
        for h in HALVES:
            heat[pl.ds((2 * (planes - 1) + h) * ny + y, STRIP), :] = new[h]

    below = rows_of(tm, PAD + (planes - 2) * ny)
    last_plane(pad, tb_old, below, rows_of(halo), gxb, gxm, gy, gz, coeff, emit)
    found[...] = found_in[...]
    copy.wait()
    early = early_groups(ordered, 2 * (rows - ny), rows)
    read_walls(early, ordered.shape[0] // READ_GROUP, ordered, row_of, masks, heat, found, rows)
    owner = line_of(packed[...], wall)
    hot = found[...]
    for k in range(lines):
        part = jnp.where(owner == k, hot, 0.0)
        sums[k : k + 1, :] = jnp.sum(part, axis=0, keepdims=True)
    mean = lax.dot_general(
        jnp.ones((8, LANES), jnp.float32),
        sums[...],
        (((1,), (1,)), ((), ())),
        precision=lax.Precision.HIGHEST,
        preferred_element_type=jnp.float32,
    )[0:1] * (1.0 / wall)
    keep = jnp.exp(-ratio[...] * film[...])
    gain = (1.0 - keep) * mean
    count = send.shape[0]
    send[...] = jnp.zeros_like(send)
    send[:, 0:lines] = jnp.broadcast_to(keep, (count, lines))
    send[:, lines : 2 * lines] = jnp.broadcast_to(gain, (count, lines))


def finish_kernel(
    wall, packed, masks, found, rows_all, direction, entry, heat_in, out, mid, heat, gains, table, high, low, ordered, row_of, sem, sems
):
    planes, ny = out.shape[0], out.shape[1]
    rows = planes * ny
    count, lines = rows_all.shape[0], mid.shape[1]
    me = lax.axis_index("brick")
    copy = unpack(packed, ordered, row_of, sem, rows)

    def pass_on(k, water):
        return rows_all[pl.ds(k, 1), :] * water + gains[pl.ds(k, 1), :]

    gains[...] = pltpu.roll(rows_all[...], LANES - lines, 1)
    table[...] = jnp.zeros_like(table)
    table[0:1, 0:lines] = entry[...]
    start = table[0:1, :]
    ahead = lax.fori_loop(0, me, pass_on, start)
    behind = lax.fori_loop(0, count - 1 - me, lambda k, w: pass_on(count - 1 - k, w), start)
    inflow = jnp.where(direction[...] == 0, ahead[:, 0:lines], behind[:, 0:lines])
    keep = rows_all[pl.ds(me, 1), :][:, 0:lines]
    coolant = 0.5 * (inflow + keep * inflow + gains[pl.ds(me, 1), :][:, 0:lines])
    mid[...] = coolant
    table[0:1, 0:lines] = 0.5 * (1.0 - keep)
    table[1:2, 0:lines] = coolant
    pull = jnp.broadcast_to(table[0:1, :], (8, LANES))
    cool = jnp.broadcast_to(table[1:2, :], (8, LANES))
    depth = high.shape[0]
    for k in range(0, depth, 8):
        owner = line_of(packed[k : k + 8, :], wall)
        a = jnp.take_along_axis(pull, owner, axis=1)
        c = jnp.take_along_axis(cool, owner, axis=1)
        change = a * (c - found[k : k + 8, :])
        first = change.astype(jnp.bfloat16).astype(jnp.float32)
        high[k : k + 8, :] = first
        low[k : k + 8, :] = change - first
    tall = lax.broadcasted_iota(jnp.int32, (WINDOW, LANES), 0)

    def work(c, base):
        here = tall == row_of[pl.ds(c, 1), :] - base
        pieces = [jnp.where(here, ref[pl.ds(c, 1), :], 0.0).astype(jnp.bfloat16) for ref in (high, low)]
        both = lax.dot_general(
            jnp.concatenate(pieces, axis=0),
            mask_of(masks, c),
            (((1,), (1,)), ((), ())),
            preferred_element_type=jnp.float32,
        )
        return both[:WINDOW] + both[WINDOW:]

    def commit(c, base, item):
        heat[pl.ds(base, WINDOW), :] = heat[pl.ds(base, WINDOW), :] + item

    def copies(j):
        x = plane_of(j, planes)
        return [
            pltpu.make_async_copy(
                heat.at[pl.ds((2 * j + h) * ny, ny), :],
                out.at[x, :, pl.ds(h * LANES, LANES)],
                sems.at[j, h],
            )
            for h in HALVES
        ]

    groups = depth // WRITE_GROUP

    def after(g, sent):
        following = row_at(ordered, jnp.minimum((g + 1) * WRITE_GROUP, depth - 1), 0, rows) & -8
        ready = jnp.where(g == groups - 1, 2 * rows, following)

        def send(j):
            for item in copies(j):
                item.start()
            return j + 1

        return lax.while_loop(lambda j: (j + 1) * 2 * ny <= ready, send, sent)

    copy.wait()
    windows(0, groups, WRITE_GROUP, ordered, rows, work, commit, after)
    for j in range(planes):
        for item in copies(j):
            item.wait()


def per_device(
    initial_voxel_degrees,
    alloy_tag_per_voxel,
    thermal_conductance_per_alloy,
    specific_storage_per_alloy,
    bore_boundary_positions,
    surface_transfer_coefficient,
    surface_over_flow_ratio,
    flow_direction_flag,
    entry_coolant_degrees,
):
    planes, ny, nz = initial_voxel_degrees.shape
    _, lines, wall = bore_boundary_positions.shape
    rows, hits = planes * ny, lines * wall
    count = lax.axis_size("brick")
    dma = pltpu.SemaphoreType.DMA
    axes = ("pour", "brick")
    pours = lax.axis_size("pour")
    on_chip, across = [], []
    for p in range(pours):
        for i in range(count):
            on_chip.append((p * count + i, p * count + (i ^ 1)))
            to = i + 1 if i % 2 else i - 1
            other = p ^ 1 if (p ^ 1) < pours else p
            inside = 0 <= to < count
            across.append((p * count + i, p * count + to if inside else other * count + i))

    def swap(value, pairs):
        return lax.ppermute(value, axes, pairs)

    initial_voxel_degrees = pltpu.with_memory_space_constraint(initial_voxel_degrees, pltpu.HBM)
    alloy_tag_per_voxel = pltpu.with_memory_space_constraint(alloy_tag_per_voxel, pltpu.HBM)

    plane = f32(2, ny, LANES)
    ta, tb = call(
        send_kernel,
        (initial_voxel_degrees, alloy_tag_per_voxel),
        [HBM, HBM],
        (f32(2, DEEP, 2, ny, LANES), f32(2, 1, 2, ny, LANES)),
        (VMEM, VMEM),
        [
            pltpu.VMEM((DEEP + 1, ny, nz), jnp.float32),
            pltpu.VMEM((DEEP + 1, ny, nz), jnp.int32),
            dma((2, DEEP + 1)),
        ],
    )
    halo_b = swap(tb, across)
    halo_a = swap(ta, on_chip)

    cell = bore_boundary_positions.reshape(hits)
    cell = cell ^ jnp.where(lax.rem(lax.axis_index("brick"), 2) == 1, 0, (planes - 1) * ny * nz)
    row = (cell // (ny * nz) * 2 + (cell // LANES) % 2) * ny + (cell // nz) % ny
    cell = (row * LANES + cell % LANES) ^ (rows * LANES)
    packed = lax.sort(cell * 8192 + lax.iota(jnp.int32, hits), is_stable=False)
    specific_storage_per_alloy, packed = lax.optimization_barrier((specific_storage_per_alloy, packed))
    packed = packed.reshape(hits // LANES, LANES)

    full = f32(2, rows + 2 * PAD, LANES)
    most = f32(2, rows - ny + 2 * PAD, LANES)
    t0, tb0, cond_a, cond_b, gxm, gy, gz, coeff = call(
        prepare_kernel,
        (initial_voxel_degrees, alloy_tag_per_voxel, thermal_conductance_per_alloy, specific_storage_per_alloy),
        [HBM, HBM, SMEM, SMEM],
        (most, plane, plane, plane, f32(2, rows - ny, LANES), full, f32(4, rows, LANES), f32(2, rows, LANES)),
        (VMEM,) * 8,
        [
            pltpu.VMEM((2, rows + 2 * PAD, LANES), jnp.float32),
            pltpu.VMEM((planes, ny, nz), jnp.int32),
            dma((planes,)),
            dma((planes, 2)),
        ],
    )
    pad = pltpu.VMEM((2, ny + 2 * PAD, LANES), jnp.float32)
    gxb, tb1 = call(
        lambda *refs: first_last_kernel(count, *refs),
        (thermal_conductance_per_alloy, t0, tb0, cond_b, halo_b, gxm, gy, gz, coeff),
        [SMEM] + [VMEM] * 8,
        (plane, plane),
        (VMEM, VMEM),
        [pad],
    )
    halo_b = swap(tb1, across)
    two = pltpu.VMEM((2, 2 * ny + 2 * PAD, LANES), jnp.float32)
    flat = pltpu.VMEM((2, 2 * ny, LANES), jnp.float32)
    t1_last, t2, t2_before, gxa = call(
        two_steps_kernel,
        (thermal_conductance_per_alloy, specific_storage_per_alloy, t0, tb0, tb1, cond_a, halo_a, gxm, gy, gz, coeff),
        [SMEM, SMEM] + [VMEM] * 9,
        (plane, most, plane, plane),
        (VMEM,) * 4,
        [
            pltpu.VMEM(most.shape, jnp.float32),
            two,
            two,
            two,
            flat,
            two,
            pltpu.VMEM((4, 2 * ny, LANES), jnp.float32),
            flat,
        ],
    )
    tb2 = call(
        next_last_kernel,
        (t1_last, tb1, halo_b, gxb, gxm, gy, gz, coeff),
        [VMEM] * 8,
        plane,
        VMEM,
        [pad],
    )
    halo_b = swap(tb2, across)

    depth = hits // LANES
    listing = [
        pltpu.SMEM((depth, LANES), jnp.int32),
        pltpu.VMEM((depth, LANES), jnp.int32),
        dma,
    ]
    heat, found, masks = call(
        lambda *refs: final_main_kernel(*refs),
        (t2, tb2, t2_before, gxa, gxm, gy, gz, coeff, packed),
        [VMEM] * 9,
        (
            f32(2 * rows + WINDOW, LANES),
            f32(depth, LANES),
            jax.ShapeDtypeStruct((hits, LANES), jnp.bfloat16),
        ),
        (VMEM,) * 3,
        listing + [pltpu.VMEM((depth, LANES), jnp.int32)],
        cost=10_000_000,
    )
    ratio = surface_over_flow_ratio.reshape(1, lines)
    heat, found, send = call(
        lambda *refs: walls_kernel(wall, *refs),
        (t2, tb2, halo_b, gxb, gxm, gy, gz, coeff, packed, masks, found, surface_transfer_coefficient, ratio, heat),
        [VMEM] * 14,
        (f32(2 * rows + WINDOW, LANES), f32(depth, LANES), f32(count, LANES)),
        (VMEM, VMEM, VMEM),
        [pad, pltpu.VMEM((lines, LANES), jnp.float32)] + listing,
        input_output_aliases={13: 0},
    )
    rows_all = lax.all_to_all(send, "brick", 0, 0, tiled=True)
    final, mid, _ = call(
        lambda *refs: finish_kernel(wall, *refs),
        (
            packed,
            masks,
            found,
            rows_all,
            flow_direction_flag.reshape(1, lines),
            entry_coolant_degrees.reshape(1, lines),
            heat,
        ),
        [VMEM] * 7,
        (f32(planes, ny, nz), f32(1, lines), f32(2 * rows + WINDOW, LANES)),
        (HBM, VMEM, VMEM),
        [
            pltpu.VMEM((count, LANES), jnp.float32),
            pltpu.VMEM((8, LANES), jnp.float32),
            pltpu.VMEM((depth, LANES), jnp.float32),
            pltpu.VMEM((depth, LANES), jnp.float32),
        ]
        + listing
        + [dma((planes, 2))],
        input_output_aliases={6: 2},
    )
    return final, mid


def solution(mesh):
    return jax.shard_map(
        per_device,
        mesh=mesh,
        in_specs=(
            P(("pour", "brick"), None, None),
            P("brick", None, None),
            P(),
            P(),
            P("brick", None, None),
            P("brick", None),
            P(),
            P(),
            P("pour"),
        ),
        out_specs=(P(("pour", "brick"), None, None), P(("pour", "brick"), None)),
        check_vma=False,
    )
```
